32 devices in a mesh: rep: 4 (over x, core), shard: 8 (over z, y).
Axes of the slice: x: 2, y: 2, z: 4, core: 2. Of those that a mesh axis runs over, the one named last changes fastest.
Arguments:
- block_input: bfloat16 [16384, 2048], P(('rep', 'shard')), may hold values from -6 to 6
- cotangent: bfloat16 [16384, 2048], P(('rep', 'shard')), may hold values from -6 to 6
- seq_lengths: int32 [4], replicated, may hold values from 1024 to 4096, as said below
- slot_order: int32 [4], replicated, may hold values from 0 to 3, each once
- norm_gain: bfloat16 [2048], P('shard'), may hold values from 0.5 to 1.5
- in_proj: bfloat16 [2048, 8192], P('shard'), may hold values from -0.125 to 0.125
- conv_weight: bfloat16 [4, 4096], P(None, 'shard'), may hold values from -3 to 3
- conv_bias: bfloat16 [4096], P('shard'), may hold values from -3 to 3
- x_proj: bfloat16 [4096, 160], P('shard'), may hold values from -0.09375 to 0.09375
- dt_proj: bfloat16 [128, 4096], P(None, 'shard'), may hold values from -0.5 to 0.5
- dt_bias: bfloat16 [4096], P('shard'), may hold values from -7 to -3
- a_log: bfloat16 [16, 4096], P(None, 'shard'), may hold values from -4 to 0.5
- d_skip: bfloat16 [4096], P('shard'), may hold values from 0.5 to 1.5
- out_proj: bfloat16 [4096, 2048], P('shard'), may hold values from -0.375 to 0.375
Outputs:
- activations: bfloat16 [16384, 2048], P(('rep', 'shard'))
- input_grad: float32 [16384, 2048], P(('rep', 'shard'))
- grad_norm_gain: float32 [2048], P('shard')
- grad_in_proj: float32 [2048, 8192], P('shard')
- grad_conv_weight: float32 [4, 4096], P(None, 'shard')
- grad_conv_bias: float32 [4096], P('shard')
- grad_x_proj: float32 [4096, 160], P('shard')
- grad_dt_proj: float32 [128, 4096], P(None, 'shard')
- grad_dt_bias: float32 [4096], P('shard')
- grad_a_log: float32 [16, 4096], P(None, 'shard')
- grad_d_skip: float32 [4096], P('shard')
- grad_out_proj: float32 [4096, 2048], P('shard')
The draws below stay inside these ranges and needn't reach their ends.
Inputs may be any that keep to these rules, and one draw needn't show every extreme that they name: `seq_lengths`: each sequence has 1024 to 4096 tokens; one sequence has exactly 4096 and one exactly 1024.
All inputs are finite; a program needn't handle non-finite values.
Results may differ from the reference program's by a relative error of at most 0.015.
Values may be sent and summed in bfloat16 or wider, within the bound.
A program may use at most 384 MiB of HBM per device.

```python
import jax
import jax.numpy as jnp
from jax import lax

D = 2048
INNER = 4096
NSTATE = 16
RANK = 128
KCONV = 4
STRETCH = 32
MINLEN = 1024
SLOT = 4096
TOKENS = 16384
NSEQ = 4


def draw_seq_lengths(key, part):
    values = jax.random.randint(key, (NSEQ,), MINLEN, SLOT + 1, dtype=jnp.int32)
    values = values.at[0].set(SLOT)
    values = values.at[1].set(MINLEN)
    return values


def steps_of(rng, extent, shards, low, largest):
    factor_of = 1.0
    for axis_at, shards_of in shards:
        heights = jax.random.uniform(jax.random.fold_in(jax.random.fold_in(rng, 6), axis_at), (shards_of,), jnp.float32, low / len(shards), largest / len(shards))
        factor_of = factor_of * jnp.repeat(jnp.exp(heights), extent[axis_at] // shards_of).reshape((-1,) + (1,) * (len(extent) - 1 - axis_at))
    return factor_of


def scatter_about(own_key, dims, scale, bound, split=(), held_as=jnp.bfloat16):
    array = scale * jax.random.normal(own_key, dims, jnp.float32)
    if split:
        array = array * steps_of(own_key, dims, split, -0.22, 0.18)
    return jnp.clip(array, -bound, bound).astype(held_as)


def setup_inputs(seed: int = 0) -> dict:
    splits = jax.random.split(jax.random.key(seed), 15)
    block_input = scatter_about(splits[0], (TOKENS, D), 1.0, 6.0, ((0, 32),))
    cotangent = scatter_about(splits[1], (TOKENS, D), 1.0, 6.0, ((0, 32),))
    seq_lengths = draw_seq_lengths(jax.random.fold_in(splits[14], 71), 0)
    slot_order = jax.random.permutation(splits[3], NSEQ).astype(jnp.int32)
    norm_gain = jnp.clip(1.0 + 0.1 * jax.random.normal(splits[4], (D,), jnp.float32), 0.5, 1.5).astype(jnp.bfloat16)
    in_proj = scatter_about(splits[5], (D, 2 * INNER), D ** -0.5, 0.125, ((0, 8),))
    conv_weight = scatter_about(splits[6], (KCONV, INNER), KCONV ** -0.5, 3.0, ((1, 8),))
    conv_bias = scatter_about(splits[7], (INNER,), 0.5, 3.0, ((0, 8),))
    x_proj = scatter_about(splits[8], (INNER, RANK + 2 * NSTATE), INNER ** -0.5, 0.09375, ((0, 8),))
    dt_proj = scatter_about(splits[9], (RANK, INNER), RANK ** -0.5, 0.5, ((1, 8),))
    dt_bias = jnp.clip(-7.0 + 4.0 * jax.random.uniform(splits[10], (INNER,), jnp.float32) ** steps_of(splits[10], (INNER,), ((0, 8),), -0.2, 0.2), -7.0, -3.0).astype(jnp.bfloat16)
    a_log = jnp.clip(-4.0 + 4.5 * jax.random.uniform(splits[11], (NSTATE, INNER), jnp.float32) ** steps_of(splits[11], (NSTATE, INNER), ((1, 8),), -0.2, 0.2), -4.0, 0.5).astype(jnp.bfloat16)
    d_skip = jnp.clip(1.0 + 0.1 * jax.random.normal(splits[12], (INNER,), jnp.float32), 0.5, 1.5).astype(jnp.bfloat16)
    out_proj = scatter_about(splits[13], (INNER, D), (INNER // 16) ** -0.5, 0.375, ((0, 8),))
    return {"block_input": block_input, "cotangent": cotangent, "seq_lengths": seq_lengths, "slot_order": slot_order, "norm_gain": norm_gain, "in_proj": in_proj, "conv_weight": conv_weight, "conv_bias": conv_bias, "x_proj": x_proj, "dt_proj": dt_proj, "dt_bias": dt_bias, "a_log": a_log, "d_skip": d_skip, "out_proj": out_proj}


EPSILON = 1e-05
HIGHEST = lax.Precision.HIGHEST

@jax.custom_vjp
def low(v):
    return lax.optimization_barrier(v.astype(jnp.bfloat16)).astype(jnp.float32)

@jax.custom_vjp
def low_back(v):
    return v

def low_keep(v):
    return (low(v), None)

def low_pass(kept, grad):
    return (grad,)

def back_keep(v):
    return (v, None)

def back_low(kept, grad):
    return (low(grad),)
low.defvjp(low_keep, low_pass)
low_back.defvjp(back_keep, back_low)

def split_blocks(values, width):
    return values.reshape((values.shape[0] // width, width) + values.shape[1:])

def selective(step_size, conv_out, input_coeff, output_coeff, rates, start_state):

    @jax.checkpoint
    def block_step(state, pieces):
        step_block, conv_block, input_block, output_block = pieces
        running = jnp.cumsum(step_block, axis=0)
        exponent = rates[None, :, :] * running[:, None, :]
        feeding = (step_block * conv_block)[:, None, :] * input_block[:, :, None]
        summed = jnp.cumsum(jnp.exp(-exponent) * feeding, axis=0)
        states = jnp.exp(exponent) * (state[None, :, :] + summed)
        emitted = jnp.einsum('qn,qne->qe', output_block, states, precision=HIGHEST)
        return (states[-1], emitted)
    final_state, emitted = lax.scan(block_step, start_state, (split_blocks(step_size, STRETCH), split_blocks(conv_out, STRETCH), split_blocks(input_coeff, STRETCH), split_blocks(output_coeff, STRETCH)))
    return (emitted.reshape(step_size.shape), final_state)

def conv_apply(conv_in, taps, bias_row):
    tok_rows = conv_in.shape[0]
    padded = jnp.concatenate([jnp.zeros((taps.shape[0] - 1, conv_in.shape[1]), jnp.float32), conv_in], axis=0)
    total = bias_row[None, :]
    for offset in range(taps.shape[0]):
        total = total + taps[offset][None, :] * padded[offset:offset + tok_rows]
    return total

def slot_forward(params, slot_input, slot_valid):
    norm_gain, in_proj, conv_weight, conv_bias, x_proj, dt_proj, dt_bias, a_log, d_skip, out_proj = params
    scale = lax.rsqrt(lax.optimization_barrier(jnp.mean(slot_input * slot_input, axis=1, keepdims=True)) + EPSILON)
    normed = low(slot_input * scale * norm_gain[None, :])
    mixed_in = low_back(jnp.dot(normed, in_proj, precision=HIGHEST))
    conv_in = low(mixed_in[:, :INNER])
    gate_in = mixed_in[:, INNER:]
    conv_out = low(jax.nn.silu(conv_apply(conv_in, conv_weight, conv_bias)))
    projected = low_back(jnp.dot(conv_out, x_proj, precision=HIGHEST))
    step_low = low(projected[:, :RANK])
    input_coeff = projected[:, RANK:RANK + NSTATE]
    output_coeff = projected[:, RANK + NSTATE:]
    step_size = jax.nn.softplus(low_back(jnp.dot(step_low, dt_proj, precision=HIGHEST)) + dt_bias[None, :])
    rates = -jnp.exp(a_log)
    scanned, final_state = selective(step_size, conv_out, input_coeff, output_coeff, rates, jnp.zeros((NSTATE, INNER), jnp.float32))
    scanned = scanned + d_skip[None, :] * conv_out
    gated = low(scanned * jax.nn.silu(gate_in))
    return slot_input + slot_valid[:, None] * jnp.dot(gated, out_proj, precision=HIGHEST)

def reference(block_input, cotangent, seq_lengths, slot_order, norm_gain, in_proj, conv_weight, conv_bias, x_proj, dt_proj, dt_bias, a_log, d_skip, out_proj):
    matches = slot_order[:, None] == jnp.arange(NSEQ, dtype=jnp.int32)[None, :]
    slot_len = lax.optimization_barrier(jnp.sum(jnp.where(matches, seq_lengths[:, None], 0), axis=0)).astype(jnp.int32)
    valid = (jnp.arange(SLOT, dtype=jnp.int32)[None, :] < slot_len[:, None]).astype(jnp.float32)
    params = (norm_gain.astype(jnp.float32), in_proj.astype(jnp.float32), conv_weight.astype(jnp.float32), conv_bias.astype(jnp.float32), x_proj.astype(jnp.float32), dt_proj.astype(jnp.float32), dt_bias.astype(jnp.float32), a_log.astype(jnp.float32), d_skip.astype(jnp.float32), out_proj.astype(jnp.float32))
    slot_step = jax.checkpoint(slot_forward)

    def forward(input_f, weights):

        def each_slot(carry, pieces):
            return (carry, slot_step(weights, pieces[0], pieces[1]))
        unused, outputs = lax.scan(each_slot, jnp.zeros((), jnp.float32), (input_f.reshape(NSEQ, SLOT, D), valid))
        return outputs.reshape(TOKENS, D)
    result, pullback = jax.vjp(forward, block_input.astype(jnp.float32), params)
    input_grad, grads = pullback(cotangent.astype(jnp.float32))
    return (result.astype(jnp.bfloat16), input_grad, grads[0], grads[1], grads[2], grads[3], grads[4], grads[5], grads[6], grads[7], grads[8], grads[9])
```

```python
from functools import partial

import jax
import jax.numpy as jnp
from jax import lax
from jax.experimental import pallas as pl
from jax.experimental.pallas import tpu as pltpu
from jax.sharding import PartitionSpec as P

EPSILON = 1e-05
SPAN_TOKENS = 4096
F32=jnp.float32; BF16=jnp.bfloat16
LN=128
def pick(n, opts):
    for o in opts:
        if n % o == 0: return o
    return n

def first_kernel(U, dt_ref, x_ref, g_ref, b_ref, c_ref, a_ref, hend_ref, adj_ref, h_s, p_s, r_s, dtx_s):
    TC, EG = dt_ref.shape
    NT = EG//LN
    c = pl.program_id(2)
    @pl.when(c == 0)
    def _():
        h_s[...] = jnp.zeros_like(h_s); p_s[...] = jnp.ones_like(p_s); r_s[...] = jnp.zeros_like(r_s)
    dtx_s[...] = dt_ref[...]*x_ref[...].astype(F32)
    sl = [slice(j*LN,(j+1)*LN) for j in range(NT)]
    A = [a_ref[:, s] for s in sl]
    def body(i, carry):
        h, p, r = [list(v) for v in carry]
        rows = pl.ds(pl.multiple_of(i*U,U),U)
        dv, xv, gv = dt_ref.at[rows], dtx_s.at[rows], g_ref.at[rows]
        for k in range(U):
            t = i*U+k
            bt = b_ref[t]; ct = c_ref[t]
            for j in range(NT):
                d = dv[k:k+1, sl[j]]
                a = jnp.exp2(d*A[j])
                h[j] = a*h[j] + xv[k:k+1, sl[j]]*bt
                p[j] = p[j]*a
                r[j] = r[j] + p[j]*(ct*gv[k:k+1, sl[j]])
        return tuple(h), tuple(p), tuple(r)
    init = tuple(tuple(s_[:, s] for s in sl) for s_ in (h_s,p_s,r_s))
    h,p,r = lax.fori_loop(0, TC//U, body, init)
    for j in range(NT):
        h_s[:, sl[j]] = h[j]; p_s[:, sl[j]] = p[j]; r_s[:, sl[j]] = r[j]
    @pl.when(c == pl.num_programs(2)-1)
    def _():
        hend_ref[...] = h_s[...]; adj_ref[...] = r_s[...]

def first_pass(dt, x, g, bx, cx, a2, Q, TC=128, EG=512, U=8):
    T,E = dt.shape; N = a2.shape[0]; L=T//Q; NC=L//TC; NE=E//EG
    row = pl.BlockSpec((TC,EG), lambda q,e,c:(q*NC+c, e))
    sp = pl.BlockSpec((TC,N,LN), lambda q,e,c:(q*NC+c,0,0))
    st = pl.BlockSpec((None,N,EG), lambda q,e,c:(q,0,e))
    return pl.pallas_call(partial(first_kernel,U), grid=(Q,NE,NC),
        in_specs=[row,row,row,sp,sp,pl.BlockSpec((N,EG), lambda q,e,c:(0,e))],
        out_specs=[st,st],
        out_shape=[jax.ShapeDtypeStruct((Q,N,E),F32)]*2,
        scratch_shapes=[pltpu.VMEM((N,EG),F32)]*3+[pltpu.VMEM((TC,EG),F32)],
        compiler_params=pltpu.CompilerParams(dimension_semantics=("arbitrary",)*3, vmem_limit_bytes=60<<20),
        name="first_pass",
        cost_estimate=pl.CostEstimate(flops=9*T*E*N, bytes_accessed=10*T*E, transcendentals=T*E*N))(dt,x,g,bx,cx,a2)

def sums(tb):
    return (lax.broadcasted_iota(jnp.int32,(tb,tb*8),1)//8 == lax.broadcasted_iota(jnp.int32,(tb,tb*8),0)).astype(BF16)

def fwd_kernel(U, TB, dt_ref, x_ref, b_ref, c_ref, a_ref, h0_ref, y_ref, ck_ref, h_s, q_s, dtx_s):
    TC, EG = dt_ref.shape
    NT = EG//LN
    c = pl.program_id(2)
    @pl.when(c == 0)
    def _(): h_s[...] = h0_ref[...]
    ck_ref[...] = h_s[...]
    dtx_s[...] = dt_ref[...]*x_ref[...].astype(F32)
    sl = [slice(j*LN,(j+1)*LN) for j in range(NT)]
    A = [a_ref[:, s] for s in sl]
    S = sums(TB)
    def block(m, h):
        def body(i, carry):
            h = list(carry)
            rows = pl.ds(pl.multiple_of(m*TB+i*U,U),U)
            dv, xv = dt_ref.at[rows], dtx_s.at[rows]
            for k in range(U):
                t = m*TB+i*U+k
                bt = b_ref[t]; ct = c_ref[t]
                for j in range(NT):
                    a = jnp.exp2(dv[k:k+1, sl[j]]*A[j])
                    h[j] = a*h[j] + xv[k:k+1, sl[j]]*bt
                    q = h[j]*ct
                    q_s[pl.ds(pl.multiple_of((i*U+k)*8,8),8), sl[j]] = q[:8]+q[8:]
            return tuple(h)
        h = lax.fori_loop(0, TB//U, body, h)
        y_ref[pl.ds(pl.multiple_of(m*TB,TB),TB),:] = jnp.dot(S, q_s[...].astype(BF16), preferred_element_type=F32)
        return h
    h = lax.fori_loop(0, TC//TB, block, tuple(h_s[:, s] for s in sl))
    for j in range(NT): h_s[:, sl[j]] = h[j]

def fwd_pass(dt, x, bx, cx, a2, h0, Q, TC=64, EG=512, U=8, TB=32):
    T,E = dt.shape; N = a2.shape[0]; L=T//Q; NC=L//TC; NE=E//EG
    row = pl.BlockSpec((TC,EG), lambda q,e,c:(q*NC+c, e))
    sp = pl.BlockSpec((TC,N,LN), lambda q,e,c:(q*NC+c,0,0))
    return pl.pallas_call(partial(fwd_kernel,U,TB), grid=(Q,NE,NC),
        in_specs=[row,row,sp,sp,pl.BlockSpec((N,EG), lambda q,e,c:(0,e)), pl.BlockSpec((None,N,EG), lambda q,e,c:(q,0,e))],
        out_specs=[row, pl.BlockSpec((None,N,EG), lambda q,e,c:(q*NC+c,0,e))],
        out_shape=[jax.ShapeDtypeStruct((T,E),F32), jax.ShapeDtypeStruct((Q*NC,N,E),F32)],
        scratch_shapes=[pltpu.VMEM((N,EG),F32), pltpu.VMEM((TB*8,EG),F32), pltpu.VMEM((TC,EG),F32)],
        compiler_params=pltpu.CompilerParams(dimension_semantics=("arbitrary",)*3, vmem_limit_bytes=60<<20),
        name="fwd_pass",
        cost_estimate=pl.CostEstimate(flops=7*T*E*N, bytes_accessed=10*T*E, transcendentals=T*E*N))(dt,x,bx,cx,a2,h0)

def bwd_kernel(U, TB, dt_ref, x_ref, g_ref, b_ref, c_ref, a_ref, ck_ref, mu0_ref,
               gs_ref, gx_ref, gb_ref, gc_ref, ga_ref,
               mu_s, ga_s, qa_s, qb_s, lam_s, dtx_s, a_s, h_s):
    TC, EG = dt_ref.shape
    N = a_ref.shape[0]
    NT = EG//LN
    q_id = pl.program_id(0); c = pl.program_id(2)
    @pl.when(c == 0)
    def _():
        mu_s[...] = mu0_ref[...]
        ga_s[...] = jnp.zeros_like(ga_s)
    dtx_s[...] = dt_ref[...]*x_ref[...].astype(F32)
    sl = [slice(j*LN,(j+1)*LN) for j in range(NT)]
    A = [a_ref[:, s] for s in sl]
    h_s[0] = ck_ref[...]
    def up(i, carry):
        h = list(carry)
        rows = pl.ds(pl.multiple_of(i*U,U),U)
        dv, xv = dt_ref.at[rows], dtx_s.at[rows]
        for k in range(U):
            t = i*U+k
            bt = b_ref[t]
            for j in range(NT):
                a = jnp.exp2(dv[k:k+1, sl[j]]*A[j])
                h[j] = a*h[j] + xv[k:k+1, sl[j]]*bt
                a_s[t, :, sl[j]] = a
                h_s[t+1, :, sl[j]] = h[j]
        return tuple(h)
    lax.fori_loop(0, TC//U, up, tuple(ck_ref[:, s] for s in sl))
    S = sums(TB)
    tn_t = lax.broadcasted_iota(jnp.int32,(TB,TB*N),1)//N == lax.broadcasted_iota(jnp.int32,(TB,TB*N),0)
    sel = (lax.broadcasted_iota(jnp.int32,(TB*N,N),0)%N == lax.broadcasted_iota(jnp.int32,(TB*N,N),1)).astype(BF16)
    def block(mm, mu):
        m = TC//TB-1-mm
        def body(ii, carry):
            mu, ga = [list(v) for v in carry]
            i = TB//U-1-ii
            rows = pl.ds(pl.multiple_of(m*TB+i*U,U),U)
            dv, gv = dt_ref.at[rows], g_ref.at[rows]
            for kk in range(U):
                k = U-1-kk
                tl = i*U+k
                t = m*TB+tl
                bt = b_ref[t]; ct = c_ref[t]
                for j in range(NT):
                    lam = mu[j] + ct*gv[k:k+1, sl[j]]
                    mu[j] = a_s[t,:,sl[j]]*lam
                    w = mu[j]*h_s[t,:,sl[j]]
                    ga[j] = ga[j] + dv[k:k+1, sl[j]]*w
                    qa = A[j]*w
                    qb = lam*bt
                    r8 = pl.ds(pl.multiple_of(tl*8,8),8)
                    qa_s[r8, sl[j]] = qa[:8]+qa[8:]
                    qb_s[r8, sl[j]] = qb[:8]+qb[8:]
                    lam_s[pl.ds(pl.multiple_of(tl*N,8),N), sl[j]] = lam
            return tuple(mu), tuple(ga)
        ga = tuple(ga_s[:, s] for s in sl)
        mu, ga = lax.fori_loop(0, TB//U, body, (mu, ga))
        for j in range(NT): ga_s[:, sl[j]] = ga[j]
        rows = pl.ds(pl.multiple_of(m*TB,TB),TB)
        sa = jnp.dot(S, qa_s[...].astype(BF16), preferred_element_type=F32)
        sb = jnp.dot(S, qb_s[...].astype(BF16), preferred_element_type=F32)
        d = dt_ref[rows,:]; xx = x_ref[rows,:].astype(F32); dx = dtx_s[rows,:]
        gs_ref[rows,:] = sa*(1.0/LOG2E) + xx*sb
        gx_ref[rows,:] = d*sb
        hb = h_s[pl.ds(m*TB+1,TB)].reshape(TB*N,EG).astype(BF16)
        nt = (((1,),(1,)),((),()))
        zc = lax.dot_general(g_ref[rows,:].astype(BF16), hb, nt, preferred_element_type=F32)
        zb = lax.dot_general(dx.astype(BF16), lam_s[...].astype(BF16), nt, preferred_element_type=F32)
        def take(z):
            z = jnp.where(tn_t, z, 0.0)
            hi = z.astype(BF16); lo = (z-hi.astype(F32)).astype(BF16)
            return jnp.dot(hi, sel, preferred_element_type=F32)+jnp.dot(lo, sel, preferred_element_type=F32)
        gc_ref[rows,:] = take(zc)
        gb_ref[rows,:] = take(zb)
        return mu
    mu = lax.fori_loop(0, TC//TB, block, tuple(mu_s[:, s] for s in sl))
    for j in range(NT): mu_s[:, sl[j]] = mu[j]
    @pl.when(c == pl.num_programs(2)-1)
    def _(): ga_ref[...] = ga_s[...]

LOG2E=1.4426950408889634
def bwd_pass(dt, x, g, bx, cx, a2, ck, mu0, Q, TC=64, EG=512, U=8, TB=32):
    T,E = dt.shape; N = a2.shape[0]; L=T//Q; NC=L//TC; NE=E//EG
    CK = ck.shape[0]//(Q*NC)
    row = pl.BlockSpec((TC,EG), lambda q,e,c:(q*NC+NC-1-c, e))
    sp = pl.BlockSpec((TC,N,LN), lambda q,e,c:(q*NC+NC-1-c,0,0))
    st = pl.BlockSpec((None,N,EG), lambda q,e,c:(q,0,e))
    nb = pl.BlockSpec((None,TC,N), lambda q,e,c:(e,q*NC+NC-1-c,0))
    return pl.pallas_call(partial(bwd_kernel,U,TB), grid=(Q,NE,NC),
        in_specs=[row,row,row,sp,sp,pl.BlockSpec((N,EG), lambda q,e,c:(0,e)), pl.BlockSpec((None,N,EG), lambda q,e,c:(q*NC+NC-1-c,0,e)), st],
        out_specs=[row,row,nb,nb,st],
        out_shape=[jax.ShapeDtypeStruct((T,E),F32)]*2+[jax.ShapeDtypeStruct((NE,T,N),F32)]*2+[jax.ShapeDtypeStruct((Q,N,E),F32)],
        scratch_shapes=[pltpu.VMEM((N,EG),F32)]*2+[pltpu.VMEM((TB*8,EG),F32)]*2+[pltpu.VMEM((TB*N,EG),F32)]+[pltpu.VMEM((TC,EG),F32)]
           +[pltpu.VMEM((TC,N,EG),F32), pltpu.VMEM((TC+1,N,EG),F32)],
        compiler_params=pltpu.CompilerParams(dimension_semantics=("arbitrary",)*3, vmem_limit_bytes=62<<20),
        name="bwd_pass",
        cost_estimate=pl.CostEstimate(flops=20*T*E*N, bytes_accessed=22*T*E, transcendentals=T*E*N))(dt,x,g,bx,cx,a2,ck,mu0)


def conv_kernel(x_ref, edge_ref, w_ref, o_ref, x_s):
    L = x_ref.shape[0]
    taps = w_ref.shape[0] - 1
    x_s[0:8, :] = edge_ref[...]
    x_s[8:, :] = x_ref[...].astype(F32)
    pre = jnp.broadcast_to(w_ref[taps:taps + 1, :], x_ref.shape)
    for k in range(taps):
        at = 8 - (taps - 1) + k
        pre = pre + w_ref[k:k + 1, :] * x_s[at:at + L, :]
    o_ref[...] = (pre * jax.nn.sigmoid(pre)).astype(BF16)


def conv_pass(conv_in, edge, wb, Q, EB=256):
    T, E = conv_in.shape
    L = T // Q
    row = pl.BlockSpec((L, EB), lambda q, e: (q, e))
    return pl.pallas_call(
        conv_kernel,
        grid=(Q, E // EB),
        in_specs=[
            row,
            pl.BlockSpec((None, 8, EB), lambda q, e: (q, 0, e)),
            pl.BlockSpec((wb.shape[0], EB), lambda q, e: (0, e)),
        ],
        out_specs=row,
        out_shape=jax.ShapeDtypeStruct((T, E), BF16),
        scratch_shapes=[pltpu.VMEM((L + 8, EB), F32)],
        compiler_params=pltpu.CompilerParams(dimension_semantics=("arbitrary",) * 2),
        name="conv_pass",
        cost_estimate=pl.CostEstimate(flops=12 * T * E, bytes_accessed=4 * T * E, transcendentals=T * E),
    )(conv_in, edge, wb)


def conv_back_kernel(gp_ref, xp_ref, gx_ref, x_ref, edge_ref, w_ref, gi_ref, head_ref, tail_ref, gw_ref, x_s, g_s):
    L = x_ref.shape[0]
    taps = w_ref.shape[0] - 1
    x_s[0:8, :] = edge_ref[...]
    x_s[8:, :] = x_ref[...].astype(F32)
    at = [8 - (taps - 1) + k for k in range(taps)]
    pre = jnp.broadcast_to(w_ref[taps:taps + 1, :], x_ref.shape)
    for k in range(taps):
        pre = pre + w_ref[k:k + 1, :] * x_s[at[k]:at[k] + L, :]
    s = jax.nn.sigmoid(pre)
    g_out = contract_cols(gp_ref[...], xp_ref[...]) + gx_ref[...]
    g_pre = g_out * s * (1.0 + pre * (1.0 - s))
    g_s[0:L, :] = g_pre
    g_s[L:, :] = jnp.zeros((8, x_ref.shape[1]), F32)
    gw = [jnp.sum(g_pre * x_s[at[k]:at[k] + L, :], axis=0, keepdims=True) for k in range(taps)]
    gw.append(jnp.sum(g_pre, axis=0, keepdims=True))
    gw_ref[...] = jnp.concatenate(gw, axis=0)
    head_ref[...] = g_s[0:8, :]
    g_in = jnp.zeros(x_ref.shape, F32)
    for k in range(taps):
        g_in = g_in + w_ref[k:k + 1, :] * g_s[taps - 1 - k:taps - 1 - k + L, :]
    gi_ref[...] = g_in.astype(BF16)
    tail_ref[...] = g_in[L - 8:, :]


def conv_back(g_projected, x_proj, gx, conv_in, edge, wb, Q, EB=256):
    T, E = conv_in.shape
    L = T // Q
    row = pl.BlockSpec((L, EB), lambda q, e: (q, e))
    edges = pl.BlockSpec((None, 8, EB), lambda q, e: (q, 0, e))
    rows = wb.shape[0]
    return pl.pallas_call(
        conv_back_kernel,
        grid=(Q, E // EB),
        in_specs=[
            pl.BlockSpec((L, g_projected.shape[1]), lambda q, e: (q, 0)),
            pl.BlockSpec((EB, x_proj.shape[1]), lambda q, e: (e, 0)),
            row,
            row,
            edges,
            pl.BlockSpec((rows, EB), lambda q, e: (0, e)),
        ],
        out_specs=[row, edges, edges, pl.BlockSpec((None, rows, EB), lambda q, e: (q, 0, e))],
        out_shape=[
            jax.ShapeDtypeStruct((T, E), BF16),
            jax.ShapeDtypeStruct((Q, 8, E), F32),
            jax.ShapeDtypeStruct((Q, 8, E), F32),
            jax.ShapeDtypeStruct((Q, rows, E), F32),
        ],
        scratch_shapes=[pltpu.VMEM((L + 8, EB), F32)] * 2,
        compiler_params=pltpu.CompilerParams(dimension_semantics=("arbitrary",) * 2),
        name="conv_back",
        cost_estimate=pl.CostEstimate(flops=400 * T * E, bytes_accessed=10 * T * E, transcendentals=T * E),
    )(g_projected, x_proj, gx, conv_in, edge, wb)


def contract_rows(left, right):
    return lax.dot_general(left, right, (((0,), (0,)), ((), ())), preferred_element_type=F32)


def contract_cols(left, right):
    return lax.dot_general(left, right, (((1,), (1,)), ((), ())), preferred_element_type=F32)


def swap(value, flip):
    return lax.ppermute(value, "rep", [(i, i ^ flip) for i in range(lax.axis_size("rep"))])


def shifted(value, steps):
    count = lax.axis_size("shard")
    first, last = (max(0, -steps), min(count, count - steps))
    return lax.ppermute(value, "shard", [(i, i + steps) for i in range(first, last)])


def rep_gather(value):
    far = swap(value, 2)
    return [value, swap(value, 1), far, swap(far, 1)]


def rep_scatter(parts):
    low = [part.astype(BF16) for part in parts]
    near = swap(jnp.stack([low[1], low[3]]), 1).astype(F32)
    mine, other = (parts[0] + near[0], parts[2] + near[1])
    return mine + swap(other.astype(BF16), 2).astype(F32)


def rep_sum(parts):
    near = swap(jnp.stack([parts[1], parts[3]]), 1)
    pair = jnp.stack([parts[0] + near[0], parts[2] + near[1]])
    far = swap(pair, 2)
    full = jnp.stack([pair[0] + far[1], pair[1] + far[0]])
    over = swap(full, 1)
    return [full[0], over[0], full[1], over[1]]


def carry_in(total, state, rates, place, reverse):
    sign = -1 if reverse else 1
    span = lax.axis_size("shard")
    total, state = (shifted(total, sign), shifted(state, sign))
    known = jnp.where(place >= 1, 1.0, 0.0)
    total, state = (total * known, state * known)
    step = 1
    while step < min(span, 8):
        far_total, far_state = (shifted(total, sign * step), shifted(state, sign * step))
        known = jnp.where(place >= step, 1.0, 0.0)
        state = state + jnp.exp(rates[None] * total[:, None, :]) * (far_state * known)
        total = total + far_total * known
        step *= 2
    return state


def on_device(
    block_input,
    cotangent,
    seq_lengths,
    slot_order,
    norm_gain,
    in_proj,
    conv_weight,
    conv_bias,
    x_proj,
    dt_proj,
    dt_bias,
    a_log,
    d_skip,
    out_proj,
):
    n_shard, n_rep = (lax.axis_size("shard"), lax.axis_size("rep"))
    shard_at, rep_at = (lax.axis_index("shard"), lax.axis_index("rep"))
    rows, width = block_input.shape
    tokens = n_rep * rows
    taps, wide = conv_weight.shape
    part = wide // n_rep
    chans = part * n_shard
    rank = dt_proj.shape[0]
    states = a_log.shape[0]
    span = max(1, min(n_shard, SPAN_TOKENS // rows))
    in_slot = shard_at % span
    keep_prev = (in_slot != 0).astype(F32)
    keep_next = (in_slot != span - 1).astype(F32)
    places = in_slot * rows + jnp.arange(rows, dtype=jnp.int32)

    def valid_of(flip):
        slot_at = ((rep_at ^ flip) * n_shard + shard_at) // span
        slot_len = jnp.sum(jnp.where(slot_order == slot_at, seq_lengths, 0))
        return (places < slot_len).astype(F32)[:, None]

    valid = [valid_of(k) for k in range(n_rep)]

    def mine(value, axis):
        return lax.dynamic_slice_in_dim(value, rep_at * part, part, axis)

    x_all = rep_gather(block_input)
    small = jnp.concatenate(
        [
            mine(x_proj, 0),
            mine(dt_proj, 1).T,
            mine(a_log, 1).T,
            mine(conv_weight, 1).T,
            mine(conv_bias, 0)[:, None],
            mine(dt_bias, 0)[:, None],
            mine(d_skip, 0)[:, None],
            norm_gain.reshape(part, -1),
        ],
        axis=1,
    )
    in_mine = lax.dynamic_index_in_dim(
        in_proj.reshape(in_proj.shape[0], 2, n_shard, n_rep, part), rep_at, 3, keepdims=False
    ).reshape(in_proj.shape[0], 2 * chans)
    small_all = lax.all_gather(small, "shard", axis=0, tiled=True)
    in_all = lax.all_gather(in_mine, "shard", axis=0, tiled=True)
    out_all = lax.all_gather(mine(out_proj, 0), "shard", axis=0, tiled=True)
    cot_all = rep_gather(cotangent)

    cut = [x_proj.shape[1], rank, states, taps, 1, 1, 1]
    ends = [sum(cut[:i + 1]) for i in range(len(cut))]
    xproj_all = small_all[:, :ends[0]]
    dtproj_all = small_all[:, ends[0]:ends[1]].T
    log_rates = small_all[:, ends[1]:ends[2]].T.astype(F32)
    wb = small_all[:, ends[2]:ends[4]].T.astype(F32)
    dtbias_all = small_all[:, ends[4]].astype(F32)
    skip_all = small_all[:, ends[5]].astype(F32)
    gain_f = small_all[:, ends[6]:].reshape(width).astype(F32)

    def norm(value):
        value = value.astype(F32)
        scale = lax.rsqrt(jnp.mean(value * value, axis=1, keepdims=True) + EPSILON)
        return (value * scale * gain_f[None, :]).astype(BF16)

    normed = jnp.concatenate([norm(value) for value in x_all], axis=0)
    conv_in = jnp.dot(normed, in_all[:, :chans], preferred_element_type=F32).astype(BF16)
    gate_in = jnp.dot(normed, in_all[:, chans:], preferred_element_type=F32)
    last = conv_in.reshape(n_rep, rows, chans)[:, rows - (taps - 1):]
    edge = shifted(last, 1).astype(F32) * keep_prev
    edge = jnp.concatenate([jnp.zeros((n_rep, 8 - (taps - 1), chans), F32), edge], axis=1)
    conv_out = conv_pass(conv_in, edge, wb, n_rep)
    proj = lax.dot_general(xproj_all, conv_out, (((0,), (1,)), ((), ())), preferred_element_type=F32)
    proj = jnp.concatenate(
        rep_sum([proj[:, k * rows:(k + 1) * rows] for k in range(n_rep)]), axis=1
    )
    step_low = proj[:rank].astype(BF16)
    b_all = jnp.broadcast_to(proj[rank:rank + states].T[:, :, None], (tokens, states, LN))
    c_all = jnp.broadcast_to(proj[rank + states:].T[:, :, None], (tokens, states, LN))
    step_pre = contract_rows(step_low, dtproj_all) + dtbias_all[None, :]
    step = jax.nn.softplus(step_pre)
    rates = -jnp.exp(log_rates)
    rates2 = rates * LOG2E
    back = jnp.concatenate(
        [(cot_all[k].astype(F32) * valid[k]).astype(BF16) for k in range(n_rep)], axis=0
    )
    sig = jax.nn.sigmoid(gate_in)
    g_gated = contract_cols(back, out_all)
    g_scanned = g_gated * (gate_in * sig)
    local_end, local_adj = first_pass(step, conv_out, g_scanned, b_all, c_all, rates2, n_rep)
    total = jnp.sum(step.reshape(n_rep, rows, chans), axis=1)
    start_state = carry_in(total, local_end, rates, in_slot, False)
    end_grad = carry_in(total, local_adj, rates, span - 1 - in_slot, True)
    scanned, kept = fwd_pass(step, conv_out, b_all, c_all, rates2, start_state, n_rep)
    scanned = scanned + skip_all[None, :] * conv_out.astype(F32)
    gated = (scanned * (gate_in * sig)).astype(BF16)
    g_gate = (g_gated * scanned * sig * (1.0 + gate_in * (1.0 - sig))).astype(BF16)
    branch = jnp.dot(gated, out_all, preferred_element_type=F32)
    branch = rep_scatter([branch[k * rows:(k + 1) * rows] for k in range(n_rep)])
    input_f = block_input.astype(F32)
    activations = (input_f + valid[0] * branch).astype(BF16)

    def scatter(value):
        return lax.psum_scatter(value.astype(BF16), "shard", scatter_dimension=0, tiled=True)

    grad_out = scatter(contract_rows(gated, back))
    grad_gate = scatter(contract_rows(normed, g_gate))
    g_step, g_scan_in, g_b, g_c, g_a = bwd_pass(
        step, conv_out, g_scanned, b_all, c_all, rates2, kept, end_grad, n_rep
    )
    g_pre_step = g_step * jax.nn.sigmoid(step_pre)
    grad_dt_bias = jnp.sum(g_pre_step, axis=0)
    g_lin = g_pre_step.astype(BF16)
    grad_dt_proj = contract_rows(g_lin, step_low.T)
    g_low = contract_cols(dtproj_all, g_lin)
    g_proj = jnp.concatenate([g_low, jnp.sum(g_b, axis=0).T, jnp.sum(g_c, axis=0).T], axis=0)
    g_proj = jnp.concatenate(
        rep_sum([g_proj[:, k * rows:(k + 1) * rows] for k in range(n_rep)]), axis=1
    )
    g_proj = g_proj.T.astype(BF16)
    grad_x_proj = contract_rows(conv_out, g_proj)
    conv_f = conv_out.astype(F32)
    g_scan_in = g_scan_in + skip_all[None, :] * g_scanned
    grad_skip = jnp.sum(g_scanned * conv_f, axis=0)
    g_in, head, tail, grad_wb = conv_back(g_proj, xproj_all, g_scan_in, conv_in, edge, wb, n_rep)
    after = shifted(head, -1) * keep_next
    joined = jnp.concatenate([jnp.zeros_like(after), after], axis=1)
    fix = tail
    for k in range(taps - 1):
        at = taps - 1 - k
        fix = fix + wb[k][None, None, :] * joined[:, at:at + 8]
    g_in = g_in.reshape(n_rep, rows, chans).at[:, rows - 8:].set(fix.astype(BF16))
    g_in = g_in.reshape(tokens, chans)
    grad_conv = scatter(contract_rows(normed, g_in))
    g_normed = contract_cols(g_in, in_all[:, :chans]) + contract_cols(g_gate, in_all[:, chans:])
    g_normed = rep_scatter([g_normed[k * rows:(k + 1) * rows] for k in range(n_rep)])
    scale = lax.rsqrt(jnp.mean(input_f * input_f, axis=1, keepdims=True) + EPSILON)
    grad_gain = jnp.sum(g_normed * input_f * scale, axis=0)
    g_hat = g_normed * gain_f[None, :]
    input_grad = (
        cotangent.astype(F32)
        + scale * g_hat
        - input_f * (scale * scale * scale) * jnp.mean(g_hat * input_f, axis=1, keepdims=True)
    )
    grad_a_log = rates * jnp.sum(g_a, axis=0)
    grad_small = scatter(
        jnp.concatenate(
            [
                grad_x_proj,
                grad_dt_proj,
                grad_a_log.T,
                jnp.sum(grad_wb, axis=0).T,
                grad_dt_bias[:, None],
                grad_skip[:, None],
                grad_gain.reshape(chans, -1),
            ],
            axis=1,
        )
    )

    def everyone(value):
        return lax.all_gather(value, "rep", axis=0)

    all_out = everyone(grad_out).reshape(wide, width).astype(F32)
    all_in = jnp.stack([everyone(grad_conv), everyone(grad_gate)], axis=0)
    all_in = all_in.reshape(2, n_rep, -1, n_shard, part).transpose(2, 0, 3, 1, 4)
    all_in = all_in.reshape(in_proj.shape).astype(F32)
    all_small = everyone(grad_small).astype(F32)
    all_gain = jnp.sum(all_small[:, :, ends[6]:], axis=0).reshape(norm_gain.shape)
    all_small = all_small.reshape(wide, -1)
    return (
        activations,
        input_grad,
        all_gain,
        all_in,
        all_small[:, ends[2]:ends[3]].T,
        all_small[:, ends[3]],
        all_small[:, :ends[0]],
        all_small[:, ends[0]:ends[1]].T,
        all_small[:, ends[4]],
        all_small[:, ends[1]:ends[2]].T,
        all_small[:, ends[5]],
        all_out,
    )


def solution(mesh):
    tokens = P(("rep", "shard"), None)
    rows, cols, line, full = (P("shard", None), P(None, "shard"), P("shard"), P())
    return jax.shard_map(
        on_device,
        mesh=mesh,
        in_specs=(tokens, tokens, full, full, line, rows, cols, line, rows, cols, line, cols, line, rows),
        out_specs=(tokens, tokens, line, rows, cols, line, rows, cols, line, cols, line, rows),
        check_vma=False,
    )
```

```python
from functools import partial

import jax
import jax.numpy as jnp
from jax import lax
from jax.experimental import pallas as pl
from jax.experimental.pallas import tpu as pltpu
from jax.sharding import PartitionSpec as P

EPSILON = 1e-05
SPAN_TOKENS = 4096
F32=jnp.float32; BF16=jnp.bfloat16
LN=128
def first_kernel(U, dt_ref, x_ref, b_ref, a_ref, hend_ref, h_s, dtx_s):
    TC, EG = dt_ref.shape
    NT = EG//LN
    c = pl.program_id(2)
    @pl.when(c == 0)
    def _():
        h_s[...] = jnp.zeros_like(h_s)
    dtx_s[...] = dt_ref[...]*x_ref[...].astype(F32)
    sl = [slice(j*LN,(j+1)*LN) for j in range(NT)]
    A = [a_ref[:, s] for s in sl]
    def body(i, carry):
        h = list(carry)
        rows = pl.ds(pl.multiple_of(i*U,U),U)
        dv, xv = dt_ref.at[rows], dtx_s.at[rows]
        for k in range(U):
            bt = b_ref[i*U+k]
            for j in range(NT):
                a = jnp.exp2(dv[k:k+1, sl[j]]*A[j])
                h[j] = a*h[j] + xv[k:k+1, sl[j]]*bt
        return tuple(h)
    h = lax.fori_loop(0, TC//U, body, tuple(h_s[:, s] for s in sl))
    for j in range(NT): h_s[:, sl[j]] = h[j]
    @pl.when(c == pl.num_programs(2)-1)
    def _():
        hend_ref[...] = h_s[...]

def first_pass(dt, x, bx, a2, Q, TC=128, EG=512, U=8):
    T,E = dt.shape; N = a2.shape[0]; L=T//Q; NC=L//TC; NE=E//EG
    row = pl.BlockSpec((TC,EG), lambda q,e,c:(q*NC+c, e))
    sp = pl.BlockSpec((TC,N,LN), lambda q,e,c:(q*NC+c,0,0))
    st = pl.BlockSpec((None,N,EG), lambda q,e,c:(q,0,e))
    return pl.pallas_call(partial(first_kernel,U), grid=(Q,NE,NC),
        in_specs=[row,row,sp,pl.BlockSpec((N,EG), lambda q,e,c:(0,e))],
        out_specs=st,
        out_shape=jax.ShapeDtypeStruct((Q,N,E),F32),
        scratch_shapes=[pltpu.VMEM((N,EG),F32),pltpu.VMEM((TC,EG),F32)],
        compiler_params=pltpu.CompilerParams(dimension_semantics=("arbitrary",)*3, vmem_limit_bytes=60<<20),
        name="first_pass",
        cost_estimate=pl.CostEstimate(flops=5*T*E*N, bytes_accessed=10*T*E, transcendentals=T*E*N))(dt,x,bx,a2)

LOG2E = 1.4426950408889634


def sums(tb):
    return (lax.broadcasted_iota(jnp.int32,(tb,tb*8),1)//8 == lax.broadcasted_iota(jnp.int32,(tb,tb*8),0)).astype(BF16)

def fwd_kernel(U, dt_ref, x_ref, gate_ref, gg_ref, b_ref, c_ref, a_ref, skip_ref, h0_ref,
               out_ref, gz_ref, g_ref, ck_ref, adj_ref, h_s, p_s, r_s, q_s, y_s, dtx_s):
    TC, EG = dt_ref.shape
    NT = EG//LN
    c = pl.program_id(2)
    @pl.when(c == 0)
    def _():
        h_s[...] = h0_ref[...]; p_s[...] = jnp.ones_like(p_s); r_s[...] = jnp.zeros_like(r_s)
        q_s[...] = jnp.zeros_like(q_s)
    ck_ref[...] = h_s[...]
    dtx_s[...] = dt_ref[...]*x_ref[...].astype(F32)
    gate = gate_ref[...]
    g_ref[...] = gg_ref[...]*(gate*jax.nn.sigmoid(gate))
    sl = [slice(j*LN,(j+1)*LN) for j in range(NT)]
    A = [a_ref[:, s] for s in sl]
    S = sums(U)
    G = TC//U
    def reduce(i):
        y_s[pl.ds(pl.multiple_of(i*U,U),U),:] = jnp.dot(S, q_s[...], preferred_element_type=F32)
    def body(i, carry):
        reduce(jnp.maximum(i-1,0))
        h, p, r = [list(v) for v in carry]
        rows = pl.ds(pl.multiple_of(i*U,U),U)
        dv, xv, gv = dt_ref.at[rows], dtx_s.at[rows], g_ref.at[rows]
        low = [None]*NT
        for k in range(U):
            t = i*U+k
            bt = b_ref[t]; ct = c_ref[t]
            for j in range(NT):
                a = jnp.exp2(dv[k:k+1, sl[j]]*A[j])
                h[j] = a*h[j] + xv[k:k+1, sl[j]]*bt
                p[j] = p[j]*a
                r[j] = r[j] + p[j]*(ct*gv[k:k+1, sl[j]])
                q = h[j]*ct
                q = q[:8]+q[8:]
                if k % 2 == 0: low[j] = q
                else: q_s[k*8-8:k*8+8, sl[j]] = jnp.concatenate([low[j],q],axis=0).astype(BF16)
        return tuple(h), tuple(p), tuple(r)
    init = tuple(tuple(s_[:, s] for s in sl) for s_ in (h_s, p_s, r_s))
    h, p, r = lax.fori_loop(0, G, body, init)
    reduce(G-1)
    for j in range(NT):
        h_s[:, sl[j]] = h[j]; p_s[:, sl[j]] = p[j]; r_s[:, sl[j]] = r[j]
    gate = gate_ref[...]
    sig = jax.nn.sigmoid(gate)
    y = y_s[...] + skip_ref[...]*x_ref[...].astype(F32)
    out_ref[...] = (y*(gate*sig)).astype(BF16)
    gz_ref[...] = (gg_ref[...]*y*sig*(1.0+gate*(1.0-sig))).astype(BF16)
    @pl.when(c == pl.num_programs(2)-1)
    def _(): adj_ref[...] = r_s[...]

def fwd_pass(dt, x, gate, gg, bx, cx, a2, skip, h0, Q, TC=64, EG=512, U=8):
    T,E = dt.shape; N = a2.shape[0]; L=T//Q; NC=L//TC; NE=E//EG
    row = pl.BlockSpec((TC,EG), lambda q,e,c:(q*NC+c, e))
    sp = pl.BlockSpec((TC,N,LN), lambda q,e,c:(q*NC+c,0,0))
    st = pl.BlockSpec((None,N,EG), lambda q,e,c:(q,0,e))
    return pl.pallas_call(partial(fwd_kernel,U), grid=(Q,NE,NC),
        in_specs=[row,row,row,row,sp,sp,pl.BlockSpec((N,EG), lambda q,e,c:(0,e)), pl.BlockSpec((1,EG), lambda q,e,c:(0,e)), st],
        out_specs=[row, row, row, pl.BlockSpec((None,N,EG), lambda q,e,c:(q*NC+c,0,e)), st],
        out_shape=[jax.ShapeDtypeStruct((T,E),BF16)]*2 + [jax.ShapeDtypeStruct((T,E),F32),
            jax.ShapeDtypeStruct((Q*NC,N,E),F32), jax.ShapeDtypeStruct((Q,N,E),F32)],
        scratch_shapes=[pltpu.VMEM((N,EG),F32)]*3 + [pltpu.VMEM((U*8,EG),BF16)] + [pltpu.VMEM((TC,EG),F32)]*2,
        compiler_params=pltpu.CompilerParams(dimension_semantics=("arbitrary",)*3, vmem_limit_bytes=60<<20),
        name="fwd_pass",
        cost_estimate=pl.CostEstimate(flops=11*T*E*N, bytes_accessed=22*T*E, transcendentals=T*E*N))(dt,x,gate,gg,bx,cx,a2,skip,h0)

def bwd_kernel(U, n_in, *refs):
    dt_ref, x_ref, g_ref, b_ref, c_ref, a_ref, skip_ref, ck_ref, mu0_ref = refs[:9]
    (gl_ref, gx_ref, gb_ref, gc_ref, ga_ref, su_ref,
     mu_s, ga_s, su_s, qa_s, qb_s, zb_s, zc_s, sa_s, sb_s, dtx_s, a_s, h_s) = refs[n_in:]
    TC, EG = dt_ref.shape
    N = a_ref.shape[0]
    NT = EG//LN
    c = pl.program_id(2)
    @pl.when(c == 0)
    def _():
        mu_s[...] = mu0_ref[...]
        for v in (ga_s, su_s, qa_s, qb_s, zb_s, zc_s): v[...] = jnp.zeros_like(v)
    dtx_s[...] = dt_ref[...]*x_ref[...].astype(F32)
    sl = [slice(j*LN,(j+1)*LN) for j in range(NT)]
    A = [a_ref[:, s] for s in sl]
    h_s[0] = ck_ref[...]
    G = TC//U
    def up(i, carry):
        h = list(carry)
        rows = pl.ds(pl.multiple_of(i*U,U),U)
        dv, xv = dt_ref.at[rows], dtx_s.at[rows]
        for k in range(U):
            t = i*U+k
            bt = b_ref[t]
            for j in range(NT):
                a = jnp.exp2(dv[k:k+1, sl[j]]*A[j])
                h[j] = a*h[j] + xv[k:k+1, sl[j]]*bt
                a_s[t, :, sl[j]] = a
                h_s[t+1, :, sl[j]] = h[j]
        return tuple(h)
    h = lax.fori_loop(0, G, up, tuple(ck_ref[:, s] for s in sl))
    S = sums(U)
    ones = jnp.ones((8,LN),BF16)
    nt = (((1,),(1,)),((),()))
    def reduce(i):
        rows = pl.ds(pl.multiple_of(i*U,U),U)
        sa_s[rows,:] = jnp.dot(S, qa_s[...], preferred_element_type=F32)
        sb_s[rows,:] = jnp.dot(S, qb_s[...], preferred_element_type=F32)
        cols = pl.ds(pl.multiple_of(i*(U*N),U*N),U*N)
        gb_ref[:,cols] = lax.dot_general(ones, zb_s[...], nt, preferred_element_type=F32)[:1]
        gc_ref[:,cols] = lax.dot_general(ones, zc_s[...], nt, preferred_element_type=F32)[:1]
    def down(ii, carry):
        i = G-1-ii
        reduce(jnp.minimum(i+1,G-1))
        mu, ga, h = [list(v) for v in carry]
        rows = pl.ds(pl.multiple_of(i*U,U),U)
        dv, gv, xv = dt_ref.at[rows], g_ref.at[rows], dtx_s.at[rows]
        la, lb = [None]*NT, [None]*NT
        for k in reversed(range(U)):
            t = i*U+k
            bt = b_ref[t]; ct = c_ref[t]
            zb = zc = None
            for j in range(NT):
                gr = gv[k:k+1, sl[j]]
                lam = mu[j] + ct*gr
                zcj = h[j]*gr
                zbj = lam*xv[k:k+1, sl[j]]
                zc = zcj if j == 0 else zc+zcj
                zb = zbj if j == 0 else zb+zbj
                mu[j] = a_s[t,:,sl[j]]*lam
                h[j] = h_s[t,:,sl[j]]
                w = mu[j]*h[j]
                ga[j] = ga[j] + dv[k:k+1, sl[j]]*w
                qa = A[j]*w
                qb = lam*bt
                qa = qa[:8]+qa[8:]
                qb = qb[:8]+qb[8:]
                if k % 2: la[j], lb[j] = qa, qb
                else:
                    qa_s[k*8:k*8+16, sl[j]] = jnp.concatenate([qa,la[j]],axis=0).astype(BF16)
                    qb_s[k*8:k*8+16, sl[j]] = jnp.concatenate([qb,lb[j]],axis=0).astype(BF16)
            zb_s[k*N:k*N+N,:] = zb.astype(BF16)
            zc_s[k*N:k*N+N,:] = zc.astype(BF16)
        return tuple(mu), tuple(ga), tuple(h)
    init = tuple(tuple(s_[:, s] for s in sl) for s_ in (mu_s, ga_s)) + (h,)
    mu, ga, h = lax.fori_loop(0, G, down, init)
    reduce(0)
    for j in range(NT): ga_s[:, sl[j]] = ga[j]; mu_s[:, sl[j]] = mu[j]
    d = dt_ref[...]; x = x_ref[...].astype(F32); g = g_ref[...]
    sb = sb_s[...]
    gx_ref[...] = d*sb + skip_ref[...]*g
    sig = jnp.where(d < 0.03, d*(1.0-d*(0.5-d*(1.0/6.0-d*(1.0/24.0)))), 1.0-jnp.exp(-d))
    gp = (sa_s[...]*(1.0/LOG2E) + x*sb)*sig
    gl_ref[...] = gp.astype(BF16)
    su_s[...] = su_s[...] + jnp.concatenate([jnp.sum(gp,axis=0,keepdims=True), jnp.sum(g*x,axis=0,keepdims=True)],axis=0)
    @pl.when(c == pl.num_programs(2)-1)
    def _():
        ga_ref[...] = ga_s[...]; su_ref[...] = su_s[...]

def bwd_pass(dt, x, g, bx, cx, a2, skip, ck, mu0, Q, at, prev, waits, TC=64, EG=512, U=8):
    T,E = dt.shape; N = a2.shape[0]; L=T//Q; NC=L//TC; NE=E//EG
    row = pl.BlockSpec((TC,EG), lambda q,e,c:(q*NC+NC-1-c, at))
    sp = pl.BlockSpec((TC,N,LN), lambda q,e,c:(q*NC+NC-1-c,0,0))
    st = pl.BlockSpec((None,N,EG), lambda q,e,c:(q,0,at))
    nb = pl.BlockSpec((None,1,TC*N), lambda q,e,c:(at,0,q*NC+NC-1-c))
    args = (dt,x,g,bx,cx,a2,skip,ck,mu0)
    n_in = len(args)+len(prev)+len(waits)
    return pl.pallas_call(partial(bwd_kernel,U,n_in), grid=(Q,1,NC),
        in_specs=[row,row,row,sp,sp,pl.BlockSpec((N,EG), lambda q,e,c:(0,at)), pl.BlockSpec((1,EG), lambda q,e,c:(0,at)),
            pl.BlockSpec((None,N,EG), lambda q,e,c:(q*NC+NC-1-c,0,at)), st]+[pl.BlockSpec(memory_space=pl.ANY)]*(len(prev)+len(waits)),
        out_specs=[row,row,nb,nb,st,pl.BlockSpec((None,2,EG), lambda q,e,c:(q,0,at))],
        out_shape=[jax.ShapeDtypeStruct((T,E),BF16), jax.ShapeDtypeStruct((T,E),F32)]+[jax.ShapeDtypeStruct((NE,1,T*N),F32)]*2
            +[jax.ShapeDtypeStruct((Q,N,E),F32), jax.ShapeDtypeStruct((Q,2,E),F32)],
        input_output_aliases={len(args)+i: i for i in range(len(prev))},
        scratch_shapes=[pltpu.VMEM((N,EG),F32)]*2+[pltpu.VMEM((2,EG),F32)]+[pltpu.VMEM((U*8,EG),BF16)]*2+[pltpu.VMEM((U*N,LN),BF16)]*2
            +[pltpu.VMEM((TC,EG),F32)]*3+[pltpu.VMEM((TC,N,EG),F32), pltpu.VMEM((TC+1,N,EG),F32)],
        compiler_params=pltpu.CompilerParams(dimension_semantics=("arbitrary",)*3, vmem_limit_bytes=62<<20),
        name="bwd_pass",
        cost_estimate=pl.CostEstimate(flops=20*T*EG*N, bytes_accessed=22*T*EG, transcendentals=T*EG*N))(*args,*prev,*waits)


def spread_kernel(in_ref, *refs):
    refs[-1][...] = jnp.concatenate([in_ref[r].astype(F32) for r in range(in_ref.shape[0])], axis=1)


def spread(pieces, rows, cols, part, half, prev):
    n_rep, n_shard = (pieces.shape[0], pieces.shape[2] // part)
    return pl.pallas_call(
        spread_kernel,
        grid=(n_shard,),
        in_specs=[pl.BlockSpec((n_rep, rows, part), lambda s: (0, 0, s))] + [pl.BlockSpec(memory_space=pl.ANY)] * len(prev),
        out_specs=pl.BlockSpec((rows, n_rep * part), lambda s: (0, half * n_shard + s)),
        out_shape=jax.ShapeDtypeStruct((rows, cols), F32),
        input_output_aliases={1 + i: i for i in range(len(prev))},
        compiler_params=pltpu.CompilerParams(dimension_semantics=("arbitrary",)),
        name="spread",
        cost_estimate=pl.CostEstimate(flops=0, bytes_accessed=3 * rows * cols, transcendentals=0),
    )(pieces, *prev)


def pick_kernel(count, at_ref, in_ref, out_ref):
    part = out_ref.shape[1] // count
    wide = in_ref.shape[1] // count
    at = at_ref[0] * part
    for k in range(count):
        out_ref[:, k * part:(k + 1) * part] = in_ref[:, pl.ds(pl.multiple_of(k * wide + at, part), part)]


def pick(value, at, n_shard, part, half):
    rows, cols = value.shape
    count = 4 if n_shard % 4 == 0 else n_shard
    steps = n_shard // count
    wide = cols // (2 * steps)
    return pl.pallas_call(
        partial(pick_kernel, count),
        grid_spec=pltpu.PrefetchScalarGridSpec(
            num_scalar_prefetch=1,
            grid=(steps,),
            in_specs=[pl.BlockSpec((rows, wide), lambda s, a: (0, half * steps + s))],
            out_specs=pl.BlockSpec((rows, count * part), lambda s, a: (0, s)),
        ),
        out_shape=jax.ShapeDtypeStruct((rows, n_shard * part), value.dtype),
        compiler_params=pltpu.CompilerParams(dimension_semantics=("arbitrary",)),
        name="pick",
        cost_estimate=pl.CostEstimate(flops=0, bytes_accessed=2 * rows * cols, transcendentals=0),
    )(at, value)


def conv_kernel(x_ref, edge_ref, w_ref, o_ref, x_s):
    L = x_ref.shape[0]
    taps = w_ref.shape[0] - 1
    x_s[0:8, :] = edge_ref[...]
    x_s[8:, :] = x_ref[...].astype(F32)
    pre = jnp.broadcast_to(w_ref[taps:taps + 1, :], x_ref.shape)
    for k in range(taps):
        at = 8 - (taps - 1) + k
        pre = pre + w_ref[k:k + 1, :] * x_s[at:at + L, :]
    o_ref[...] = (pre * jax.nn.sigmoid(pre)).astype(BF16)


def conv_pass(conv_in, edge, wb, Q, EB=256):
    T, E = conv_in.shape
    L = T // Q
    row = pl.BlockSpec((L, EB), lambda q, e: (q, e))
    return pl.pallas_call(
        conv_kernel,
        grid=(Q, E // EB),
        in_specs=[
            row,
            pl.BlockSpec((None, 8, EB), lambda q, e: (q, 0, e)),
            pl.BlockSpec((wb.shape[0], EB), lambda q, e: (0, e)),
        ],
        out_specs=row,
        out_shape=jax.ShapeDtypeStruct((T, E), BF16),
        scratch_shapes=[pltpu.VMEM((L + 8, EB), F32)],
        compiler_params=pltpu.CompilerParams(dimension_semantics=("arbitrary",) * 2),
        name="conv_pass",
        cost_estimate=pl.CostEstimate(flops=12 * T * E, bytes_accessed=4 * T * E, transcendentals=T * E),
    )(conv_in, edge, wb)


def conv_back_kernel(n_in, *refs):
    gp_ref, xp_ref, gx_ref, x_ref, edge_ref, w_ref = refs[:6]
    gi_ref, head_ref, tail_ref, gw_ref, x_s, g_s = refs[n_in:]
    L = x_ref.shape[0]
    taps = w_ref.shape[0] - 1
    x_s[0:8, :] = edge_ref[...]
    x_s[8:, :] = x_ref[...].astype(F32)
    at = [8 - (taps - 1) + k for k in range(taps)]
    pre = jnp.broadcast_to(w_ref[taps:taps + 1, :], x_ref.shape)
    for k in range(taps):
        pre = pre + w_ref[k:k + 1, :] * x_s[at[k]:at[k] + L, :]
    s = jax.nn.sigmoid(pre)
    g_out = contract_cols(gp_ref[...], xp_ref[...]) + gx_ref[...]
    g_pre = g_out * s * (1.0 + pre * (1.0 - s))
    g_s[0:L, :] = g_pre
    g_s[L:, :] = jnp.zeros((8, x_ref.shape[1]), F32)
    gw = [jnp.sum(g_pre * x_s[at[k]:at[k] + L, :], axis=0, keepdims=True) for k in range(taps)]
    gw.append(jnp.sum(g_pre, axis=0, keepdims=True))
    gw_ref[...] = jnp.concatenate(gw, axis=0)
    head_ref[...] = g_s[0:8, :]
    g_in = jnp.zeros(x_ref.shape, F32)
    for k in range(taps):
        g_in = g_in + w_ref[k:k + 1, :] * g_s[taps - 1 - k:taps - 1 - k + L, :]
    gi_ref[...] = g_in.astype(BF16)
    tail_ref[...] = g_in[L - 8:, :]


def conv_back(g_projected, x_proj, gx, conv_in, edge, wb, waits, Q, EB=256):
    T, E = conv_in.shape
    L = T // Q
    row = pl.BlockSpec((L, EB), lambda q, e: (q, e))
    edges = pl.BlockSpec((None, 8, EB), lambda q, e: (q, 0, e))
    rows = wb.shape[0]
    return pl.pallas_call(
        partial(conv_back_kernel, 6 + len(waits)),
        grid=(Q, E // EB),
        in_specs=[
            pl.BlockSpec((L, g_projected.shape[1]), lambda q, e: (q, 0)),
            pl.BlockSpec((EB, x_proj.shape[1]), lambda q, e: (e, 0)),
            row,
            row,
            edges,
            pl.BlockSpec((rows, EB), lambda q, e: (0, e)),
        ] + [pl.BlockSpec(memory_space=pl.ANY)] * len(waits),
        out_specs=[row, edges, edges, pl.BlockSpec((None, rows, EB), lambda q, e: (q, 0, e))],
        out_shape=[
            jax.ShapeDtypeStruct((T, E), BF16),
            jax.ShapeDtypeStruct((Q, 8, E), F32),
            jax.ShapeDtypeStruct((Q, 8, E), F32),
            jax.ShapeDtypeStruct((Q, rows, E), F32),
        ],
        scratch_shapes=[pltpu.VMEM((L + 8, EB), F32)] * 2,
        compiler_params=pltpu.CompilerParams(dimension_semantics=("arbitrary",) * 2),
        name="conv_back",
        cost_estimate=pl.CostEstimate(flops=400 * T * E, bytes_accessed=10 * T * E, transcendentals=T * E),
    )(g_projected, x_proj, gx, conv_in, edge, wb, *waits)


def contract_rows(left, right):
    return lax.dot_general(left, right, (((0,), (0,)), ((), ())), preferred_element_type=F32)


def contract_cols(left, right):
    return lax.dot_general(left, right, (((1,), (1,)), ((), ())), preferred_element_type=F32)


def swap(value, flip):
    return lax.ppermute(value, "rep", [(i, i ^ flip) for i in range(lax.axis_size("rep"))])


def shifted(value, steps):
    count = lax.axis_size("shard")
    first, last = (max(0, -steps), min(count, count - steps))
    return lax.ppermute(value, "shard", [(i, i + steps) for i in range(first, last)])


def rep_gather(value):
    far = swap(value, 2)
    return [value, swap(value, 1), far, swap(far, 1)]


def rep_near(parts):
    low = [part.astype(BF16) for part in parts]
    near = [swap(low[k], 1).astype(F32) for k in (1, 3)]
    return parts[0] + near[0], (parts[2] + near[1]).astype(BF16)


def rep_far(mine, other):
    return mine + swap(other, 2).astype(F32)


def rep_sum(parts):
    near = [swap(parts[k], 1) for k in (1, 3)]
    pair = [parts[0] + near[0], parts[2] + near[1]]
    far = [swap(value, 2) for value in pair]
    full = [pair[0] + far[1], pair[1] + far[0]]
    over = [swap(value, 1) for value in full]
    return [full[0], over[0], full[1], over[1]]


def add_all(value, axis):
    step = 1
    while step < lax.axis_size(axis):
        value = value + lax.ppermute(value, axis, [(i, i ^ step) for i in range(lax.axis_size(axis))])
        step *= 2
    return value


def carry_in(total, state, rates, place, reverse):
    sign = -1 if reverse else 1
    span = lax.axis_size("shard")
    both = shifted(jnp.concatenate([state, total[:, None, :]], axis=1), sign)
    both = both * jnp.where(place >= 1, 1.0, 0.0)
    step = 1
    while step < min(span, 8):
        far = shifted(both, sign * step) * jnp.where(place >= step, 1.0, 0.0)
        total = both[:, -1:]
        state = both[:, :-1] + jnp.exp(rates[None] * total) * far[:, :-1]
        both = jnp.concatenate([state, total + far[:, -1:]], axis=1)
        step *= 2
    return both[:, :-1]


def on_device(
    block_input,
    cotangent,
    seq_lengths,
    slot_order,
    norm_gain,
    in_proj,
    conv_weight,
    conv_bias,
    x_proj,
    dt_proj,
    dt_bias,
    a_log,
    d_skip,
    out_proj,
):
    n_shard, n_rep = (lax.axis_size("shard"), lax.axis_size("rep"))
    shard_at, rep_at = (lax.axis_index("shard"), lax.axis_index("rep"))
    rows, width = block_input.shape
    tokens = n_rep * rows
    taps, wide = conv_weight.shape
    part = wide // n_rep
    chans = part * n_shard
    rank = dt_proj.shape[0]
    states = a_log.shape[0]
    span = max(1, min(n_shard, SPAN_TOKENS // rows))
    in_slot = shard_at % span
    keep_prev = (in_slot != 0).astype(F32)
    keep_next = (in_slot != span - 1).astype(F32)
    places = in_slot * rows + jnp.arange(rows, dtype=jnp.int32)

    def valid_of(flip):
        slot_at = ((rep_at ^ flip) * n_shard + shard_at) // span
        slot_len = jnp.sum(jnp.where(slot_order == slot_at, seq_lengths, 0))
        return (places < slot_len).astype(F32)[:, None]

    valid = [valid_of(k) for k in range(n_rep)]

    def mine(value, axis):
        return lax.dynamic_slice_in_dim(value, rep_at * part, part, axis)

    x_all = rep_gather(block_input)
    small = jnp.concatenate(
        [
            mine(x_proj, 0),
            mine(dt_proj, 1).T,
            mine(a_log, 1).T,
            mine(conv_weight, 1).T,
            mine(conv_bias, 0)[:, None],
            mine(dt_bias, 0)[:, None],
            mine(d_skip, 0)[:, None],
            norm_gain.reshape(part, -1),
        ],
        axis=1,
    )
    if part % LN:
        in_mine = lax.dynamic_index_in_dim(
            in_proj.reshape(in_proj.shape[0], 2, n_shard, n_rep, part), rep_at, 3, keepdims=False
        ).reshape(in_proj.shape[0], 2, chans)
        in_conv, in_gate = (in_mine[:, 0], in_mine[:, 1])
    else:
        in_conv, in_gate = [pick(in_proj, rep_at.reshape(1), n_shard, part, k) for k in range(2)]
    small_all = lax.all_gather(small, "shard", axis=0, tiled=True)
    conv_w = lax.all_gather(in_conv, "shard", axis=0, tiled=True)
    gate_w = lax.all_gather(in_gate, "shard", axis=0, tiled=True)
    out_all = lax.all_gather(mine(out_proj, 0), "shard", axis=0, tiled=True)
    cot_all = rep_gather(cotangent)

    cut = [x_proj.shape[1], rank, states, taps, 1, 1, 1]
    ends = [sum(cut[:i + 1]) for i in range(len(cut))]
    xproj_all = small_all[:, :ends[0]]
    dtproj_all = small_all[:, ends[0]:ends[1]].T
    log_rates = small_all[:, ends[1]:ends[2]].T.astype(F32)
    wb = small_all[:, ends[2]:ends[4]].T.astype(F32)
    dtbias_all = small_all[:, ends[4]].astype(F32)
    skip_all = small_all[:, ends[5]].astype(F32)
    gain_f = small_all[:, ends[6]:].reshape(width).astype(F32)

    def norm(value):
        value = value.astype(F32)
        scale = lax.rsqrt(jnp.mean(value * value, axis=1, keepdims=True) + EPSILON)
        return (value * scale * gain_f[None, :]).astype(BF16)

    normed = jnp.concatenate([norm(value) for value in x_all], axis=0)
    conv_in = jnp.dot(normed, conv_w, preferred_element_type=F32).astype(BF16)
    last = conv_in.reshape(n_rep, rows, chans)[:, rows - (taps - 1):]
    edge = shifted(last, 1).astype(F32) * keep_prev
    edge = jnp.concatenate([jnp.zeros((n_rep, 8 - (taps - 1), chans), F32), edge], axis=1)
    conv_out = conv_pass(conv_in, edge, wb, n_rep)
    proj = lax.dot_general(xproj_all, conv_out, (((0,), (1,)), ((), ())), preferred_element_type=F32)
    proj = jnp.concatenate(
        rep_sum([proj[:, k * rows:(k + 1) * rows] for k in range(n_rep)]), axis=1
    )
    step_low = proj[:rank].astype(BF16)
    b_all = jnp.broadcast_to(proj[rank:rank + states].T[:, :, None], (tokens, states, LN))
    c_all = jnp.broadcast_to(proj[rank + states:].T[:, :, None], (tokens, states, LN))
    step = jax.nn.softplus(contract_rows(step_low, dtproj_all) + dtbias_all[None, :])
    rates = -jnp.exp(log_rates)
    rates2 = rates * LOG2E
    gate_in = jnp.dot(normed, gate_w, preferred_element_type=F32)
    back = jnp.concatenate(
        [(cot_all[k].astype(F32) * valid[k]).astype(BF16) for k in range(n_rep)], axis=0
    )
    g_gated = contract_cols(back, out_all)
    skip = skip_all[None, :]
    local_end = first_pass(step, conv_out, b_all, rates2, n_rep)
    total = jnp.sum(step.reshape(n_rep, rows, chans), axis=1)
    start_state = carry_in(total, local_end, rates, in_slot, False)
    gated, g_gate, g_scanned, kept, local_adj = fwd_pass(
        step, conv_out, gate_in, g_gated, b_all, c_all, rates2, skip, start_state, n_rep
    )
    end_grad = carry_in(total, local_adj, rates, span - 1 - in_slot, True)
    branch = jnp.dot(gated, out_all, preferred_element_type=F32)
    near, other = rep_near([branch[k * rows:(k + 1) * rows] for k in range(n_rep)])
    pieces = width // chans
    held = in_proj.shape[0]
    local = [contract_rows(normed, g_gate).astype(BF16).reshape(n_shard, held, chans)]
    for k in range(pieces):
        piece = contract_rows(gated, back[:, k * chans:(k + 1) * chans])
        local.append(piece.astype(BF16).reshape(n_shard, part, chans))
    local = jnp.concatenate(local, axis=1).reshape(-1, chans)
    branch = rep_far(near, other)
    input_f = block_input.astype(F32)
    activations = (input_f + valid[0] * branch).astype(BF16)

    def scatter(value):
        return lax.psum_scatter(value, "shard", scatter_dimension=0, tiled=True)

    def everyone(value):
        return lax.all_gather(value, "rep", axis=0)

    early = scatter(local)
    back_args = (step, conv_out, g_scanned, b_all, c_all, rates2, skip, kept, end_grad, n_rep)
    prev, groups = ([], chans // 512)
    for k in range(groups):
        prev = bwd_pass(*back_args, k, prev, [local, other] if k == 0 else [activations])
    g_lin, g_scan_in, g_b, g_c, g_a, g_sums = prev
    grad_dt_bias, grad_skip = jnp.sum(g_sums, axis=0)
    grad_dt_proj = contract_rows(g_lin, step_low.T)
    g_low = contract_cols(dtproj_all, g_lin)
    g_b, g_c = [jnp.sum(v, axis=(0, 1)).reshape(tokens, states).T for v in (g_b, g_c)]
    g_proj = jnp.concatenate([g_low, g_b, g_c], axis=0)
    g_proj = jnp.concatenate(
        rep_sum([g_proj[:, k * rows:(k + 1) * rows] for k in range(n_rep)]), axis=1
    )
    g_proj = g_proj.T.astype(BF16)
    grad_x_proj = contract_rows(conv_out, g_proj)
    g_in, head, tail, grad_wb = conv_back(g_proj, xproj_all, g_scan_in, conv_in, edge, wb, [early], n_rep)
    after = shifted(head, -1) * keep_next
    joined = jnp.concatenate([jnp.zeros_like(after), after], axis=1)
    fix = tail
    for k in range(taps - 1):
        at = taps - 1 - k
        fix = fix + wb[k][None, None, :] * joined[:, at:at + 8]
    g_in = g_in.reshape(n_rep, rows, chans).at[:, rows - 8:].set(fix.astype(BF16))
    g_in = g_in.reshape(tokens, chans)
    grad_a_log = rates * jnp.sum(g_a, axis=0)
    small = [grad_x_proj, grad_dt_proj, grad_a_log.T, jnp.sum(grad_wb, axis=0).T, grad_dt_bias[:, None], grad_skip[:, None]]
    small.append(jnp.zeros((chans, -ends[6] % LN), F32))
    small = jnp.concatenate(small, axis=1).astype(BF16).reshape(n_shard, part, -1, LN)
    lanes = small.shape[2]
    small = small.transpose(0, 2, 1, 3).reshape(n_shard, -1, chans)
    late = contract_rows(normed, g_in).astype(BF16).reshape(n_shard, held, chans)
    late = scatter(jnp.concatenate([late, small], axis=1).reshape(-1, chans))
    half = rows // 2
    g_normed = []
    for at in (0, half):
        conv_rows = g_in.reshape(n_rep, rows, chans)[:, at:at + half].reshape(n_rep * half, chans)
        gate_rows = g_gate.reshape(n_rep, rows, chans)[:, at:at + half].reshape(n_rep * half, chans)
        both = contract_cols(conv_rows, conv_w) + contract_cols(gate_rows, gate_w)
        g_normed.append(rep_far(*rep_near([both[k * half:(k + 1) * half] for k in range(n_rep)])))
    g_normed = jnp.concatenate(g_normed, axis=0)
    scale = lax.rsqrt(jnp.mean(input_f * input_f, axis=1, keepdims=True) + EPSILON)
    grad_gain = jnp.sum(g_normed * input_f * scale, axis=0)
    g_hat = g_normed * gain_f[None, :]
    input_grad = (
        cotangent.astype(F32)
        + scale * g_hat
        - input_f * (scale * scale * scale) * jnp.mean(g_hat * input_f, axis=1, keepdims=True)
    )
    grad_gain = add_all(add_all(grad_gain.reshape(-1, LN), "rep"), "shard").reshape(width)
    all_gain = lax.dynamic_slice_in_dim(grad_gain, shard_at * norm_gain.shape[0], norm_gain.shape[0])
    all_early, all_late = (everyone(early), everyone(late))
    all_out = all_early[:, held:].reshape(n_rep, pieces, part, chans).transpose(0, 2, 1, 3)
    all_out = all_out.reshape(wide, width).astype(F32)
    if part % LN:
        all_in = jnp.stack([all_late[:, :held], all_early[:, :held]], axis=0)
        all_in = all_in.reshape(2, n_rep, -1, n_shard, part).transpose(2, 0, 3, 1, 4)
        all_in = all_in.reshape(in_proj.shape).astype(F32)
    else:
        all_in = spread(all_early, *in_proj.shape, part, 1, [])
        all_in = spread(all_late, *in_proj.shape, part, 0, [all_in])
    all_small = all_late[:, held:].reshape(n_rep, lanes, part, LN).transpose(0, 2, 1, 3)
    all_small = all_small.reshape(wide, lanes * LN).astype(F32)
    return (
        activations,
        input_grad,
        all_gain,
        all_in,
        all_small[:, ends[2]:ends[3]].T,
        all_small[:, ends[3]],
        all_small[:, :ends[0]],
        all_small[:, ends[0]:ends[1]].T,
        all_small[:, ends[4]],
        all_small[:, ends[1]:ends[2]].T,
        all_small[:, ends[5]],
        all_out,
    )


def solution(mesh):
    tokens = P(("rep", "shard"), None)
    rows, cols, line, full = (P("shard", None), P(None, "shard"), P("shard"), P())
    return jax.shard_map(
        on_device,
        mesh=mesh,
        in_specs=(tokens, tokens, full, full, line, rows, cols, line, rows, cols, line, cols, line, rows),
        out_specs=(tokens, tokens, line, rows, cols, line, rows, cols, line, cols, line, rows),
        check_vma=False,
    )
```

```python
from functools import partial

import jax
import jax.numpy as jnp
from jax import lax
from jax.experimental import pallas as pl
from jax.experimental.pallas import tpu as pltpu
from jax.sharding import PartitionSpec as P

EPSILON = 1e-05
SPAN_TOKENS = 4096
F32=jnp.float32; BF16=jnp.bfloat16
LN=128
def first_kernel(U, dt_ref, x_ref, b_ref, a_ref, hend_ref, h_s, dtx_s):
    TC, EG = dt_ref.shape
    NT = EG//LN
    c = pl.program_id(2)
    @pl.when(c == 0)
    def _():
        h_s[...] = jnp.zeros_like(h_s)
    dtx_s[...] = dt_ref[...]*x_ref[...].astype(F32)
    sl = [slice(j*LN,(j+1)*LN) for j in range(NT)]
    A = [a_ref[:, s] for s in sl]
    def body(i, carry):
        h = list(carry)
        rows = pl.ds(pl.multiple_of(i*U,U),U)
        dv, xv = dt_ref.at[rows], dtx_s.at[rows]
        for k in range(U):
            bt = b_ref[i*U+k]
            for j in range(NT):
                a = jnp.exp2(dv[k:k+1, sl[j]]*A[j])
                h[j] = a*h[j] + xv[k:k+1, sl[j]]*bt
        return tuple(h)
    h = lax.fori_loop(0, TC//U, body, tuple(h_s[:, s] for s in sl))
    for j in range(NT): h_s[:, sl[j]] = h[j]
    @pl.when(c == pl.num_programs(2)-1)
    def _():
        hend_ref[...] = h_s[...]

def first_pass(dt, x, bx, a2, Q, TC=128, EG=512, U=8):
    T,E = dt.shape; N = a2.shape[0]; L=T//Q; NC=L//TC; NE=E//EG
    row = pl.BlockSpec((TC,EG), lambda q,e,c:(q*NC+c, e))
    sp = pl.BlockSpec((TC,N,LN), lambda q,e,c:(q*NC+c,0,0))
    st = pl.BlockSpec((None,N,EG), lambda q,e,c:(q,0,e))
    return pl.pallas_call(partial(first_kernel,U), grid=(Q,NE,NC),
        in_specs=[row,row,sp,pl.BlockSpec((N,EG), lambda q,e,c:(0,e))],
        out_specs=st,
        out_shape=jax.ShapeDtypeStruct((Q,N,E),F32),
        scratch_shapes=[pltpu.VMEM((N,EG),F32),pltpu.VMEM((TC,EG),F32)],
        compiler_params=pltpu.CompilerParams(dimension_semantics=("arbitrary",)*3, vmem_limit_bytes=60<<20),
        name="first_pass",
        cost_estimate=pl.CostEstimate(flops=5*T*E*N, bytes_accessed=10*T*E, transcendentals=T*E*N))(dt,x,bx,a2)

LOG2E = 1.4426950408889634


def sums(tb):
    return (lax.broadcasted_iota(jnp.int32,(tb,tb*8),1)//8 == lax.broadcasted_iota(jnp.int32,(tb,tb*8),0)).astype(BF16)

def fwd_kernel(U, TB, dt_ref, x_ref, gate_ref, gg_ref, b_ref, c_ref, a_ref, skip_ref, h0_ref,
               out_ref, gz_ref, g_ref, ck_ref, adj_ref, h_s, p_s, r_s, q_s, y_s, dtx_s):
    TC, EG = dt_ref.shape
    NT = EG//LN
    c = pl.program_id(2)
    @pl.when(c == 0)
    def _():
        h_s[...] = h0_ref[...]; p_s[...] = jnp.ones_like(p_s); r_s[...] = jnp.zeros_like(r_s)
    ck_ref[...] = h_s[...]
    dtx_s[...] = dt_ref[...]*x_ref[...].astype(F32)
    gate = gate_ref[...]
    g_ref[...] = gg_ref[...]*(gate*jax.nn.sigmoid(gate))
    sl = [slice(j*LN,(j+1)*LN) for j in range(NT)]
    A = [a_ref[:, s] for s in sl]
    G = TC//U
    def body(i, carry):
        h, p, r = [list(v) for v in carry]
        rows = pl.ds(pl.multiple_of(i*U,U),U)
        dv, xv, gv = dt_ref.at[rows], dtx_s.at[rows], g_ref.at[rows]
        low = [None]*NT
        for k in range(U):
            t = i*U+k
            bt = b_ref[t]; ct = c_ref[t]
            for j in range(NT):
                a = jnp.exp2(dv[k:k+1, sl[j]]*A[j])
                h[j] = a*h[j] + xv[k:k+1, sl[j]]*bt
                p[j] = p[j]*a
                r[j] = r[j] + p[j]*(ct*gv[k:k+1, sl[j]])
                q = h[j]*ct
                q = q[:8]+q[8:]
                if k % 2 == 0: low[j] = q
                else: q_s[pl.ds(pl.multiple_of(i*(U*8)+k*8-8,16),16), sl[j]] = jnp.concatenate([low[j],q],axis=0).astype(BF16)
        return tuple(h), tuple(p), tuple(r)
    init = tuple(tuple(s_[:, s] for s in sl) for s_ in (h_s, p_s, r_s))
    h, p, r = lax.fori_loop(0, G, body, init)
    S = sums(TB)
    for m in range(0, TC, TB):
        y_s[m:m+TB,:] = jnp.dot(S, q_s[m*8:(m+TB)*8,:], preferred_element_type=F32)
    for j in range(NT):
        h_s[:, sl[j]] = h[j]; p_s[:, sl[j]] = p[j]; r_s[:, sl[j]] = r[j]
    gate = gate_ref[...]
    sig = jax.nn.sigmoid(gate)
    y = y_s[...] + skip_ref[...]*x_ref[...].astype(F32)
    out_ref[...] = (y*(gate*sig)).astype(BF16)
    gz_ref[...] = (gg_ref[...]*y*sig*(1.0+gate*(1.0-sig))).astype(BF16)
    @pl.when(c == pl.num_programs(2)-1)
    def _(): adj_ref[...] = r_s[...]

def fwd_pass(dt, x, gate, gg, bx, cx, a2, skip, h0, Q, TC=128, EG=512, U=8, TB=32):
    T,E = dt.shape; N = a2.shape[0]; L=T//Q; NC=L//TC; NE=E//EG
    row = pl.BlockSpec((TC,EG), lambda q,e,c:(q*NC+c, e))
    sp = pl.BlockSpec((TC,N,LN), lambda q,e,c:(q*NC+c,0,0))
    st = pl.BlockSpec((None,N,EG), lambda q,e,c:(q,0,e))
    return pl.pallas_call(partial(fwd_kernel,U,TB), grid=(Q,NE,NC),
        in_specs=[row,row,row,row,sp,sp,pl.BlockSpec((N,EG), lambda q,e,c:(0,e)), pl.BlockSpec((1,EG), lambda q,e,c:(0,e)), st],
        out_specs=[row, row, row, pl.BlockSpec((None,N,EG), lambda q,e,c:(q*NC+c,0,e)), st],
        out_shape=[jax.ShapeDtypeStruct((T,E),BF16)]*2 + [jax.ShapeDtypeStruct((T,E),F32),
            jax.ShapeDtypeStruct((Q*NC,N,E),F32), jax.ShapeDtypeStruct((Q,N,E),F32)],
        scratch_shapes=[pltpu.VMEM((N,EG),F32)]*3 + [pltpu.VMEM((TC*8,EG),BF16)] + [pltpu.VMEM((TC,EG),F32)]*2,
        compiler_params=pltpu.CompilerParams(dimension_semantics=("arbitrary",)*3, vmem_limit_bytes=60<<20),
        name="fwd_pass",
        cost_estimate=pl.CostEstimate(flops=11*T*E*N, bytes_accessed=22*T*E, transcendentals=T*E*N))(dt,x,gate,gg,bx,cx,a2,skip,h0)

def bwd_kernel(U, TB, n_in, *refs):
    dt_ref, x_ref, g_ref, b_ref, c_ref, a_ref, skip_ref, ck_ref, mu0_ref = refs[:9]
    (gl_ref, gx_ref, gb_ref, gc_ref, ga_ref, su_ref,
     mu_s, ga_s, su_s, qa_s, qb_s, zb_s, zc_s, sa_s, sb_s, dtx_s, a_s, h_s) = refs[n_in:]
    TC, EG = dt_ref.shape
    N = a_ref.shape[0]
    NT = EG//LN
    c = pl.program_id(2)
    @pl.when(c == 0)
    def _():
        mu_s[...] = mu0_ref[...]
        for v in (ga_s, su_s): v[...] = jnp.zeros_like(v)
    dtx_s[...] = dt_ref[...]*x_ref[...].astype(F32)
    sl = [slice(j*LN,(j+1)*LN) for j in range(NT)]
    A = [a_ref[:, s] for s in sl]
    h_s[0] = ck_ref[...]
    G = TC//U
    def up(i, carry):
        h = list(carry)
        rows = pl.ds(pl.multiple_of(i*U,U),U)
        dv, xv = dt_ref.at[rows], dtx_s.at[rows]
        for k in range(U):
            t = i*U+k
            bt = b_ref[t]
            for j in range(NT):
                a = jnp.exp2(dv[k:k+1, sl[j]]*A[j])
                h[j] = a*h[j] + xv[k:k+1, sl[j]]*bt
                a_s[t, :, sl[j]] = a
                h_s[t+1, :, sl[j]] = h[j]
        return tuple(h)
    h = lax.fori_loop(0, G, up, tuple(ck_ref[:, s] for s in sl))
    def down(ii, carry):
        i = G-1-ii
        mu, ga, h = [list(v) for v in carry]
        rows = pl.ds(pl.multiple_of(i*U,U),U)
        dv, gv, xv = dt_ref.at[rows], g_ref.at[rows], dtx_s.at[rows]
        la, lb = [None]*NT, [None]*NT
        for k in reversed(range(U)):
            t = i*U+k
            bt = b_ref[t]; ct = c_ref[t]
            zb = zc = None
            for j in range(NT):
                gr = gv[k:k+1, sl[j]]
                lam = mu[j] + ct*gr
                zcj = h[j]*gr
                zbj = lam*xv[k:k+1, sl[j]]
                zc = zcj if j == 0 else zc+zcj
                zb = zbj if j == 0 else zb+zbj
                mu[j] = a_s[t,:,sl[j]]*lam
                h[j] = h_s[t,:,sl[j]]
                w = mu[j]*h[j]
                ga[j] = ga[j] + dv[k:k+1, sl[j]]*w
                qa = A[j]*w
                qb = lam*bt
                qa = qa[:8]+qa[8:]
                qb = qb[:8]+qb[8:]
                if k % 2: la[j], lb[j] = qa, qb
                else:
                    r16 = pl.ds(pl.multiple_of(i*(U*8)+k*8,16),16)
                    qa_s[r16, sl[j]] = jnp.concatenate([qa,la[j]],axis=0).astype(BF16)
                    qb_s[r16, sl[j]] = jnp.concatenate([qb,lb[j]],axis=0).astype(BF16)
            rn = pl.ds(pl.multiple_of(t*N,N),N)
            zb_s[rn,:] = zb.astype(BF16)
            zc_s[rn,:] = zc.astype(BF16)
        return tuple(mu), tuple(ga), tuple(h)
    init = tuple(tuple(s_[:, s] for s in sl) for s_ in (mu_s, ga_s)) + (h,)
    mu, ga, h = lax.fori_loop(0, G, down, init)
    S = sums(TB)
    for m in range(0, TC, TB):
        sa_s[m:m+TB,:] = jnp.dot(S, qa_s[m*8:(m+TB)*8,:], preferred_element_type=F32)
        sb_s[m:m+TB,:] = jnp.dot(S, qb_s[m*8:(m+TB)*8,:], preferred_element_type=F32)
    ones = jnp.ones((8,LN),BF16)
    nt = (((1,),(1,)),((),()))
    gb_ref[...] = lax.dot_general(ones, zb_s[...], nt, preferred_element_type=F32)[:1]
    gc_ref[...] = lax.dot_general(ones, zc_s[...], nt, preferred_element_type=F32)[:1]
    for j in range(NT): ga_s[:, sl[j]] = ga[j]; mu_s[:, sl[j]] = mu[j]
    d = dt_ref[...]; x = x_ref[...].astype(F32); g = g_ref[...]
    sb = sb_s[...]
    gx_ref[...] = d*sb + skip_ref[...]*g
    sig = jnp.where(d < 0.03, d*(1.0-d*(0.5-d*(1.0/6.0-d*(1.0/24.0)))), 1.0-jnp.exp(-d))
    gp = (sa_s[...]*(1.0/LOG2E) + x*sb)*sig
    gl_ref[...] = gp.astype(BF16)
    su_s[...] = su_s[...] + jnp.concatenate([jnp.sum(gp,axis=0,keepdims=True), jnp.sum(g*x,axis=0,keepdims=True)],axis=0)
    @pl.when(c == pl.num_programs(2)-1)
    def _():
        ga_ref[...] = ga_s[...]; su_ref[...] = su_s[...]

def bwd_pass(dt, x, g, bx, cx, a2, skip, ck, mu0, Q, at, prev, waits, TC=128, EG=512, U=8, TB=32):
    T,E = dt.shape; N = a2.shape[0]; L=T//Q; NC=L//TC; NE=E//EG
    row = pl.BlockSpec((TC,EG), lambda q,e,c:(q*NC+NC-1-c, at))
    sp = pl.BlockSpec((TC,N,LN), lambda q,e,c:(q*NC+NC-1-c,0,0))
    st = pl.BlockSpec((None,N,EG), lambda q,e,c:(q,0,at))
    nb = pl.BlockSpec((None,1,TC*N), lambda q,e,c:(at,0,q*NC+NC-1-c))
    args = (dt,x,g,bx,cx,a2,skip,ck,mu0)
    n_in = len(args)+len(prev)+len(waits)
    return pl.pallas_call(partial(bwd_kernel,U,TB,n_in), grid=(Q,1,NC),
        in_specs=[row,row,row,sp,sp,pl.BlockSpec((N,EG), lambda q,e,c:(0,at)), pl.BlockSpec((1,EG), lambda q,e,c:(0,at)),
            pl.BlockSpec((None,N,EG), lambda q,e,c:(q*NC+NC-1-c,0,at)), st]+[pl.BlockSpec(memory_space=pl.ANY)]*(len(prev)+len(waits)),
        out_specs=[row,row,nb,nb,st,pl.BlockSpec((None,2,EG), lambda q,e,c:(q,0,at))],
        out_shape=[jax.ShapeDtypeStruct((T,E),BF16), jax.ShapeDtypeStruct((T,E),F32)]+[jax.ShapeDtypeStruct((NE,1,T*N),F32)]*2
            +[jax.ShapeDtypeStruct((Q,N,E),F32), jax.ShapeDtypeStruct((Q,2,E),F32)],
        input_output_aliases={len(args)+i: i for i in range(len(prev))},
        scratch_shapes=[pltpu.VMEM((N,EG),F32)]*2+[pltpu.VMEM((2,EG),F32)]+[pltpu.VMEM((TC*8,EG),BF16)]*2+[pltpu.VMEM((TC*N,LN),BF16)]*2
            +[pltpu.VMEM((TC,EG),F32)]*3+[pltpu.VMEM((TC,N,EG),F32), pltpu.VMEM((TC+1,N,EG),F32)],
        compiler_params=pltpu.CompilerParams(dimension_semantics=("arbitrary",)*3, vmem_limit_bytes=62<<20),
        name="bwd_pass",
        cost_estimate=pl.CostEstimate(flops=20*T*EG*N, bytes_accessed=22*T*EG, transcendentals=T*EG*N))(*args,*prev,*waits)


def spread_kernel(in_ref, *refs):
    refs[-1][...] = jnp.concatenate([in_ref[r].astype(F32) for r in range(in_ref.shape[0])], axis=1)


def spread(pieces, rows, cols, part, half, prev):
    n_rep, n_shard = (pieces.shape[0], pieces.shape[2] // part)
    return pl.pallas_call(
        spread_kernel,
        grid=(n_shard,),
        in_specs=[pl.BlockSpec((n_rep, rows, part), lambda s: (0, 0, s))] + [pl.BlockSpec(memory_space=pl.ANY)] * len(prev),
        out_specs=pl.BlockSpec((rows, n_rep * part), lambda s: (0, half * n_shard + s)),
        out_shape=jax.ShapeDtypeStruct((rows, cols), F32),
        input_output_aliases={1 + i: i for i in range(len(prev))},
        compiler_params=pltpu.CompilerParams(dimension_semantics=("arbitrary",)),
        name="spread",
        cost_estimate=pl.CostEstimate(flops=0, bytes_accessed=3 * rows * cols, transcendentals=0),
    )(pieces, *prev)


def pick_kernel(count, at_ref, in_ref, out_ref):
    part = out_ref.shape[1] // count
    wide = in_ref.shape[1] // count
    at = at_ref[0] * part
    for k in range(count):
        out_ref[:, k * part:(k + 1) * part] = in_ref[:, pl.ds(pl.multiple_of(k * wide + at, part), part)]


def pick(value, at, n_shard, part, half):
    rows, cols = value.shape
    count = 4 if n_shard % 4 == 0 else n_shard
    steps = n_shard // count
    wide = cols // (2 * steps)
    return pl.pallas_call(
        partial(pick_kernel, count),
        grid_spec=pltpu.PrefetchScalarGridSpec(
            num_scalar_prefetch=1,
            grid=(steps,),
            in_specs=[pl.BlockSpec((rows, wide), lambda s, a: (0, half * steps + s))],
            out_specs=pl.BlockSpec((rows, count * part), lambda s, a: (0, s)),
        ),
        out_shape=jax.ShapeDtypeStruct((rows, n_shard * part), value.dtype),
        compiler_params=pltpu.CompilerParams(dimension_semantics=("arbitrary",)),
        name="pick",
        cost_estimate=pl.CostEstimate(flops=0, bytes_accessed=2 * rows * cols, transcendentals=0),
    )(at, value)


def conv_kernel(x_ref, edge_ref, w_ref, o_ref, x_s):
    L = x_ref.shape[0]
    taps = w_ref.shape[0] - 1
    x_s[0:8, :] = edge_ref[...]
    x_s[8:, :] = x_ref[...].astype(F32)
    pre = jnp.broadcast_to(w_ref[taps:taps + 1, :], x_ref.shape)
    for k in range(taps):
        at = 8 - (taps - 1) + k
        pre = pre + w_ref[k:k + 1, :] * x_s[at:at + L, :]
    o_ref[...] = (pre * jax.nn.sigmoid(pre)).astype(BF16)


def conv_pass(conv_in, edge, wb, Q, EB=256):
    T, E = conv_in.shape
    L = T // Q
    row = pl.BlockSpec((L, EB), lambda q, e: (q, e))
    return pl.pallas_call(
        conv_kernel,
        grid=(Q, E // EB),
        in_specs=[
            row,
            pl.BlockSpec((None, 8, EB), lambda q, e: (q, 0, e)),
            pl.BlockSpec((wb.shape[0], EB), lambda q, e: (0, e)),
        ],
        out_specs=row,
        out_shape=jax.ShapeDtypeStruct((T, E), BF16),
        scratch_shapes=[pltpu.VMEM((L + 8, EB), F32)],
        compiler_params=pltpu.CompilerParams(dimension_semantics=("arbitrary",) * 2),
        name="conv_pass",
        cost_estimate=pl.CostEstimate(flops=12 * T * E, bytes_accessed=4 * T * E, transcendentals=T * E),
    )(conv_in, edge, wb)


def conv_back_kernel(n_in, *refs):
    gp_ref, xp_ref, gx_ref, x_ref, edge_ref, w_ref = refs[:6]
    gi_ref, head_ref, tail_ref, gw_ref, x_s, g_s = refs[n_in:]
    L = x_ref.shape[0]
    taps = w_ref.shape[0] - 1
    x_s[0:8, :] = edge_ref[...]
    x_s[8:, :] = x_ref[...].astype(F32)
    at = [8 - (taps - 1) + k for k in range(taps)]
    pre = jnp.broadcast_to(w_ref[taps:taps + 1, :], x_ref.shape)
    for k in range(taps):
        pre = pre + w_ref[k:k + 1, :] * x_s[at[k]:at[k] + L, :]
    s = jax.nn.sigmoid(pre)
    g_out = contract_cols(gp_ref[...], xp_ref[...]) + gx_ref[...]
    g_pre = g_out * s * (1.0 + pre * (1.0 - s))
    g_s[0:L, :] = g_pre
    g_s[L:, :] = jnp.zeros((8, x_ref.shape[1]), F32)
    gw = [jnp.sum(g_pre * x_s[at[k]:at[k] + L, :], axis=0, keepdims=True) for k in range(taps)]
    gw.append(jnp.sum(g_pre, axis=0, keepdims=True))
    gw_ref[...] = jnp.concatenate(gw, axis=0)
    head_ref[...] = g_s[0:8, :]
    g_in = jnp.zeros(x_ref.shape, F32)
    for k in range(taps):
        g_in = g_in + w_ref[k:k + 1, :] * g_s[taps - 1 - k:taps - 1 - k + L, :]
    gi_ref[...] = g_in.astype(BF16)
    tail_ref[...] = g_in[L - 8:, :]


def conv_back(g_projected, x_proj, gx, conv_in, edge, wb, waits, Q, EB=256):
    T, E = conv_in.shape
    L = T // Q
    row = pl.BlockSpec((L, EB), lambda q, e: (q, e))
    edges = pl.BlockSpec((None, 8, EB), lambda q, e: (q, 0, e))
    rows = wb.shape[0]
    return pl.pallas_call(
        partial(conv_back_kernel, 6 + len(waits)),
        grid=(Q, E // EB),
        in_specs=[
            pl.BlockSpec((L, g_projected.shape[1]), lambda q, e: (q, 0)),
            pl.BlockSpec((EB, x_proj.shape[1]), lambda q, e: (e, 0)),
            row,
            row,
            edges,
            pl.BlockSpec((rows, EB), lambda q, e: (0, e)),
        ] + [pl.BlockSpec(memory_space=pl.ANY)] * len(waits),
        out_specs=[row, edges, edges, pl.BlockSpec((None, rows, EB), lambda q, e: (q, 0, e))],
        out_shape=[
            jax.ShapeDtypeStruct((T, E), BF16),
            jax.ShapeDtypeStruct((Q, 8, E), F32),
            jax.ShapeDtypeStruct((Q, 8, E), F32),
            jax.ShapeDtypeStruct((Q, rows, E), F32),
        ],
        scratch_shapes=[pltpu.VMEM((L + 8, EB), F32)] * 2,
        compiler_params=pltpu.CompilerParams(dimension_semantics=("arbitrary",) * 2),
        name="conv_back",
        cost_estimate=pl.CostEstimate(flops=400 * T * E, bytes_accessed=10 * T * E, transcendentals=T * E),
    )(g_projected, x_proj, gx, conv_in, edge, wb, *waits)


def contract_rows(left, right):
    return lax.dot_general(left, right, (((0,), (0,)), ((), ())), preferred_element_type=F32)


def contract_cols(left, right):
    return lax.dot_general(left, right, (((1,), (1,)), ((), ())), preferred_element_type=F32)


def swap(value, flip):
    return lax.ppermute(value, "rep", [(i, i ^ flip) for i in range(lax.axis_size("rep"))])


def shifted(value, steps):
    count = lax.axis_size("shard")
    first, last = (max(0, -steps), min(count, count - steps))
    return lax.ppermute(value, "shard", [(i, i + steps) for i in range(first, last)])


def rep_gather(value):
    far = swap(value, 2)
    return [value, swap(value, 1), far, swap(far, 1)]


def rep_near(parts):
    low = [part.astype(BF16) for part in parts]
    near = [swap(low[k], 1).astype(F32) for k in (1, 3)]
    return parts[0] + near[0], (parts[2] + near[1]).astype(BF16)


def rep_far(mine, other):
    return mine + swap(other, 2).astype(F32)


def rep_sum(parts):
    near = [swap(parts[k], 1) for k in (1, 3)]
    pair = [parts[0] + near[0], parts[2] + near[1]]
    far = [swap(value, 2) for value in pair]
    full = [pair[0] + far[1], pair[1] + far[0]]
    over = [swap(value, 1) for value in full]
    return [full[0], over[0], full[1], over[1]]


def add_all(value, axis):
    step = 1
    while step < lax.axis_size(axis):
        value = value + lax.ppermute(value, axis, [(i, i ^ step) for i in range(lax.axis_size(axis))])
        step *= 2
    return value


def carry_in(total, state, rates, place, span, reverse):
    if span == 1:
        return jnp.zeros_like(state)
    n_rep, states, chans = state.shape
    count = lax.axis_size("shard")
    group = 2 if span % 2 == 0 else 1

    def moved(total, state, target):
        sent = jnp.concatenate([state.reshape(n_rep * states, chans), total], axis=0).astype(BF16)
        pairs = [(i, target(i)) for i in range(count)]
        pairs = [(i, j) for i, j in pairs if 0 <= j < count and i // span == j // span]
        got = lax.ppermute(sent, "shard", pairs).astype(F32)
        return got[n_rep * states:], got[:n_rep * states].reshape(state.shape)

    def decay(amount):
        return jnp.exp(rates[None] * amount[:, None, :])

    second = place % group == 1
    if group == 2:
        other_total, other_state = moved(total, state, lambda i: i ^ 1)
        first_state, last_state = jnp.where(second, other_state, state), jnp.where(second, state, other_state)
        last_total = jnp.where(second, total, other_total)
        block_state = decay(last_total) * first_state + last_state
        block_total = total + other_total
    else:
        block_total, block_state = (total, state)
    step = -group if reverse else group
    got = [moved(block_total, block_state, lambda i, k=k: i + k * step) for k in range(1, span // group)]
    start, gone = (jnp.zeros_like(state), jnp.zeros_like(total))
    for far_total, far_state in got:
        start = start + decay(gone) * far_state
        gone = gone + far_total
    if group == 2:
        start = jnp.where(second, decay(other_total) * start + other_state, start)
    return start


def on_device(
    block_input,
    cotangent,
    seq_lengths,
    slot_order,
    norm_gain,
    in_proj,
    conv_weight,
    conv_bias,
    x_proj,
    dt_proj,
    dt_bias,
    a_log,
    d_skip,
    out_proj,
):
    n_shard, n_rep = (lax.axis_size("shard"), lax.axis_size("rep"))
    shard_at, rep_at = (lax.axis_index("shard"), lax.axis_index("rep"))
    rows, width = block_input.shape
    tokens = n_rep * rows
    taps, wide = conv_weight.shape
    part = wide // n_rep
    chans = part * n_shard
    rank = dt_proj.shape[0]
    states = a_log.shape[0]
    span = max(1, min(n_shard, SPAN_TOKENS // rows))
    in_slot = shard_at % span
    keep_prev = (in_slot != 0).astype(F32)
    keep_next = (in_slot != span - 1).astype(F32)
    places = in_slot * rows + jnp.arange(rows, dtype=jnp.int32)

    def valid_of(flip):
        slot_at = ((rep_at ^ flip) * n_shard + shard_at) // span
        slot_len = jnp.sum(jnp.where(slot_order == slot_at, seq_lengths, 0))
        return (places < slot_len).astype(F32)[:, None]

    valid = [valid_of(k) for k in range(n_rep)]

    def mine(value, axis):
        return lax.dynamic_slice_in_dim(value, rep_at * part, part, axis)

    x_all = rep_gather(block_input)
    small = jnp.concatenate(
        [
            mine(x_proj, 0),
            mine(dt_proj, 1).T,
            mine(a_log, 1).T,
            mine(conv_weight, 1).T,
            mine(conv_bias, 0)[:, None],
            mine(dt_bias, 0)[:, None],
            mine(d_skip, 0)[:, None],
            norm_gain.reshape(part, -1),
        ],
        axis=1,
    )
    if part % LN:
        in_mine = lax.dynamic_index_in_dim(
            in_proj.reshape(in_proj.shape[0], 2, n_shard, n_rep, part), rep_at, 3, keepdims=False
        ).reshape(in_proj.shape[0], 2, chans)
        in_conv, in_gate = (in_mine[:, 0], in_mine[:, 1])
    else:
        in_conv, in_gate = [pick(in_proj, rep_at.reshape(1), n_shard, part, k) for k in range(2)]
    small_all = lax.all_gather(small, "shard", axis=0, tiled=True)
    conv_w = lax.all_gather(in_conv, "shard", axis=0, tiled=True)
    gate_w = lax.all_gather(in_gate, "shard", axis=0, tiled=True)
    out_all = lax.all_gather(mine(out_proj, 0), "shard", axis=0, tiled=True)
    cot_all = rep_gather(cotangent)

    cut = [x_proj.shape[1], rank, states, taps, 1, 1, 1]
    ends = [sum(cut[:i + 1]) for i in range(len(cut))]
    xproj_all = small_all[:, :ends[0]]
    dtproj_all = small_all[:, ends[0]:ends[1]].T
    log_rates = small_all[:, ends[1]:ends[2]].T.astype(F32)
    wb = small_all[:, ends[2]:ends[4]].T.astype(F32)
    dtbias_all = small_all[:, ends[4]].astype(F32)
    skip_all = small_all[:, ends[5]].astype(F32)
    gain_f = small_all[:, ends[6]:].reshape(width).astype(F32)

    def norm(value):
        value = value.astype(F32)
        scale = lax.rsqrt(jnp.mean(value * value, axis=1, keepdims=True) + EPSILON)
        return (value * scale * gain_f[None, :]).astype(BF16)

    normed = jnp.concatenate([norm(value) for value in x_all], axis=0)
    conv_in = jnp.dot(normed, conv_w, preferred_element_type=F32).astype(BF16)
    last = conv_in.reshape(n_rep, rows, chans)[:, rows - (taps - 1):]
    edge = shifted(last, 1).astype(F32) * keep_prev
    edge = jnp.concatenate([jnp.zeros((n_rep, 8 - (taps - 1), chans), F32), edge], axis=1)
    conv_out = conv_pass(conv_in, edge, wb, n_rep)
    proj = lax.dot_general(xproj_all, conv_out, (((0,), (1,)), ((), ())), preferred_element_type=F32)
    proj = jnp.concatenate(
        rep_sum([proj[:, k * rows:(k + 1) * rows] for k in range(n_rep)]), axis=1
    )
    step_low = proj[:rank].astype(BF16)
    b_all = jnp.broadcast_to(proj[rank:rank + states].T[:, :, None], (tokens, states, LN))
    c_all = jnp.broadcast_to(proj[rank + states:].T[:, :, None], (tokens, states, LN))
    step = jax.nn.softplus(contract_rows(step_low, dtproj_all) + dtbias_all[None, :])
    rates = -jnp.exp(log_rates)
    rates2 = rates * LOG2E
    gate_in = jnp.dot(normed, gate_w, preferred_element_type=F32)
    back = jnp.concatenate(
        [(cot_all[k].astype(F32) * valid[k]).astype(BF16) for k in range(n_rep)], axis=0
    )
    g_gated = contract_cols(back, out_all)
    skip = skip_all[None, :]
    local_end = first_pass(step, conv_out, b_all, rates2, n_rep)
    total = jnp.sum(step.reshape(n_rep, rows, chans), axis=1)
    start_state = carry_in(total, local_end, rates, in_slot, span, False)
    gated, g_gate, g_scanned, kept, local_adj = fwd_pass(
        step, conv_out, gate_in, g_gated, b_all, c_all, rates2, skip, start_state, n_rep
    )
    end_grad = carry_in(total, local_adj, rates, span - 1 - in_slot, span, True)
    branch = jnp.dot(gated, out_all, preferred_element_type=F32)
    near, other = rep_near([branch[k * rows:(k + 1) * rows] for k in range(n_rep)])
    pieces = width // chans
    held = in_proj.shape[0]
    local = [contract_rows(normed, g_gate).astype(BF16).reshape(n_shard, held, chans)]
    for k in range(pieces):
        piece = contract_rows(gated, back[:, k * chans:(k + 1) * chans])
        local.append(piece.astype(BF16).reshape(n_shard, part, chans))
    local = jnp.concatenate(local, axis=1).reshape(-1, chans)
    local, other, end_grad = lax.optimization_barrier((local, other, end_grad))
    branch = rep_far(near, other)
    input_f = block_input.astype(F32)
    activations = (input_f + valid[0] * branch).astype(BF16)

    def scatter(value):
        return lax.psum_scatter(value, "shard", scatter_dimension=0, tiled=True)

    def everyone(value):
        return lax.all_gather(value, "rep", axis=0)

    early = scatter(local)
    back_args = (step, conv_out, g_scanned, b_all, c_all, rates2, skip, kept, end_grad, n_rep)
    prev, groups = ([], chans // 512)
    for k in range(groups):
        prev = bwd_pass(*back_args, k, prev, [local, other] if k == 0 else [activations])
    g_lin, g_scan_in, g_b, g_c, g_a, g_sums = prev
    grad_dt_bias, grad_skip = jnp.sum(g_sums, axis=0)
    grad_dt_proj = contract_rows(g_lin, step_low.T)
    g_low = contract_cols(dtproj_all, g_lin)
    g_b, g_c = [jnp.sum(v, axis=(0, 1)).reshape(tokens, states).T for v in (g_b, g_c)]
    g_proj = jnp.concatenate([g_low, g_b, g_c], axis=0)
    g_proj = jnp.concatenate(
        rep_sum([g_proj[:, k * rows:(k + 1) * rows] for k in range(n_rep)]), axis=1
    )
    g_proj = g_proj.T.astype(BF16)
    early, g_proj = lax.optimization_barrier((early, g_proj))
    all_early = everyone(early)
    grad_x_proj = contract_rows(conv_out, g_proj)
    g_in, head, tail, grad_wb = conv_back(g_proj, xproj_all, g_scan_in, conv_in, edge, wb, [], n_rep)
    after = shifted(head, -1) * keep_next
    joined = jnp.concatenate([jnp.zeros_like(after), after], axis=1)
    fix = tail
    for k in range(taps - 1):
        at = taps - 1 - k
        fix = fix + wb[k][None, None, :] * joined[:, at:at + 8]
    g_in = g_in.reshape(n_rep, rows, chans).at[:, rows - 8:].set(fix.astype(BF16))
    g_in = g_in.reshape(tokens, chans)
    grad_a_log = rates * jnp.sum(g_a, axis=0)
    small = [grad_x_proj, grad_dt_proj, grad_a_log.T, jnp.sum(grad_wb, axis=0).T, grad_dt_bias[:, None], grad_skip[:, None]]
    small.append(jnp.zeros((chans, -ends[6] % LN), F32))
    small = jnp.concatenate(small, axis=1).astype(BF16).reshape(n_shard, part, -1, LN)
    lanes = small.shape[2]
    small = small.transpose(0, 2, 1, 3).reshape(n_shard, -1, chans)
    late = contract_rows(normed, g_in).astype(BF16).reshape(n_shard, held, chans)
    late = jnp.concatenate([late, small], axis=1).reshape(-1, chans)
    late, all_early = lax.optimization_barrier((late, all_early))
    late = scatter(late)
    half = rows // 2
    g_normed = []
    for at in (0, half):
        conv_rows = g_in.reshape(n_rep, rows, chans)[:, at:at + half].reshape(n_rep * half, chans)
        gate_rows = g_gate.reshape(n_rep, rows, chans)[:, at:at + half].reshape(n_rep * half, chans)
        both = contract_cols(conv_rows, conv_w) + contract_cols(gate_rows, gate_w)
        g_normed.append(rep_far(*rep_near([both[k * half:(k + 1) * half] for k in range(n_rep)])))
    g_normed = jnp.concatenate(g_normed, axis=0)
    scale = lax.rsqrt(jnp.mean(input_f * input_f, axis=1, keepdims=True) + EPSILON)
    grad_gain = jnp.sum(g_normed * input_f * scale, axis=0)
    g_hat = g_normed * gain_f[None, :]
    input_grad = (
        cotangent.astype(F32)
        + scale * g_hat
        - input_f * (scale * scale * scale) * jnp.mean(g_hat * input_f, axis=1, keepdims=True)
    )
    grad_gain = add_all(add_all(grad_gain.reshape(-1, LN), "rep"), "shard").reshape(width)
    all_gain = lax.dynamic_slice_in_dim(grad_gain, shard_at * norm_gain.shape[0], norm_gain.shape[0])
    all_late = everyone(late)
    all_out = all_early[:, held:].reshape(n_rep, pieces, part, chans).transpose(0, 2, 1, 3)
    all_out = all_out.reshape(wide, width).astype(F32)
    if part % LN:
        all_in = jnp.stack([all_late[:, :held], all_early[:, :held]], axis=0)
        all_in = all_in.reshape(2, n_rep, -1, n_shard, part).transpose(2, 0, 3, 1, 4)
        all_in = all_in.reshape(in_proj.shape).astype(F32)
    else:
        all_in = spread(all_early, *in_proj.shape, part, 1, [])
        all_in = spread(all_late, *in_proj.shape, part, 0, [all_in])
    all_small = all_late[:, held:].reshape(n_rep, lanes, part, LN).transpose(0, 2, 1, 3)
    all_small = all_small.reshape(wide, lanes * LN).astype(F32)
    return (
        activations,
        input_grad,
        all_gain,
        all_in,
        all_small[:, ends[2]:ends[3]].T,
        all_small[:, ends[3]],
        all_small[:, :ends[0]],
        all_small[:, ends[0]:ends[1]].T,
        all_small[:, ends[4]],
        all_small[:, ends[1]:ends[2]].T,
        all_small[:, ends[5]],
        all_out,
    )


def solution(mesh):
    tokens = P(("rep", "shard"), None)
    rows, cols, line, full = (P("shard", None), P(None, "shard"), P("shard"), P())
    return jax.shard_map(
        on_device,
        mesh=mesh,
        in_specs=(tokens, tokens, full, full, line, rows, cols, line, rows, cols, line, cols, line, rows),
        out_specs=(tokens, tokens, line, rows, cols, line, rows, cols, line, cols, line, rows),
        check_vma=False,
    )
```

```python
from functools import partial

import jax
import jax.numpy as jnp
from jax import lax
from jax.experimental import pallas as pl
from jax.experimental.pallas import tpu as pltpu
from jax.sharding import PartitionSpec as P

EPSILON = 1e-05
SPAN_TOKENS = 4096
GROUP = 512
F32=jnp.float32; BF16=jnp.bfloat16
LN=128
def first_kernel(U, dt_ref, x_ref, b_ref, a_ref, hend_ref, h_s, dtx_s):
    TC, EG = dt_ref.shape
    NT = EG//LN
    c = pl.program_id(2)
    @pl.when(c == 0)
    def _():
        h_s[...] = jnp.zeros_like(h_s)
    dtx_s[...] = dt_ref[...]*x_ref[...].astype(F32)
    sl = [slice(j*LN,(j+1)*LN) for j in range(NT)]
    A = [a_ref[:, s] for s in sl]
    def body(i, carry):
        h = list(carry)
        rows = pl.ds(pl.multiple_of(i*U,U),U)
        dv, xv = dt_ref.at[rows], dtx_s.at[rows]
        for k in range(U):
            bt = b_ref[i*U+k]
            for j in range(NT):
                a = jnp.exp2(dv[k:k+1, sl[j]]*A[j])
                h[j] = a*h[j] + xv[k:k+1, sl[j]]*bt
        return tuple(h)
    h = lax.fori_loop(0, TC//U, body, tuple(h_s[:, s] for s in sl))
    for j in range(NT): h_s[:, sl[j]] = h[j]
    @pl.when(c == pl.num_programs(2)-1)
    def _():
        hend_ref[...] = h_s[...]

def first_pass(dt, x, bx, a2, Q, TC=256, EG=GROUP, U=8):
    T,E = dt.shape; N = a2.shape[0]; L=T//Q; NC=L//TC; NE=E//EG
    row = pl.BlockSpec((TC,EG), lambda q,e,c:(q*NC+c, e))
    sp = pl.BlockSpec((TC,N,LN), lambda q,e,c:(q*NC+c,0,0))
    st = pl.BlockSpec((None,N,EG), lambda q,e,c:(q,0,e))
    return pl.pallas_call(partial(first_kernel,U), grid=(Q,NE,NC),
        in_specs=[row,row,sp,pl.BlockSpec((N,EG), lambda q,e,c:(0,e))],
        out_specs=st,
        out_shape=jax.ShapeDtypeStruct((Q,N,E),F32),
        scratch_shapes=[pltpu.VMEM((N,EG),F32),pltpu.VMEM((TC,EG),F32)],
        compiler_params=pltpu.CompilerParams(dimension_semantics=("arbitrary",)*3, vmem_limit_bytes=60<<20),
        name="first_pass",
        cost_estimate=pl.CostEstimate(flops=5*T*E*N, bytes_accessed=10*T*E, transcendentals=T*E*N))(dt,x,bx,a2)

LOG2E = 1.4426950408889634


def sums(tb):
    return (lax.broadcasted_iota(jnp.int32,(tb,tb*8),1)//8 == lax.broadcasted_iota(jnp.int32,(tb,tb*8),0)).astype(BF16)

def fwd_kernel(U, TB, dt_ref, x_ref, gate_ref, gg_ref, b_ref, c_ref, a_ref, skip_ref, h0_ref,
               out_ref, gz_ref, g_ref, ck_ref, adj_ref, h_s, p_s, r_s, q_s, y_s, dtx_s):
    TC, EG = dt_ref.shape
    NT = EG//LN
    c = pl.program_id(2)
    @pl.when(c == 0)
    def _():
        h_s[...] = h0_ref[...]; p_s[...] = jnp.ones_like(p_s); r_s[...] = jnp.zeros_like(r_s)
    ck_ref[...] = h_s[...]
    dtx_s[...] = dt_ref[...]*x_ref[...].astype(F32)
    gate = gate_ref[...]
    g_ref[...] = gg_ref[...]*(gate*jax.nn.sigmoid(gate))
    sl = [slice(j*LN,(j+1)*LN) for j in range(NT)]
    A = [a_ref[:, s] for s in sl]
    G = TC//U
    def body(i, carry):
        h, p, r = [list(v) for v in carry]
        rows = pl.ds(pl.multiple_of(i*U,U),U)
        dv, xv, gv = dt_ref.at[rows], dtx_s.at[rows], g_ref.at[rows]
        low = [None]*NT
        for k in range(U):
            t = i*U+k
            bt = b_ref[t]; ct = c_ref[t]
            for j in range(NT):
                a = jnp.exp2(dv[k:k+1, sl[j]]*A[j])
                h[j] = a*h[j] + xv[k:k+1, sl[j]]*bt
                p[j] = p[j]*a
                r[j] = r[j] + p[j]*(ct*gv[k:k+1, sl[j]])
                q = h[j]*ct
                q = q[:8]+q[8:]
                if k % 2 == 0: low[j] = q
                else: q_s[pl.ds(pl.multiple_of(i*(U*8)+k*8-8,16),16), sl[j]] = jnp.concatenate([low[j],q],axis=0).astype(BF16)
        return tuple(h), tuple(p), tuple(r)
    init = tuple(tuple(s_[:, s] for s in sl) for s_ in (h_s, p_s, r_s))
    h, p, r = lax.fori_loop(0, G, body, init)
    S = sums(TB)
    for m in range(0, TC, TB):
        y_s[m:m+TB,:] = jnp.dot(S, q_s[m*8:(m+TB)*8,:], preferred_element_type=F32)
    for j in range(NT):
        h_s[:, sl[j]] = h[j]; p_s[:, sl[j]] = p[j]; r_s[:, sl[j]] = r[j]
    gate = gate_ref[...]
    sig = jax.nn.sigmoid(gate)
    y = y_s[...] + skip_ref[...]*x_ref[...].astype(F32)
    out_ref[...] = (y*(gate*sig)).astype(BF16)
    gz_ref[...] = (gg_ref[...]*y*sig*(1.0+gate*(1.0-sig))).astype(BF16)
    @pl.when(c == pl.num_programs(2)-1)
    def _(): adj_ref[...] = r_s[...]

def fwd_pass(dt, x, gate, gg, bx, cx, a2, skip, h0, Q, TC=256, EG=GROUP, U=8, TB=32):
    T,E = dt.shape; N = a2.shape[0]; L=T//Q; NC=L//TC; NE=E//EG
    row = pl.BlockSpec((TC,EG), lambda q,e,c:(q*NC+c, e))
    sp = pl.BlockSpec((TC,N,LN), lambda q,e,c:(q*NC+c,0,0))
    st = pl.BlockSpec((None,N,EG), lambda q,e,c:(q,0,e))
    return pl.pallas_call(partial(fwd_kernel,U,TB), grid=(Q,NE,NC),
        in_specs=[row,row,row,row,sp,sp,pl.BlockSpec((N,EG), lambda q,e,c:(0,e)), pl.BlockSpec((1,EG), lambda q,e,c:(0,e)), st],
        out_specs=[row, row, row, pl.BlockSpec((None,N,EG), lambda q,e,c:(q*NC+c,0,e)), st],
        out_shape=[jax.ShapeDtypeStruct((T,E),BF16)]*2 + [jax.ShapeDtypeStruct((T,E),F32),
            jax.ShapeDtypeStruct((Q*NC,N,E),F32), jax.ShapeDtypeStruct((Q,N,E),F32)],
        scratch_shapes=[pltpu.VMEM((N,EG),F32)]*3 + [pltpu.VMEM((TC*8,EG),BF16)] + [pltpu.VMEM((TC,EG),F32)]*2,
        compiler_params=pltpu.CompilerParams(dimension_semantics=("arbitrary",)*3, vmem_limit_bytes=60<<20),
        name="fwd_pass",
        cost_estimate=pl.CostEstimate(flops=11*T*E*N, bytes_accessed=22*T*E, transcendentals=T*E*N))(dt,x,gate,gg,bx,cx,a2,skip,h0)

def bwd_kernel(U, TB, n_in, *refs):
    dt_ref, x_ref, g_ref, b_ref, c_ref, a_ref, skip_ref, ck_ref, mu0_ref = refs[:9]
    (gl_ref, gx_ref, gb_ref, gc_ref, ga_ref, su_ref,
     mu_s, ga_s, su_s, qa_s, qb_s, zb_s, zc_s, sa_s, sb_s, dtx_s, a_s, h_s) = refs[n_in:]
    TC, EG = dt_ref.shape
    N = a_ref.shape[0]
    NT = EG//LN
    c = pl.program_id(2)
    @pl.when(c == 0)
    def _():
        mu_s[...] = mu0_ref[...]
        for v in (ga_s, su_s): v[...] = jnp.zeros_like(v)
    dtx_s[...] = dt_ref[...]*x_ref[...].astype(F32)
    sl = [slice(j*LN,(j+1)*LN) for j in range(NT)]
    A = [a_ref[:, s] for s in sl]
    h_s[0] = ck_ref[...]
    G = TC//U
    def up(i, carry):
        h = list(carry)
        rows = pl.ds(pl.multiple_of(i*U,U),U)
        dv, xv = dt_ref.at[rows], dtx_s.at[rows]
        for k in range(U):
            t = i*U+k
            bt = b_ref[t]
            for j in range(NT):
                a = jnp.exp2(dv[k:k+1, sl[j]]*A[j])
                h[j] = a*h[j] + xv[k:k+1, sl[j]]*bt
                a_s[t, :, sl[j]] = a
                h_s[t+1, :, sl[j]] = h[j]
        return tuple(h)
    h = lax.fori_loop(0, G, up, tuple(ck_ref[:, s] for s in sl))
    def down(ii, carry):
        i = G-1-ii
        mu, ga, h = [list(v) for v in carry]
        rows = pl.ds(pl.multiple_of(i*U,U),U)
        dv, gv, xv = dt_ref.at[rows], g_ref.at[rows], dtx_s.at[rows]
        la, lb = [None]*NT, [None]*NT
        for k in reversed(range(U)):
            t = i*U+k
            bt = b_ref[t]; ct = c_ref[t]
            zb = zc = None
            for j in range(NT):
                gr = gv[k:k+1, sl[j]]
                lam = mu[j] + ct*gr
                zcj = h[j]*gr
                zbj = lam*xv[k:k+1, sl[j]]
                zc = zcj if j == 0 else zc+zcj
                zb = zbj if j == 0 else zb+zbj
                mu[j] = a_s[t,:,sl[j]]*lam
                h[j] = h_s[t,:,sl[j]]
                w = mu[j]*h[j]
                ga[j] = ga[j] + dv[k:k+1, sl[j]]*w
                qa = A[j]*w
                qb = lam*bt
                qa = qa[:8]+qa[8:]
                qb = qb[:8]+qb[8:]
                if k % 2: la[j], lb[j] = qa, qb
                else:
                    r16 = pl.ds(pl.multiple_of(i*(U*8)+k*8,16),16)
                    qa_s[r16, sl[j]] = jnp.concatenate([qa,la[j]],axis=0).astype(BF16)
                    qb_s[r16, sl[j]] = jnp.concatenate([qb,lb[j]],axis=0).astype(BF16)
            rn = pl.ds(pl.multiple_of(t*N,N),N)
            zb_s[rn,:] = zb.astype(BF16)
            zc_s[rn,:] = zc.astype(BF16)
        return tuple(mu), tuple(ga), tuple(h)
    init = tuple(tuple(s_[:, s] for s in sl) for s_ in (mu_s, ga_s)) + (h,)
    mu, ga, h = lax.fori_loop(0, G, down, init)
    S = sums(TB)
    for m in range(0, TC, TB):
        sa_s[m:m+TB,:] = jnp.dot(S, qa_s[m*8:(m+TB)*8,:], preferred_element_type=F32)
        sb_s[m:m+TB,:] = jnp.dot(S, qb_s[m*8:(m+TB)*8,:], preferred_element_type=F32)
    ones = jnp.ones((8,LN),BF16)
    nt = (((1,),(1,)),((),()))
    gb_ref[...] = lax.dot_general(ones, zb_s[...], nt, preferred_element_type=F32)[:1]
    gc_ref[...] = lax.dot_general(ones, zc_s[...], nt, preferred_element_type=F32)[:1]
    for j in range(NT): ga_s[:, sl[j]] = ga[j]; mu_s[:, sl[j]] = mu[j]
    d = dt_ref[...]; x = x_ref[...].astype(F32); g = g_ref[...]
    sb = sb_s[...]
    gx_ref[...] = d*sb + skip_ref[...]*g
    sig = jnp.where(d < 0.03, d*(1.0-d*(0.5-d*(1.0/6.0-d*(1.0/24.0)))), 1.0-jnp.exp(-d))
    gp = (sa_s[...]*(1.0/LOG2E) + x*sb)*sig
    gl_ref[...] = gp.astype(BF16)
    su_s[...] = su_s[...] + jnp.concatenate([jnp.sum(gp,axis=0,keepdims=True), jnp.sum(g*x,axis=0,keepdims=True)],axis=0)
    @pl.when(c == pl.num_programs(2)-1)
    def _():
        ga_ref[...] = ga_s[...]; su_ref[...] = su_s[...]

def bwd_pass(dt, x, g, bx, cx, a2, skip, ck, mu0, Q, at, prev, waits, TC=256, EG=GROUP, U=8, TB=32):
    T,E = dt.shape; N = a2.shape[0]; L=T//Q; NC=L//TC; NE=E//EG
    row = pl.BlockSpec((TC,EG), lambda q,e,c:(q*NC+NC-1-c, at))
    sp = pl.BlockSpec((TC,N,LN), lambda q,e,c:(q*NC+NC-1-c,0,0))
    st = pl.BlockSpec((None,N,EG), lambda q,e,c:(q,0,at))
    nb = pl.BlockSpec((None,1,TC*N), lambda q,e,c:(at,0,q*NC+NC-1-c))
    args = (dt,x,g,bx,cx,a2,skip,ck,mu0)
    n_in = len(args)+len(prev)+len(waits)
    return pl.pallas_call(partial(bwd_kernel,U,TB,n_in), grid=(Q,1,NC),
        in_specs=[row,row,row,sp,sp,pl.BlockSpec((N,EG), lambda q,e,c:(0,at)), pl.BlockSpec((1,EG), lambda q,e,c:(0,at)),
            pl.BlockSpec((None,N,EG), lambda q,e,c:(q*NC+NC-1-c,0,at)), st]+[pl.BlockSpec(memory_space=pl.ANY)]*(len(prev)+len(waits)),
        out_specs=[row,row,nb,nb,st,pl.BlockSpec((None,2,EG), lambda q,e,c:(q,0,at))],
        out_shape=[jax.ShapeDtypeStruct((T,E),BF16), jax.ShapeDtypeStruct((T,E),F32)]+[jax.ShapeDtypeStruct((NE,1,T*N),F32)]*2
            +[jax.ShapeDtypeStruct((Q,N,E),F32), jax.ShapeDtypeStruct((Q,2,E),F32)],
        input_output_aliases={len(args)+i: i for i in range(len(prev))},
        scratch_shapes=[pltpu.VMEM((N,EG),F32)]*2+[pltpu.VMEM((2,EG),F32)]+[pltpu.VMEM((TC*8,EG),BF16)]*2+[pltpu.VMEM((TC*N,LN),BF16)]*2
            +[pltpu.VMEM((TC,EG),F32)]*3+[pltpu.VMEM((TC,N,EG),F32), pltpu.VMEM((TC+1,N,EG),F32)],
        compiler_params=pltpu.CompilerParams(dimension_semantics=("arbitrary",)*3, vmem_limit_bytes=62<<20),
        name="bwd_pass",
        cost_estimate=pl.CostEstimate(flops=20*T*EG*N, bytes_accessed=22*T*EG, transcendentals=T*EG*N))(*args,*prev,*waits)


def spread_kernel(count, at_ref, *refs):
    out_ref = refs[-1]
    part = out_ref.shape[1] // count
    for k in range(count):
        at = pl.multiple_of((at_ref[0] ^ k) * part, part)
        out_ref[:, pl.ds(at, part)] = refs[k][...].astype(F32)


def spread(pieces, at, rows, cols, part, start, prev):
    count = len(pieces)
    piece = pl.BlockSpec((rows, part), lambda s, a: (0, s))
    return pl.pallas_call(
        partial(spread_kernel, count),
        grid_spec=pltpu.PrefetchScalarGridSpec(
            num_scalar_prefetch=1,
            grid=(pieces[0].shape[1] // part,),
            in_specs=[piece] * count + [pl.BlockSpec(memory_space=pl.ANY)] * len(prev),
            out_specs=pl.BlockSpec((rows, count * part), lambda s, a: (0, start + s)),
        ),
        out_shape=jax.ShapeDtypeStruct((rows, cols), F32),
        input_output_aliases={1 + count + i: i for i in range(len(prev))},
        compiler_params=pltpu.CompilerParams(dimension_semantics=("arbitrary",)),
        name="spread",
        cost_estimate=pl.CostEstimate(flops=0, bytes_accessed=3 * rows * cols, transcendentals=0),
    )(at, *pieces, *prev)


def pick_kernel(count, at_ref, in_ref, out_ref):
    part = out_ref.shape[1] // count
    wide = in_ref.shape[1] // count
    at = at_ref[0] * part
    for k in range(count):
        out_ref[:, k * part:(k + 1) * part] = in_ref[:, pl.ds(pl.multiple_of(k * wide + at, part), part)]


def pick(value, at, n_rep, n_shard, part, half):
    rows, cols = value.shape
    count = 4 if n_shard % 4 == 0 else n_shard
    steps = n_shard // count
    wide = n_rep * part * count
    return pl.pallas_call(
        partial(pick_kernel, count),
        grid_spec=pltpu.PrefetchScalarGridSpec(
            num_scalar_prefetch=1,
            grid=(steps,),
            in_specs=[pl.BlockSpec((rows, wide), lambda s, a: (0, half * steps + s))],
            out_specs=pl.BlockSpec((rows, count * part), lambda s, a: (0, s)),
        ),
        out_shape=jax.ShapeDtypeStruct((rows, n_shard * part), value.dtype),
        compiler_params=pltpu.CompilerParams(dimension_semantics=("arbitrary",)),
        name="pick",
        cost_estimate=pl.CostEstimate(flops=0, bytes_accessed=2 * rows * cols, transcendentals=0),
    )(at, value)


def conv_kernel(x_ref, edge_ref, w_ref, *refs):
    o_ref, x_s = refs[-2:]
    L = x_ref.shape[0]
    taps = w_ref.shape[0] - 1
    x_s[0:8, :] = edge_ref[...]
    x_s[8:, :] = x_ref[...].astype(F32)
    pre = jnp.broadcast_to(w_ref[taps:taps + 1, :], x_ref.shape)
    for k in range(taps):
        at = 8 - (taps - 1) + k
        pre = pre + w_ref[k:k + 1, :] * x_s[at:at + L, :]
    o_ref[...] = (pre * jax.nn.sigmoid(pre)).astype(BF16)


def conv_pass(conv_in, edge, wb, Q, at, prev, EB=256):
    T, E = conv_in.shape
    L = T // Q
    at = at * (E // EB)
    row = pl.BlockSpec((L, EB), lambda q, e: (q, e))
    return pl.pallas_call(
        conv_kernel,
        grid=(Q, E // EB),
        in_specs=[
            row,
            pl.BlockSpec((None, 8, EB), lambda q, e: (q, 0, e)),
            pl.BlockSpec((wb.shape[0], EB), lambda q, e: (0, at + e)),
        ] + [pl.BlockSpec(memory_space=pl.ANY)] * len(prev),
        out_specs=pl.BlockSpec((L, EB), lambda q, e: (q, at + e)),
        out_shape=jax.ShapeDtypeStruct((T, wb.shape[1]), BF16),
        input_output_aliases={3 + i: i for i in range(len(prev))},
        scratch_shapes=[pltpu.VMEM((L + 8, EB), F32)],
        compiler_params=pltpu.CompilerParams(dimension_semantics=("arbitrary",) * 2),
        name="conv_pass",
        cost_estimate=pl.CostEstimate(flops=12 * T * E, bytes_accessed=4 * T * E, transcendentals=T * E),
    )(conv_in, edge, wb, *prev)


def conv_back_kernel(gp_ref, xp_ref, gx_ref, x_ref, edge_ref, w_ref, gi_ref, head_ref, tail_ref, gw_ref, x_s, g_s):
    L = x_ref.shape[0]
    taps = w_ref.shape[0] - 1
    x_s[0:8, :] = edge_ref[...]
    x_s[8:, :] = x_ref[...].astype(F32)
    at = [8 - (taps - 1) + k for k in range(taps)]
    pre = jnp.broadcast_to(w_ref[taps:taps + 1, :], x_ref.shape)
    for k in range(taps):
        pre = pre + w_ref[k:k + 1, :] * x_s[at[k]:at[k] + L, :]
    s = jax.nn.sigmoid(pre)
    g_out = contract_cols(gp_ref[...], xp_ref[...]) + gx_ref[...]
    g_pre = g_out * s * (1.0 + pre * (1.0 - s))
    g_s[0:L, :] = g_pre
    g_s[L:, :] = jnp.zeros((8, x_ref.shape[1]), F32)
    gw = [jnp.sum(g_pre * x_s[at[k]:at[k] + L, :], axis=0, keepdims=True) for k in range(taps)]
    gw.append(jnp.sum(g_pre, axis=0, keepdims=True))
    gw_ref[...] = jnp.concatenate(gw, axis=0)
    head_ref[...] = g_s[0:8, :]
    g_in = jnp.zeros(x_ref.shape, F32)
    for k in range(taps):
        g_in = g_in + w_ref[k:k + 1, :] * g_s[taps - 1 - k:taps - 1 - k + L, :]
    gi_ref[...] = g_in.astype(BF16)
    tail_ref[...] = g_in[L - 8:, :]


def conv_back(g_projected, x_proj, gx, conv_in, edge, wb, Q, at, EB=256):
    T, E = conv_in.shape
    L = T // Q
    at = at * (E // EB)
    row = pl.BlockSpec((L, EB), lambda q, e: (q, e))
    edges = pl.BlockSpec((None, 8, EB), lambda q, e: (q, 0, e))
    rows = wb.shape[0]
    return pl.pallas_call(
        conv_back_kernel,
        grid=(Q, E // EB),
        in_specs=[
            pl.BlockSpec((L, g_projected.shape[1]), lambda q, e: (q, 0)),
            pl.BlockSpec((EB, x_proj.shape[1]), lambda q, e: (at + e, 0)),
            pl.BlockSpec((L, EB), lambda q, e: (q, at + e)),
            row,
            edges,
            pl.BlockSpec((rows, EB), lambda q, e: (0, at + e)),
        ],
        out_specs=[row, edges, edges, pl.BlockSpec((None, rows, EB), lambda q, e: (q, 0, e))],
        out_shape=[
            jax.ShapeDtypeStruct((T, E), BF16),
            jax.ShapeDtypeStruct((Q, 8, E), F32),
            jax.ShapeDtypeStruct((Q, 8, E), F32),
            jax.ShapeDtypeStruct((Q, rows, E), F32),
        ],
        scratch_shapes=[pltpu.VMEM((L + 8, EB), F32)] * 2,
        compiler_params=pltpu.CompilerParams(dimension_semantics=("arbitrary",) * 2),
        name="conv_back",
        cost_estimate=pl.CostEstimate(flops=400 * T * E, bytes_accessed=10 * T * E, transcendentals=T * E),
    )(g_projected, x_proj, gx, conv_in, edge, wb)


def contract_rows(left, right):
    return lax.dot_general(left, right, (((0,), (0,)), ((), ())), preferred_element_type=F32)


def contract_cols(left, right):
    return lax.dot_general(left, right, (((1,), (1,)), ((), ())), preferred_element_type=F32)


def swap(value, flip):
    return lax.ppermute(value, "rep", [(i, i ^ flip) for i in range(lax.axis_size("rep"))])


def shifted(value, steps):
    count = lax.axis_size("shard")
    first, last = (max(0, -steps), min(count, count - steps))
    return lax.ppermute(value, "shard", [(i, i + steps) for i in range(first, last)])


def rep_gather(value):
    far = swap(value, 2)
    return [value, swap(value, 1), far, swap(far, 1)]


def rep_near(parts):
    low = [part.astype(BF16) for part in parts]
    near = [swap(low[k], 1).astype(F32) for k in (1, 3)]
    return parts[0] + near[0], (parts[2] + near[1]).astype(BF16)


def rep_far(mine, other):
    return mine + swap(other, 2).astype(F32)


def rep_sum(value):
    wide = value.shape[1] // lax.axis_size("rep")
    parts = [value[:, k * wide:(k + 1) * wide] for k in range(lax.axis_size("rep"))]
    near = [swap(parts[k].astype(BF16), 1).astype(F32) for k in (1, 3)]
    pair = [(parts[0] + near[0]).astype(BF16), (parts[2] + near[1]).astype(BF16)]
    far = [swap(value, 2).astype(F32) for value in pair]
    full = [pair[0].astype(F32) + far[1], pair[1].astype(F32) + far[0]]
    over = [swap(value.astype(BF16), 1).astype(F32) for value in full]
    return jnp.concatenate([full[0], over[0], full[1], over[1]], axis=1)


def in_order(pieces, at):
    def piece(k):
        flip = at ^ k
        odd, far = (flip % 2 == 1, flip // 2 == 1)
        return jnp.where(far, jnp.where(odd, pieces[3], pieces[2]), jnp.where(odd, pieces[1], pieces[0]))

    return [piece(k) for k in range(len(pieces))]


def other(value, axis, flip):
    return lax.ppermute(value, axis, [(i, i ^ flip) for i in range(lax.axis_size(axis))])


def add_all(value, axis):
    step = 1
    while step < lax.axis_size(axis):
        pair = value + other(value, axis, step)
        if step * 4 <= lax.axis_size(axis):
            far = [other(value, axis, step * k) for k in (2, 3)]
            pair = pair + (far[0] + far[1])
            step *= 2
        value = pair
        step *= 2
    return value


def halve(value):
    step = lax.axis_size("shard") // 2
    while step:
        own = lax.axis_index("shard") // step % 2
        keep = lax.dynamic_slice_in_dim(value, own * step, step, 0)
        send = lax.dynamic_slice_in_dim(value, (1 - own) * step, step, 0)
        value = keep + other(send.astype(BF16), "shard", step).astype(F32)
        step //= 2
    return value[0]


def carry_in(total, state, rates, place, span, reverse):
    if span == 1:
        return jnp.zeros_like(state)
    n_rep, states, chans = state.shape
    count = lax.axis_size("shard")
    group = 2 if span % 2 == 0 else 1

    def moved(total, state, target):
        sent = jnp.concatenate([state.reshape(n_rep * states, chans), total], axis=0).astype(BF16)
        pairs = [(i, target(i)) for i in range(count)]
        pairs = [(i, j) for i, j in pairs if 0 <= j < count and i // span == j // span]
        got = lax.ppermute(sent, "shard", pairs).astype(F32)
        return got[n_rep * states:], got[:n_rep * states].reshape(state.shape)

    def decay(amount):
        return jnp.exp(rates[None] * amount[:, None, :])

    second = place % group == 1
    if group == 2:
        other_total, other_state = moved(total, state, lambda i: i ^ 1)
        first_state, last_state = jnp.where(second, other_state, state), jnp.where(second, state, other_state)
        last_total = jnp.where(second, total, other_total)
        block_state = decay(last_total) * first_state + last_state
        block_total = total + other_total
    else:
        block_total, block_state = (total, state)
    step = -group if reverse else group
    got = [moved(block_total, block_state, lambda i, k=k: i + k * step) for k in range(1, span // group)]
    start, gone = (jnp.zeros_like(state), jnp.zeros_like(total))
    for far_total, far_state in got:
        start = start + decay(gone) * far_state
        gone = gone + far_total
    if group == 2:
        start = jnp.where(second, decay(other_total) * start + other_state, start)
    return start


def on_device(
    block_input,
    cotangent,
    seq_lengths,
    slot_order,
    norm_gain,
    in_proj,
    conv_weight,
    conv_bias,
    x_proj,
    dt_proj,
    dt_bias,
    a_log,
    d_skip,
    out_proj,
):
    n_shard, n_rep = (lax.axis_size("shard"), lax.axis_size("rep"))
    shard_at, rep_at = (lax.axis_index("shard"), lax.axis_index("rep"))
    rows, width = block_input.shape
    tokens = n_rep * rows
    taps, wide = conv_weight.shape
    part = wide // n_rep
    chans = part * n_shard
    rank = dt_proj.shape[0]
    states = a_log.shape[0]
    span = max(1, min(n_shard, SPAN_TOKENS // rows))
    in_slot = shard_at % span
    keep_prev = (in_slot != 0).astype(F32)
    keep_next = (in_slot != span - 1).astype(F32)
    places = in_slot * rows + jnp.arange(rows, dtype=jnp.int32)

    def valid_of(flip):
        slot_at = ((rep_at ^ flip) * n_shard + shard_at) // span
        slot_len = jnp.sum(jnp.where(slot_order == slot_at, seq_lengths, 0))
        return (places < slot_len).astype(F32)[:, None]

    valid = [valid_of(k) for k in range(n_rep)]

    def mine(value, axis):
        return lax.dynamic_slice_in_dim(value, rep_at * part, part, axis)

    x_far = swap(block_input, 2)
    small = jnp.concatenate(
        [
            mine(x_proj, 0),
            mine(dt_proj, 1).T,
            mine(a_log, 1).T,
            mine(conv_weight, 1).T,
            mine(conv_bias, 0)[:, None],
            mine(dt_bias, 0)[:, None],
            mine(d_skip, 0)[:, None],
            norm_gain.reshape(part, -1),
        ],
        axis=1,
    )
    groups = chans // GROUP
    if part % LN:
        in_mine = lax.dynamic_index_in_dim(
            in_proj.reshape(in_proj.shape[0], 2, n_shard, n_rep, part), rep_at, 3, keepdims=False
        ).reshape(in_proj.shape[0], 2, chans)
        in_conv, in_gate = (in_mine[:, 0], in_mine[:, 1])
        in_conv = [in_conv]
    else:
        in_conv = [pick(in_proj, rep_at.reshape(1), n_rep, n_shard, part, 0)]
        in_gate = pick(in_proj, rep_at.reshape(1), n_rep, n_shard, part, 1)
    small_all = lax.all_gather(small, "shard", axis=0, tiled=True)
    x_far, small_all = lax.optimization_barrier((x_far, small_all))
    x_all = [block_input, swap(block_input, 1), x_far, swap(x_far, 1)]
    conv_w = [lax.all_gather(value, "shard", axis=0, tiled=True) for value in in_conv]
    gate_w = lax.all_gather(in_gate, "shard", axis=0, tiled=True)
    out_all = lax.all_gather(mine(out_proj, 0), "shard", axis=0, tiled=True)

    cut = [x_proj.shape[1], rank, states, taps, 1, 1, 1]
    ends = [sum(cut[:i + 1]) for i in range(len(cut))]
    xproj_all = small_all[:, :ends[0]]
    dtproj_all = small_all[:, ends[0]:ends[1]].T
    log_rates = small_all[:, ends[1]:ends[2]].T.astype(F32)
    wb = small_all[:, ends[2]:ends[4]].T.astype(F32)
    dtbias_all = small_all[:, ends[4]].astype(F32)
    skip_all = small_all[:, ends[5]].astype(F32)
    gain_f = small_all[:, ends[6]:].reshape(width).astype(F32)

    def norm(value):
        value = value.astype(F32)
        scale = lax.rsqrt(jnp.mean(value * value, axis=1, keepdims=True) + EPSILON)
        return (value * scale * gain_f[None, :]).astype(BF16)

    normed = jnp.concatenate([norm(value) for value in x_all], axis=0)
    cot, normed = lax.optimization_barrier((cotangent, normed))
    cot_all = rep_gather(cot)
    conv_in, edge, conv_out = ([], [], [])
    for k in range(1):
        if k:
            normed, conv_out[0] = lax.optimization_barrier((normed, conv_out[0]))
        conv_in.append(jnp.dot(normed, conv_w[k], preferred_element_type=F32).astype(BF16))
        last = conv_in[k].reshape(n_rep, rows, chans)[:, rows - (taps - 1):]
        before = shifted(last, 1).astype(F32) * keep_prev
        edge.append(jnp.concatenate([jnp.zeros((n_rep, 8 - (taps - 1), chans), F32), before], axis=1))
        conv_out = [conv_pass(conv_in[k], edge[k], wb, n_rep, k, conv_out)]
    conv_out = conv_out[0]
    proj = rep_sum(lax.dot_general(xproj_all, conv_out, (((0,), (1,)), ((), ())), preferred_element_type=F32))
    step_low = proj[:rank].astype(BF16)
    b_all = jnp.broadcast_to(proj[rank:rank + states].T[:, :, None], (tokens, states, LN))
    c_all = jnp.broadcast_to(proj[rank + states:].T[:, :, None], (tokens, states, LN))
    step = jax.nn.softplus(contract_rows(step_low, dtproj_all) + dtbias_all[None, :])
    rates = -jnp.exp(log_rates)
    rates2 = rates * LOG2E
    gate_in = jnp.dot(normed, gate_w, preferred_element_type=F32)
    back = jnp.concatenate(
        [(cot_all[k].astype(F32) * valid[k]).astype(BF16) for k in range(n_rep)], axis=0
    )
    g_gated = contract_cols(back, out_all)
    skip = skip_all[None, :]
    local_end = first_pass(step, conv_out, b_all, rates2, n_rep)
    total = jnp.sum(step.reshape(n_rep, rows, chans), axis=1)
    start_state = carry_in(total, local_end, rates, in_slot, span, False)
    gated, g_gate, g_scanned, kept, local_adj = fwd_pass(
        step, conv_out, gate_in, g_gated, b_all, c_all, rates2, skip, start_state, n_rep
    )
    end_grad = carry_in(total, local_adj, rates, span - 1 - in_slot, span, True)
    branch = jnp.dot(gated, out_all, preferred_element_type=F32)
    near, other = rep_near([branch[k * rows:(k + 1) * rows] for k in range(n_rep)])
    pieces = width // chans
    held = in_proj.shape[0]
    local = [contract_rows(normed, g_gate).astype(BF16).reshape(n_shard, held, chans)]
    for k in range(pieces):
        piece = contract_rows(gated, back[:, k * chans:(k + 1) * chans])
        local.append(piece.astype(BF16).reshape(n_shard, part, chans))
    local = jnp.concatenate(local, axis=1).reshape(-1, chans)
    local, other, end_grad = lax.optimization_barrier((local, other, end_grad))
    branch = rep_far(near, other)
    input_f = block_input.astype(F32)
    activations = (input_f + valid[0] * branch).astype(BF16)

    def scatter(value):
        return lax.psum_scatter(value, "shard", scatter_dimension=0, tiled=True)

    early = scatter(local)
    back_args = (step, conv_out, g_scanned, b_all, c_all, rates2, skip, kept, end_grad, n_rep)
    prev = []
    for k in range(groups):
        prev = bwd_pass(*back_args, k, prev, [local, other] if k == 0 else [activations])
    g_lin, g_scan_in, g_b, g_c, g_a, g_sums = prev
    grad_dt_bias, grad_skip = jnp.sum(g_sums, axis=0)
    grad_dt_proj = contract_rows(g_lin, step_low.T)
    g_low = contract_cols(dtproj_all, g_lin)
    g_b, g_c = [jnp.sum(v, axis=(0, 1)).reshape(tokens, states).T for v in (g_b, g_c)]
    g_proj = jnp.concatenate([g_low, g_b, g_c], axis=0)
    g_proj = rep_sum(g_proj).T.astype(BF16)
    half = rows // 2

    def rows_of(value, at):
        value = value.reshape(n_rep, rows, -1)[:, at:at + half]
        return value.reshape(n_rep * half, -1)

    early, g_proj = lax.optimization_barrier((early, g_proj))
    early = rep_gather(early)
    grad_x_proj = contract_rows(conv_out, g_proj)
    grad_a_log = rates * jnp.sum(g_a, axis=0)
    g_in, late, grad_wb = ([], [], [])
    for k in range(1):
        taps_k = wb[:, k * chans:(k + 1) * chans]
        out, head, tail, grad_taps = conv_back(g_proj, xproj_all, g_scan_in, conv_in[k], edge[k], wb, n_rep, k)
        grad_wb.append(jnp.sum(grad_taps, axis=0))
        after = shifted(head, -1) * keep_next
        joined = jnp.concatenate([jnp.zeros_like(after), after], axis=1)
        fix = tail
        for i in range(taps - 1):
            at = taps - 1 - i
            fix = fix + taps_k[i][None, None, :] * joined[:, at:at + 8]
        out = out.reshape(n_rep, rows, chans).at[:, rows - 8:].set(fix.astype(BF16)).reshape(tokens, chans)
        grad = contract_rows(normed, out).astype(BF16).reshape(n_shard, held, chans)
        small = [grad_x_proj, grad_dt_proj, grad_a_log.T, grad_wb[0].T, grad_dt_bias[:, None], grad_skip[:, None]]
        small.append(jnp.zeros((chans, -ends[6] % LN), F32))
        small = halve(jnp.concatenate(small, axis=1).reshape(n_shard, part, -1)).astype(BF16)
        small = rep_gather(small)
        grad = grad.reshape(-1, chans)
        g_in.append(out)
        late.append(scatter(grad))
    pairs = []
    for at in (0, half):
        both = contract_cols(rows_of(g_in[0], at), conv_w[0]) + contract_cols(rows_of(g_gate, at), gate_w)
        pairs.append(rep_near([both[k * half:(k + 1) * half] for k in range(n_rep)]))
    all_out = [value[held:].reshape(pieces, part, chans).transpose(1, 0, 2).reshape(part, width) for value in early]
    all_out = jnp.concatenate(in_order(all_out, rep_at), axis=0).astype(F32)
    early = [value[:held] for value in early]
    at = rep_at.reshape(1)
    direct = part % LN == 0
    if direct:
        all_in = spread(early, at, *in_proj.shape, part, n_shard, [])
        tied = [late[0], all_in, all_out, pairs[-1][0]]
        late[0], all_in, all_out, mine_last = lax.optimization_barrier(tied)
        pairs[-1] = (mine_last, pairs[-1][1])
    g_normed = [rep_far(*pair) for pair in pairs]
    g_normed = jnp.concatenate(g_normed, axis=0)
    scale = lax.rsqrt(jnp.mean(input_f * input_f, axis=1, keepdims=True) + EPSILON)
    grad_gain = jnp.sum(g_normed * input_f * scale, axis=0)
    g_hat = g_normed * gain_f[None, :]
    input_grad = (
        cotangent.astype(F32)
        + scale * g_hat
        - input_f * (scale * scale * scale) * jnp.mean(g_hat * input_f, axis=1, keepdims=True)
    )
    grad_gain = add_all(add_all(grad_gain.reshape(-1, LN), "rep"), "shard").reshape(width)
    all_gain = lax.dynamic_slice_in_dim(grad_gain, shard_at * norm_gain.shape[0], norm_gain.shape[0])
    late = [rep_gather(value) for value in late]
    all_small = jnp.concatenate(in_order(small, rep_at), axis=0).astype(F32)
    if direct:
        all_in = spread(late[0], at, *in_proj.shape, part, 0, [all_in])
    else:
        late = [jnp.concatenate([values[k] for values in late], axis=1) for k in range(n_rep)]
        all_in = jnp.stack([jnp.stack(in_order(value, rep_at), axis=0) for value in (late, early)], axis=0)
        all_in = all_in.reshape(2, n_rep, -1, n_shard, part).transpose(2, 0, 3, 1, 4)
        all_in = all_in.reshape(in_proj.shape).astype(F32)
    return (
        activations,
        input_grad,
        all_gain,
        all_in,
        all_small[:, ends[2]:ends[3]].T,
        all_small[:, ends[3]],
        all_small[:, :ends[0]],
        all_small[:, ends[0]:ends[1]].T,
        all_small[:, ends[4]],
        all_small[:, ends[1]:ends[2]].T,
        all_small[:, ends[5]],
        all_out,
    )


def solution(mesh):
    tokens = P(("rep", "shard"), None)
    rows, cols, line, full = (P("shard", None), P(None, "shard"), P("shard"), P())
    return jax.shard_map(
        on_device,
        mesh=mesh,
        in_specs=(tokens, tokens, full, full, line, rows, cols, line, rows, cols, line, cols, line, rows),
        out_specs=(tokens, tokens, line, rows, cols, line, rows, cols, line, cols, line, rows),
        check_vma=False,
    )
```

```python
from functools import partial

import jax
import jax.numpy as jnp
from jax import lax
from jax.experimental import pallas as pl
from jax.experimental.pallas import tpu as pltpu
from jax.sharding import PartitionSpec as P

EPSILON = 1e-05
SPAN_TOKENS = 4096
GROUP = 512
F32=jnp.float32; BF16=jnp.bfloat16
LN=128
def first_kernel(U, dt_ref, x_ref, b_ref, a_ref, *refs):
    hend_ref, h_s, dtx_s = refs[-3:]
    TC, EG = dt_ref.shape
    NT = EG//LN
    c = pl.program_id(2)
    @pl.when(c == 0)
    def _():
        h_s[...] = jnp.zeros_like(h_s)
    dtx_s[...] = dt_ref[...]*x_ref[...].astype(F32)
    sl = [slice(j*LN,(j+1)*LN) for j in range(NT)]
    A = [a_ref[:, s] for s in sl]
    def body(i, carry):
        h = list(carry)
        rows = pl.ds(pl.multiple_of(i*U,U),U)
        dv, xv = dt_ref.at[rows], dtx_s.at[rows]
        for k in range(U):
            bt = b_ref[i*U+k]
            for j in range(NT):
                a = jnp.exp2(dv[k:k+1, sl[j]]*A[j])
                h[j] = a*h[j] + xv[k:k+1, sl[j]]*bt
        return tuple(h)
    h = lax.fori_loop(0, TC//U, body, tuple(h_s[:, s] for s in sl))
    for j in range(NT): h_s[:, sl[j]] = h[j]
    @pl.when(c == pl.num_programs(2)-1)
    def _():
        hend_ref[...] = h_s[...]

def first_pass(dt, x, bx, a2, waits, Q, TC=256, EG=GROUP, U=8):
    T,E = dt.shape; N = a2.shape[0]; L=T//Q; NC=L//TC; NE=E//EG
    row = pl.BlockSpec((TC,EG), lambda q,e,c:(q*NC+c, e))
    sp = pl.BlockSpec((TC,N,LN), lambda q,e,c:(q*NC+c,0,0))
    st = pl.BlockSpec((None,N,EG), lambda q,e,c:(q,0,e))
    return pl.pallas_call(partial(first_kernel,U), grid=(Q,NE,NC),
        in_specs=[row,row,sp,pl.BlockSpec((N,EG), lambda q,e,c:(0,e))]+[pl.BlockSpec(memory_space=pl.ANY)]*len(waits),
        out_specs=st,
        out_shape=jax.ShapeDtypeStruct((Q,N,E),F32),
        scratch_shapes=[pltpu.VMEM((N,EG),F32),pltpu.VMEM((TC,EG),F32)],
        compiler_params=pltpu.CompilerParams(dimension_semantics=("arbitrary",)*3, vmem_limit_bytes=60<<20),
        name="first_pass",
        cost_estimate=pl.CostEstimate(flops=5*T*E*N, bytes_accessed=10*T*E, transcendentals=T*E*N))(dt,x,bx,a2,*waits)

LOG2E = 1.4426950408889634


def sums(tb):
    return (lax.broadcasted_iota(jnp.int32,(tb,tb*8),1)//8 == lax.broadcasted_iota(jnp.int32,(tb,tb*8),0)).astype(BF16)

def fwd_kernel(U, TB, dt_ref, x_ref, gate_ref, gg_ref, b_ref, c_ref, a_ref, skip_ref, h0_ref,
               out_ref, gz_ref, g_ref, ck_ref, adj_ref, h_s, p_s, r_s, q_s, y_s, dtx_s):
    TC, EG = dt_ref.shape
    NT = EG//LN
    c = pl.program_id(2)
    @pl.when(c == 0)
    def _():
        h_s[...] = h0_ref[...]; p_s[...] = jnp.ones_like(p_s); r_s[...] = jnp.zeros_like(r_s)
    ck_ref[...] = h_s[...]
    dtx_s[...] = dt_ref[...]*x_ref[...].astype(F32)
    gate = gate_ref[...]
    g_ref[...] = gg_ref[...]*(gate*jax.nn.sigmoid(gate))
    sl = [slice(j*LN,(j+1)*LN) for j in range(NT)]
    A = [a_ref[:, s] for s in sl]
    G = TC//U
    def body(i, carry):
        h, p, r = [list(v) for v in carry]
        rows = pl.ds(pl.multiple_of(i*U,U),U)
        dv, xv, gv = dt_ref.at[rows], dtx_s.at[rows], g_ref.at[rows]
        low = [None]*NT
        for k in range(U):
            t = i*U+k
            bt = b_ref[t]; ct = c_ref[t]
            for j in range(NT):
                a = jnp.exp2(dv[k:k+1, sl[j]]*A[j])
                h[j] = a*h[j] + xv[k:k+1, sl[j]]*bt
                p[j] = p[j]*a
                r[j] = r[j] + p[j]*(ct*gv[k:k+1, sl[j]])
                q = h[j]*ct
                q = q[:8]+q[8:]
                if k % 2 == 0: low[j] = q
                else: q_s[pl.ds(pl.multiple_of(i*(U*8)+k*8-8,16),16), sl[j]] = jnp.concatenate([low[j],q],axis=0).astype(BF16)
        return tuple(h), tuple(p), tuple(r)
    init = tuple(tuple(s_[:, s] for s in sl) for s_ in (h_s, p_s, r_s))
    h, p, r = lax.fori_loop(0, G, body, init)
    S = sums(TB)
    for m in range(0, TC, TB):
        y_s[m:m+TB,:] = jnp.dot(S, q_s[m*8:(m+TB)*8,:], preferred_element_type=F32)
    for j in range(NT):
        h_s[:, sl[j]] = h[j]; p_s[:, sl[j]] = p[j]; r_s[:, sl[j]] = r[j]
    gate = gate_ref[...]
    sig = jax.nn.sigmoid(gate)
    y = y_s[...] + skip_ref[...]*x_ref[...].astype(F32)
    out_ref[...] = (y*(gate*sig)).astype(BF16)
    gz_ref[...] = (gg_ref[...]*y*sig*(1.0+gate*(1.0-sig))).astype(BF16)
    @pl.when(c == pl.num_programs(2)-1)
    def _(): adj_ref[...] = r_s[...]

def fwd_pass(dt, x, gate, gg, bx, cx, a2, skip, h0, Q, TC=256, EG=GROUP, U=8, TB=32):
    T,E = dt.shape; N = a2.shape[0]; L=T//Q; NC=L//TC; NE=E//EG
    row = pl.BlockSpec((TC,EG), lambda q,e,c:(q*NC+c, e))
    sp = pl.BlockSpec((TC,N,LN), lambda q,e,c:(q*NC+c,0,0))
    st = pl.BlockSpec((None,N,EG), lambda q,e,c:(q,0,e))
    return pl.pallas_call(partial(fwd_kernel,U,TB), grid=(Q,NE,NC),
        in_specs=[row,row,row,row,sp,sp,pl.BlockSpec((N,EG), lambda q,e,c:(0,e)), pl.BlockSpec((1,EG), lambda q,e,c:(0,e)), st],
        out_specs=[row, row, row, pl.BlockSpec((None,N,EG), lambda q,e,c:(q*NC+c,0,e)), st],
        out_shape=[jax.ShapeDtypeStruct((T,E),BF16)]*2 + [jax.ShapeDtypeStruct((T,E),F32),
            jax.ShapeDtypeStruct((Q*NC,N,E),F32), jax.ShapeDtypeStruct((Q,N,E),F32)],
        scratch_shapes=[pltpu.VMEM((N,EG),F32)]*3 + [pltpu.VMEM((TC*8,EG),BF16)] + [pltpu.VMEM((TC,EG),F32)]*2,
        compiler_params=pltpu.CompilerParams(dimension_semantics=("arbitrary",)*3, vmem_limit_bytes=60<<20),
        name="fwd_pass",
        cost_estimate=pl.CostEstimate(flops=11*T*E*N, bytes_accessed=22*T*E, transcendentals=T*E*N))(dt,x,gate,gg,bx,cx,a2,skip,h0)

def bwd_kernel(U, TB, n_in, *refs):
    dt_ref, x_ref, g_ref, b_ref, c_ref, a_ref, skip_ref, ck_ref, mu0_ref = refs[:9]
    (gl_ref, gx_ref, gb_ref, gc_ref, ga_ref, su_ref,
     mu_s, ga_s, su_s, qa_s, qb_s, zb_s, zc_s, sa_s, sb_s, dtx_s, a_s, h_s) = refs[n_in:]
    TC, EG = dt_ref.shape
    N = a_ref.shape[0]
    NT = EG//LN
    c = pl.program_id(2)
    @pl.when(c == 0)
    def _():
        mu_s[...] = mu0_ref[...]
        for v in (ga_s, su_s): v[...] = jnp.zeros_like(v)
    dtx_s[...] = dt_ref[...]*x_ref[...].astype(F32)
    sl = [slice(j*LN,(j+1)*LN) for j in range(NT)]
    A = [a_ref[:, s] for s in sl]
    h_s[0] = ck_ref[...]
    G = TC//U
    def up(i, carry):
        h = list(carry)
        rows = pl.ds(pl.multiple_of(i*U,U),U)
        dv, xv = dt_ref.at[rows], dtx_s.at[rows]
        for k in range(U):
            t = i*U+k
            bt = b_ref[t]
            for j in range(NT):
                a = jnp.exp2(dv[k:k+1, sl[j]]*A[j])
                h[j] = a*h[j] + xv[k:k+1, sl[j]]*bt
                a_s[t, :, sl[j]] = a
                h_s[t+1, :, sl[j]] = h[j]
        return tuple(h)
    h = lax.fori_loop(0, G, up, tuple(ck_ref[:, s] for s in sl))
    def down(ii, carry):
        i = G-1-ii
        mu, ga, h = [list(v) for v in carry]
        rows = pl.ds(pl.multiple_of(i*U,U),U)
        dv, gv, xv = dt_ref.at[rows], g_ref.at[rows], dtx_s.at[rows]
        la, lb = [None]*NT, [None]*NT
        for k in reversed(range(U)):
            t = i*U+k
            bt = b_ref[t]; ct = c_ref[t]
            zb = zc = None
            for j in range(NT):
                gr = gv[k:k+1, sl[j]]
                lam = mu[j] + ct*gr
                zcj = h[j]*gr
                zbj = lam*xv[k:k+1, sl[j]]
                zc = zcj if j == 0 else zc+zcj
                zb = zbj if j == 0 else zb+zbj
                mu[j] = a_s[t,:,sl[j]]*lam
                h[j] = h_s[t,:,sl[j]]
                w = mu[j]*h[j]
                ga[j] = ga[j] + dv[k:k+1, sl[j]]*w
                qa = A[j]*w
                qb = lam*bt
                qa = qa[:8]+qa[8:]
                qb = qb[:8]+qb[8:]
                if k % 2: la[j], lb[j] = qa, qb
                else:
                    r16 = pl.ds(pl.multiple_of(i*(U*8)+k*8,16),16)
                    qa_s[r16, sl[j]] = jnp.concatenate([qa,la[j]],axis=0).astype(BF16)
                    qb_s[r16, sl[j]] = jnp.concatenate([qb,lb[j]],axis=0).astype(BF16)
            rn = pl.ds(pl.multiple_of(t*N,N),N)
            zb_s[rn,:] = zb.astype(BF16)
            zc_s[rn,:] = zc.astype(BF16)
        return tuple(mu), tuple(ga), tuple(h)
    init = tuple(tuple(s_[:, s] for s in sl) for s_ in (mu_s, ga_s)) + (h,)
    mu, ga, h = lax.fori_loop(0, G, down, init)
    S = sums(TB)
    for m in range(0, TC, TB):
        sa_s[m:m+TB,:] = jnp.dot(S, qa_s[m*8:(m+TB)*8,:], preferred_element_type=F32)
        sb_s[m:m+TB,:] = jnp.dot(S, qb_s[m*8:(m+TB)*8,:], preferred_element_type=F32)
    ones = jnp.ones((8,LN),BF16)
    nt = (((1,),(1,)),((),()))
    gb_ref[...] = lax.dot_general(ones, zb_s[...], nt, preferred_element_type=F32)[:1]
    gc_ref[...] = lax.dot_general(ones, zc_s[...], nt, preferred_element_type=F32)[:1]
    for j in range(NT): ga_s[:, sl[j]] = ga[j]; mu_s[:, sl[j]] = mu[j]
    d = dt_ref[...]; x = x_ref[...].astype(F32); g = g_ref[...]
    sb = sb_s[...]
    gx_ref[...] = d*sb + skip_ref[...]*g
    sig = jnp.where(d < 0.03, d*(1.0-d*(0.5-d*(1.0/6.0-d*(1.0/24.0)))), 1.0-jnp.exp(-d))
    gp = (sa_s[...]*(1.0/LOG2E) + x*sb)*sig
    gl_ref[...] = gp.astype(BF16)
    su_s[...] = su_s[...] + jnp.concatenate([jnp.sum(gp,axis=0,keepdims=True), jnp.sum(g*x,axis=0,keepdims=True)],axis=0)
    @pl.when(c == pl.num_programs(2)-1)
    def _():
        ga_ref[...] = ga_s[...]; su_ref[...] = su_s[...]

def bwd_pass(dt, x, g, bx, cx, a2, skip, ck, mu0, Q, at, prev, waits, TC=256, EG=GROUP, U=8, TB=32):
    T,E = dt.shape; N = a2.shape[0]; L=T//Q; NC=L//TC; NE=E//EG
    row = pl.BlockSpec((TC,EG), lambda q,e,c:(q*NC+NC-1-c, at))
    sp = pl.BlockSpec((TC,N,LN), lambda q,e,c:(q*NC+NC-1-c,0,0))
    st = pl.BlockSpec((None,N,EG), lambda q,e,c:(q,0,at))
    nb = pl.BlockSpec((None,1,TC*N), lambda q,e,c:(at,0,q*NC+NC-1-c))
    args = (dt,x,g,bx,cx,a2,skip,ck,mu0)
    n_in = len(args)+len(prev)+len(waits)
    return pl.pallas_call(partial(bwd_kernel,U,TB,n_in), grid=(Q,1,NC),
        in_specs=[row,row,row,sp,sp,pl.BlockSpec((N,EG), lambda q,e,c:(0,at)), pl.BlockSpec((1,EG), lambda q,e,c:(0,at)),
            pl.BlockSpec((None,N,EG), lambda q,e,c:(q*NC+NC-1-c,0,at)), st]+[pl.BlockSpec(memory_space=pl.ANY)]*(len(prev)+len(waits)),
        out_specs=[row,row,nb,nb,st,pl.BlockSpec((None,2,EG), lambda q,e,c:(q,0,at))],
        out_shape=[jax.ShapeDtypeStruct((T,E),BF16), jax.ShapeDtypeStruct((T,E),F32)]+[jax.ShapeDtypeStruct((NE,1,T*N),F32)]*2
            +[jax.ShapeDtypeStruct((Q,N,E),F32), jax.ShapeDtypeStruct((Q,2,E),F32)],
        input_output_aliases={len(args)+i: i for i in range(len(prev))},
        scratch_shapes=[pltpu.VMEM((N,EG),F32)]*2+[pltpu.VMEM((2,EG),F32)]+[pltpu.VMEM((TC*8,EG),BF16)]*2+[pltpu.VMEM((TC*N,LN),BF16)]*2
            +[pltpu.VMEM((TC,EG),F32)]*3+[pltpu.VMEM((TC,N,EG),F32), pltpu.VMEM((TC+1,N,EG),F32)],
        compiler_params=pltpu.CompilerParams(dimension_semantics=("arbitrary",)*3, vmem_limit_bytes=62<<20),
        name="bwd_pass",
        cost_estimate=pl.CostEstimate(flops=20*T*EG*N, bytes_accessed=22*T*EG, transcendentals=T*EG*N))(*args,*prev,*waits)


def spread_kernel(count, at_ref, *refs):
    out_ref = refs[-1]
    part = out_ref.shape[1] // count
    for k in range(count):
        at = pl.multiple_of((at_ref[0] ^ k) * part, part)
        out_ref[:, pl.ds(at, part)] = refs[k][...].astype(F32)


def spread(pieces, at, rows, cols, part, start, prev):
    count = len(pieces)
    piece = pl.BlockSpec((rows, part), lambda s, a: (0, s))
    return pl.pallas_call(
        partial(spread_kernel, count),
        grid_spec=pltpu.PrefetchScalarGridSpec(
            num_scalar_prefetch=1,
            grid=(pieces[0].shape[1] // part,),
            in_specs=[piece] * count + [pl.BlockSpec(memory_space=pl.ANY)] * len(prev),
            out_specs=pl.BlockSpec((rows, count * part), lambda s, a: (0, start + s)),
        ),
        out_shape=jax.ShapeDtypeStruct((rows, cols), F32),
        input_output_aliases={1 + count + i: i for i in range(len(prev))},
        compiler_params=pltpu.CompilerParams(dimension_semantics=("arbitrary",)),
        name="spread",
        cost_estimate=pl.CostEstimate(flops=0, bytes_accessed=3 * rows * cols, transcendentals=0),
    )(at, *pieces, *prev)


def pick_kernel(count, at_ref, in_ref, out_ref):
    part = out_ref.shape[1] // count
    wide = in_ref.shape[1] // count
    at = at_ref[0] * part
    for k in range(count):
        out_ref[:, k * part:(k + 1) * part] = in_ref[:, pl.ds(pl.multiple_of(k * wide + at, part), part)]


def pick(value, at, n_rep, n_shard, part, half):
    rows, cols = value.shape
    count = 4 if n_shard % 4 == 0 else n_shard
    steps = n_shard // count
    wide = n_rep * part * count
    return pl.pallas_call(
        partial(pick_kernel, count),
        grid_spec=pltpu.PrefetchScalarGridSpec(
            num_scalar_prefetch=1,
            grid=(steps,),
            in_specs=[pl.BlockSpec((rows, wide), lambda s, a: (0, half * steps + s))],
            out_specs=pl.BlockSpec((rows, count * part), lambda s, a: (0, s)),
        ),
        out_shape=jax.ShapeDtypeStruct((rows, n_shard * part), value.dtype),
        compiler_params=pltpu.CompilerParams(dimension_semantics=("arbitrary",)),
        name="pick",
        cost_estimate=pl.CostEstimate(flops=0, bytes_accessed=2 * rows * cols, transcendentals=0),
    )(at, value)


def conv_kernel(x_ref, edge_ref, w_ref, *refs):
    o_ref, x_s = refs[-2:]
    L = x_ref.shape[0]
    taps = w_ref.shape[0] - 1
    x_s[0:8, :] = edge_ref[...]
    x_s[8:, :] = x_ref[...].astype(F32)
    pre = jnp.broadcast_to(w_ref[taps:taps + 1, :], x_ref.shape)
    for k in range(taps):
        at = 8 - (taps - 1) + k
        pre = pre + w_ref[k:k + 1, :] * x_s[at:at + L, :]
    o_ref[...] = (pre * jax.nn.sigmoid(pre)).astype(BF16)


def conv_pass(conv_in, edge, wb, Q, at, prev, EB=256):
    T, E = conv_in.shape
    L = T // Q
    at = at * (E // EB)
    row = pl.BlockSpec((L, EB), lambda q, e: (q, e))
    return pl.pallas_call(
        conv_kernel,
        grid=(Q, E // EB),
        in_specs=[
            row,
            pl.BlockSpec((None, 8, EB), lambda q, e: (q, 0, e)),
            pl.BlockSpec((wb.shape[0], EB), lambda q, e: (0, at + e)),
        ] + [pl.BlockSpec(memory_space=pl.ANY)] * len(prev),
        out_specs=pl.BlockSpec((L, EB), lambda q, e: (q, at + e)),
        out_shape=jax.ShapeDtypeStruct((T, wb.shape[1]), BF16),
        input_output_aliases={3 + i: i for i in range(len(prev))},
        scratch_shapes=[pltpu.VMEM((L + 8, EB), F32)],
        compiler_params=pltpu.CompilerParams(dimension_semantics=("arbitrary",) * 2),
        name="conv_pass",
        cost_estimate=pl.CostEstimate(flops=12 * T * E, bytes_accessed=4 * T * E, transcendentals=T * E),
    )(conv_in, edge, wb, *prev)


def conv_back_kernel(gp_ref, xp_ref, gx_ref, x_ref, edge_ref, w_ref, gi_ref, head_ref, tail_ref, gw_ref, x_s, g_s):
    L = x_ref.shape[0]
    taps = w_ref.shape[0] - 1
    x_s[0:8, :] = edge_ref[...]
    x_s[8:, :] = x_ref[...].astype(F32)
    at = [8 - (taps - 1) + k for k in range(taps)]
    pre = jnp.broadcast_to(w_ref[taps:taps + 1, :], x_ref.shape)
    for k in range(taps):
        pre = pre + w_ref[k:k + 1, :] * x_s[at[k]:at[k] + L, :]
    s = jax.nn.sigmoid(pre)
    g_out = contract_cols(gp_ref[...], xp_ref[...]) + gx_ref[...]
    g_pre = g_out * s * (1.0 + pre * (1.0 - s))
    g_s[0:L, :] = g_pre
    g_s[L:, :] = jnp.zeros((8, x_ref.shape[1]), F32)
    gw = [jnp.sum(g_pre * x_s[at[k]:at[k] + L, :], axis=0, keepdims=True) for k in range(taps)]
    gw.append(jnp.sum(g_pre, axis=0, keepdims=True))
    gw_ref[...] = jnp.concatenate(gw, axis=0)
    head_ref[...] = g_s[0:8, :]
    g_in = jnp.zeros(x_ref.shape, F32)
    for k in range(taps):
        g_in = g_in + w_ref[k:k + 1, :] * g_s[taps - 1 - k:taps - 1 - k + L, :]
    gi_ref[...] = g_in.astype(BF16)
    tail_ref[...] = g_in[L - 8:, :]


def conv_back(g_projected, x_proj, gx, conv_in, edge, wb, Q, at, EB=256):
    T, E = conv_in.shape
    L = T // Q
    at = at * (E // EB)
    row = pl.BlockSpec((L, EB), lambda q, e: (q, e))
    edges = pl.BlockSpec((None, 8, EB), lambda q, e: (q, 0, e))
    rows = wb.shape[0]
    return pl.pallas_call(
        conv_back_kernel,
        grid=(Q, E // EB),
        in_specs=[
            pl.BlockSpec((L, g_projected.shape[1]), lambda q, e: (q, 0)),
            pl.BlockSpec((EB, x_proj.shape[1]), lambda q, e: (at + e, 0)),
            pl.BlockSpec((L, EB), lambda q, e: (q, at + e)),
            row,
            edges,
            pl.BlockSpec((rows, EB), lambda q, e: (0, at + e)),
        ],
        out_specs=[row, edges, edges, pl.BlockSpec((None, rows, EB), lambda q, e: (q, 0, e))],
        out_shape=[
            jax.ShapeDtypeStruct((T, E), BF16),
            jax.ShapeDtypeStruct((Q, 8, E), F32),
            jax.ShapeDtypeStruct((Q, 8, E), F32),
            jax.ShapeDtypeStruct((Q, rows, E), F32),
        ],
        scratch_shapes=[pltpu.VMEM((L + 8, EB), F32)] * 2,
        compiler_params=pltpu.CompilerParams(dimension_semantics=("arbitrary",) * 2),
        name="conv_back",
        cost_estimate=pl.CostEstimate(flops=400 * T * E, bytes_accessed=10 * T * E, transcendentals=T * E),
    )(g_projected, x_proj, gx, conv_in, edge, wb)


def contract_rows(left, right):
    return lax.dot_general(left, right, (((0,), (0,)), ((), ())), preferred_element_type=F32)


def contract_cols(left, right):
    return lax.dot_general(left, right, (((1,), (1,)), ((), ())), preferred_element_type=F32)


def swap(value, flip):
    return lax.ppermute(value, "rep", [(i, i ^ flip) for i in range(lax.axis_size("rep"))])


def shifted(value, steps):
    count = lax.axis_size("shard")
    first, last = (max(0, -steps), min(count, count - steps))
    return lax.ppermute(value, "shard", [(i, i + steps) for i in range(first, last)])


def rep_gather(value):
    far = swap(value, 2)
    return [value, swap(value, 1), far, swap(far, 1)]


def rep_near(parts):
    low = [part.astype(BF16) for part in parts]
    near = [swap(low[k], 1).astype(F32) for k in (1, 3)]
    return parts[0] + near[0], (parts[2] + near[1]).astype(BF16)


def rep_far(mine, other):
    return mine + swap(other, 2).astype(F32)


def rep_sum(value):
    wide = value.shape[1] // lax.axis_size("rep")
    parts = [value[:, k * wide:(k + 1) * wide] for k in range(lax.axis_size("rep"))]
    near = [swap(parts[k].astype(BF16), 1).astype(F32) for k in (1, 3)]
    pair = [(parts[0] + near[0]).astype(BF16), (parts[2] + near[1]).astype(BF16)]
    far = [swap(value, 2).astype(F32) for value in pair]
    full = [pair[0].astype(F32) + far[1], pair[1].astype(F32) + far[0]]
    over = [swap(value.astype(BF16), 1).astype(F32) for value in full]
    return jnp.concatenate([full[0], over[0], full[1], over[1]], axis=1)


def in_order(pieces, at):
    def piece(k):
        flip = at ^ k
        odd, far = (flip % 2 == 1, flip // 2 == 1)
        return jnp.where(far, jnp.where(odd, pieces[3], pieces[2]), jnp.where(odd, pieces[1], pieces[0]))

    return [piece(k) for k in range(len(pieces))]


def other(value, axis, flip):
    return lax.ppermute(value, axis, [(i, i ^ flip) for i in range(lax.axis_size(axis))])


def add_all(value, axis):
    step = 1
    while step < lax.axis_size(axis):
        pair = value + other(value, axis, step)
        if step * 4 <= lax.axis_size(axis):
            far = [other(value, axis, step * k) for k in (2, 3)]
            pair = pair + (far[0] + far[1])
            step *= 2
        value = pair
        step *= 2
    return value


def halve(value):
    step = value.shape[0] // 2
    own = lax.axis_index("shard") // step % 2
    keep = lax.dynamic_slice_in_dim(value, own * step, step, 0)
    send = lax.dynamic_slice_in_dim(value, (1 - own) * step, step, 0)
    return keep + other(send.astype(BF16), "shard", step).astype(F32)


def carry_in(total, state, rates, place, span, reverse):
    if span == 1:
        return jnp.zeros_like(state)
    n_rep, states, chans = state.shape
    count = lax.axis_size("shard")
    group = 2 if span % 2 == 0 else 1

    def moved(total, state, target):
        sent = jnp.concatenate([state.reshape(n_rep * states, chans), total], axis=0).astype(BF16)
        pairs = [(i, target(i)) for i in range(count)]
        pairs = [(i, j) for i, j in pairs if 0 <= j < count and i // span == j // span]
        got = lax.ppermute(sent, "shard", pairs).astype(F32)
        return got[n_rep * states:], got[:n_rep * states].reshape(state.shape)

    def decay(amount):
        return jnp.exp(rates[None] * amount[:, None, :])

    second = place % group == 1
    if group == 2:
        other_total, other_state = moved(total, state, lambda i: i ^ 1)
        first_state, last_state = jnp.where(second, other_state, state), jnp.where(second, state, other_state)
        last_total = jnp.where(second, total, other_total)
        block_state = decay(last_total) * first_state + last_state
        block_total = total + other_total
    else:
        block_total, block_state = (total, state)
    step = -group if reverse else group
    got = [moved(block_total, block_state, lambda i, k=k: i + k * step) for k in range(1, span // group)]
    start, gone = (jnp.zeros_like(state), jnp.zeros_like(total))
    for far_total, far_state in got:
        start = start + decay(gone) * far_state
        gone = gone + far_total
    if group == 2:
        start = jnp.where(second, decay(other_total) * start + other_state, start)
    return start


def on_device(
    block_input,
    cotangent,
    seq_lengths,
    slot_order,
    norm_gain,
    in_proj,
    conv_weight,
    conv_bias,
    x_proj,
    dt_proj,
    dt_bias,
    a_log,
    d_skip,
    out_proj,
):
    n_shard, n_rep = (lax.axis_size("shard"), lax.axis_size("rep"))
    shard_at, rep_at = (lax.axis_index("shard"), lax.axis_index("rep"))
    rows, width = block_input.shape
    tokens = n_rep * rows
    taps, wide = conv_weight.shape
    part = wide // n_rep
    chans = part * n_shard
    rank = dt_proj.shape[0]
    states = a_log.shape[0]
    span = max(1, min(n_shard, SPAN_TOKENS // rows))
    in_slot = shard_at % span
    keep_prev = (in_slot != 0).astype(F32)
    keep_next = (in_slot != span - 1).astype(F32)
    places = in_slot * rows + jnp.arange(rows, dtype=jnp.int32)

    def valid_of(flip):
        slot_at = ((rep_at ^ flip) * n_shard + shard_at) // span
        slot_len = jnp.sum(jnp.where(slot_order == slot_at, seq_lengths, 0))
        return (places < slot_len).astype(F32)[:, None]

    valid = [valid_of(k) for k in range(n_rep)]

    def mine(value, axis):
        return lax.dynamic_slice_in_dim(value, rep_at * part, part, axis)

    x_far = swap(block_input, 2)
    small = jnp.concatenate(
        [
            mine(x_proj, 0),
            mine(dt_proj, 1).T,
            mine(a_log, 1).T,
            mine(conv_weight, 1).T,
            mine(conv_bias, 0)[:, None],
            mine(dt_bias, 0)[:, None],
            mine(d_skip, 0)[:, None],
            norm_gain.reshape(part, -1),
        ],
        axis=1,
    )
    groups = chans // GROUP
    if part % LN:
        in_mine = lax.dynamic_index_in_dim(
            in_proj.reshape(in_proj.shape[0], 2, n_shard, n_rep, part), rep_at, 3, keepdims=False
        ).reshape(in_proj.shape[0], 2, chans)
        in_conv, in_gate = (in_mine[:, 0], in_mine[:, 1])
        in_conv = [in_conv]
    else:
        in_conv = [pick(in_proj, rep_at.reshape(1), n_rep, n_shard, part, 0)]
        in_gate = pick(in_proj, rep_at.reshape(1), n_rep, n_shard, part, 1)
    small_all = lax.all_gather(small, "shard", axis=0, tiled=True)
    x_far, small_all = lax.optimization_barrier((x_far, small_all))
    x_all = [block_input, swap(block_input, 1), x_far, swap(x_far, 1)]
    conv_w = [lax.all_gather(value, "shard", axis=0, tiled=True) for value in in_conv]
    gate_w = lax.all_gather(in_gate, "shard", axis=0, tiled=True)
    out_all = lax.all_gather(mine(out_proj, 0), "shard", axis=0, tiled=True)

    cut = [x_proj.shape[1], rank, states, taps, 1, 1, 1]
    ends = [sum(cut[:i + 1]) for i in range(len(cut))]
    xproj_all = small_all[:, :ends[0]]
    dtproj_all = small_all[:, ends[0]:ends[1]].T
    log_rates = small_all[:, ends[1]:ends[2]].T.astype(F32)
    wb = small_all[:, ends[2]:ends[4]].T.astype(F32)
    dtbias_all = small_all[:, ends[4]].astype(F32)
    skip_all = small_all[:, ends[5]].astype(F32)
    gain_f = small_all[:, ends[6]:].reshape(width).astype(F32)

    def norm(value):
        value = value.astype(F32)
        scale = lax.rsqrt(jnp.mean(value * value, axis=1, keepdims=True) + EPSILON)
        return (value * scale * gain_f[None, :]).astype(BF16)

    normed = jnp.concatenate([norm(value) for value in x_all], axis=0)
    cot, normed = lax.optimization_barrier((cotangent, normed))
    cot_all = rep_gather(cot)
    conv_in, edge, conv_out = ([], [], [])
    for k in range(1):
        if k:
            normed, conv_out[0] = lax.optimization_barrier((normed, conv_out[0]))
        conv_in.append(jnp.dot(normed, conv_w[k], preferred_element_type=F32).astype(BF16))
        last = conv_in[k].reshape(n_rep, rows, chans)[:, rows - (taps - 1):]
        before = shifted(last, 1).astype(F32) * keep_prev
        edge.append(jnp.concatenate([jnp.zeros((n_rep, 8 - (taps - 1), chans), F32), before], axis=1))
        conv_out = [conv_pass(conv_in[k], edge[k], wb, n_rep, k, conv_out)]
    conv_out = conv_out[0]
    proj = rep_sum(lax.dot_general(xproj_all, conv_out, (((0,), (1,)), ((), ())), preferred_element_type=F32))
    step_low = proj[:rank].astype(BF16)
    b_all = jnp.broadcast_to(proj[rank:rank + states].T[:, :, None], (tokens, states, LN))
    c_all = jnp.broadcast_to(proj[rank + states:].T[:, :, None], (tokens, states, LN))
    step = jax.nn.softplus(contract_rows(step_low, dtproj_all) + dtbias_all[None, :])
    rates = -jnp.exp(log_rates)
    rates2 = rates * LOG2E
    gate_in = jnp.dot(normed, gate_w, preferred_element_type=F32)
    back = jnp.concatenate(
        [(cot_all[k].astype(F32) * valid[k]).astype(BF16) for k in range(n_rep)], axis=0
    )
    g_gated = contract_cols(back, out_all)
    skip = skip_all[None, :]
    local_end = first_pass(step, conv_out, b_all, rates2, [c_all, back], n_rep)
    total = jnp.sum(step.reshape(n_rep, rows, chans), axis=1)
    start_state = carry_in(total, local_end, rates, in_slot, span, False)
    gated, g_gate, g_scanned, kept, local_adj = fwd_pass(
        step, conv_out, gate_in, g_gated, b_all, c_all, rates2, skip, start_state, n_rep
    )
    end_grad = carry_in(total, local_adj, rates, span - 1 - in_slot, span, True)
    branch = jnp.dot(gated, out_all, preferred_element_type=F32)
    near, other = rep_near([branch[k * rows:(k + 1) * rows] for k in range(n_rep)])
    pieces = width // chans
    held = in_proj.shape[0]
    local = [contract_rows(normed, g_gate).astype(BF16).reshape(n_shard, held, chans)]
    for k in range(pieces):
        piece = contract_rows(gated, back[:, k * chans:(k + 1) * chans])
        local.append(piece.astype(BF16).reshape(n_shard, part, chans))
    local = jnp.concatenate(local, axis=1).reshape(-1, chans)
    local, other, end_grad = lax.optimization_barrier((local, other, end_grad))
    branch = rep_far(near, other)
    input_f = block_input.astype(F32)
    activations = (input_f + valid[0] * branch).astype(BF16)

    def scatter(value):
        return lax.psum_scatter(value, "shard", scatter_dimension=0, tiled=True)

    early = scatter(local)
    back_args = (step, conv_out, g_scanned, b_all, c_all, rates2, skip, kept, end_grad, n_rep)
    prev = []
    for k in range(groups):
        prev = bwd_pass(*back_args, k, prev, [local, other] if k == 0 else [activations])
    g_lin, g_scan_in, g_b, g_c, g_a, g_sums = prev
    grad_dt_bias, grad_skip = jnp.sum(g_sums, axis=0)
    grad_dt_proj = contract_rows(g_lin, step_low.T)
    g_low = contract_cols(dtproj_all, g_lin)
    g_b, g_c = [jnp.sum(v, axis=(0, 1)).reshape(tokens, states).T for v in (g_b, g_c)]
    g_proj = jnp.concatenate([g_low, g_b, g_c], axis=0)
    g_proj = rep_sum(g_proj).T.astype(BF16)
    half = rows // 2

    def rows_of(value, at):
        value = value.reshape(n_rep, rows, -1)[:, at:at + half]
        return value.reshape(n_rep * half, -1)

    early, g_proj = lax.optimization_barrier((early, g_proj))
    early = rep_gather(early)
    grad_x_proj = contract_rows(conv_out, g_proj)
    grad_a_log = rates * jnp.sum(g_a, axis=0)
    g_in, late, grad_wb = ([], [], [])
    for k in range(1):
        taps_k = wb[:, k * chans:(k + 1) * chans]
        out, head, tail, grad_taps = conv_back(g_proj, xproj_all, g_scan_in, conv_in[k], edge[k], wb, n_rep, k)
        grad_wb.append(jnp.sum(grad_taps, axis=0))
        after = shifted(head, -1) * keep_next
        joined = jnp.concatenate([jnp.zeros_like(after), after], axis=1)
        fix = tail
        for i in range(taps - 1):
            at = taps - 1 - i
            fix = fix + taps_k[i][None, None, :] * joined[:, at:at + 8]
        out = out.reshape(n_rep, rows, chans).at[:, rows - 8:].set(fix.astype(BF16)).reshape(tokens, chans)
        grad = contract_rows(normed, out).astype(BF16).reshape(n_shard, held, chans)
        small = [grad_x_proj, grad_dt_proj, grad_a_log.T, grad_wb[0].T, grad_dt_bias[:, None], grad_skip[:, None]]
        small.append(jnp.zeros((chans, -ends[6] % LN), F32))
        small = halve(jnp.concatenate(small, axis=1).reshape(n_shard, part, -1))
        grad = grad.reshape(-1, chans)
        grad, *early = lax.optimization_barrier((grad, *early))
        g_in.append(out)
        late.append(scatter(grad))
    pairs = []
    for at in (0, half):
        conv_rows, gate_rows = (rows_of(g_in[0], at), rows_of(g_gate, at))
        both = contract_cols(conv_rows, conv_w[0]) + contract_cols(gate_rows, gate_w)
        both = [both[k * half:(k + 1) * half] for k in range(n_rep)]
        pairs.append(rep_near(both))
    all_out = [value[held:].reshape(pieces, part, chans).transpose(1, 0, 2).reshape(part, width) for value in early]
    all_out = jnp.concatenate(in_order(all_out, rep_at), axis=0).astype(F32)
    early = [value[:held] for value in early]
    at = rep_at.reshape(1)
    direct = part % LN == 0
    if direct:
        all_in = spread(early, at, *in_proj.shape, part, n_shard, [])
        tied = [late[0], all_in, all_out, pairs[-1][0]]
        late[0], all_in, all_out, mine_last = lax.optimization_barrier(tied)
        pairs[-1] = (mine_last, pairs[-1][1])
    g_normed = [rep_far(*pair) for pair in pairs]
    g_normed[0], small = lax.optimization_barrier((g_normed[0], small))
    while small.shape[0] > 1:
        small = halve(small)
    small = rep_gather(small[0].astype(BF16))
    g_normed = jnp.concatenate(g_normed, axis=0)
    scale = lax.rsqrt(jnp.mean(input_f * input_f, axis=1, keepdims=True) + EPSILON)
    grad_gain = jnp.sum(g_normed * input_f * scale, axis=0)
    g_hat = g_normed * gain_f[None, :]
    input_grad = (
        cotangent.astype(F32)
        + scale * g_hat
        - input_f * (scale * scale * scale) * jnp.mean(g_hat * input_f, axis=1, keepdims=True)
    )
    grad_gain = add_all(add_all(grad_gain.reshape(-1, LN), "rep"), "shard").reshape(width)
    all_gain = lax.dynamic_slice_in_dim(grad_gain, shard_at * norm_gain.shape[0], norm_gain.shape[0])
    late = [rep_gather(value) for value in late]
    all_small = jnp.concatenate(in_order(small, rep_at), axis=0).astype(F32)
    if direct:
        all_in = spread(late[0], at, *in_proj.shape, part, 0, [all_in])
    else:
        late = [jnp.concatenate([values[k] for values in late], axis=1) for k in range(n_rep)]
        all_in = jnp.stack([jnp.stack(in_order(value, rep_at), axis=0) for value in (late, early)], axis=0)
        all_in = all_in.reshape(2, n_rep, -1, n_shard, part).transpose(2, 0, 3, 1, 4)
        all_in = all_in.reshape(in_proj.shape).astype(F32)
    return (
        activations,
        input_grad,
        all_gain,
        all_in,
        all_small[:, ends[2]:ends[3]].T,
        all_small[:, ends[3]],
        all_small[:, :ends[0]],
        all_small[:, ends[0]:ends[1]].T,
        all_small[:, ends[4]],
        all_small[:, ends[1]:ends[2]].T,
        all_small[:, ends[5]],
        all_out,
    )


def solution(mesh):
    tokens = P(("rep", "shard"), None)
    rows, cols, line, full = (P("shard", None), P(None, "shard"), P("shard"), P())
    return jax.shard_map(
        on_device,
        mesh=mesh,
        in_specs=(tokens, tokens, full, full, line, rows, cols, line, rows, cols, line, cols, line, rows),
        out_specs=(tokens, tokens, line, rows, cols, line, rows, cols, line, cols, line, rows),
        check_vma=False,
    )
```

```python
from functools import partial

import jax
import jax.numpy as jnp
from jax import lax
from jax.experimental import pallas as pl
from jax.experimental.pallas import tpu as pltpu
from jax.sharding import PartitionSpec as P

EPSILON = 1e-05
SPAN_TOKENS = 4096
GROUP = 512
F32=jnp.float32; BF16=jnp.bfloat16
LN=128
def first_kernel(U, dt_ref, x_ref, b_ref, a_ref, *refs):
    hend_ref, h_s, dtx_s = refs[-3:]
    TC, EG = dt_ref.shape
    NT = EG//LN
    c = pl.program_id(2)
    @pl.when(c == 0)
    def _():
        h_s[...] = jnp.zeros_like(h_s)
    dtx_s[...] = dt_ref[...]*x_ref[...].astype(F32)
    sl = [slice(j*LN,(j+1)*LN) for j in range(NT)]
    A = [a_ref[:, s] for s in sl]
    def body(i, carry):
        h = list(carry)
        rows = pl.ds(pl.multiple_of(i*U,U),U)
        dv, xv = dt_ref.at[rows], dtx_s.at[rows]
        for k in range(U):
            bt = b_ref[i*U+k]
            for j in range(NT):
                a = jnp.exp2(dv[k:k+1, sl[j]]*A[j])
                h[j] = a*h[j] + xv[k:k+1, sl[j]]*bt
        return tuple(h)
    h = lax.fori_loop(0, TC//U, body, tuple(h_s[:, s] for s in sl))
    for j in range(NT): h_s[:, sl[j]] = h[j]
    @pl.when(c == pl.num_programs(2)-1)
    def _():
        hend_ref[...] = h_s[...]

def first_pass(dt, x, bx, a2, waits, Q, TC=256, EG=GROUP, U=8):
    T,E = dt.shape; N = a2.shape[0]; L=T//Q; NC=L//TC; NE=E//EG
    row = pl.BlockSpec((TC,EG), lambda q,e,c:(q*NC+c, e))
    sp = pl.BlockSpec((TC,N,LN), lambda q,e,c:(q*NC+c,0,0))
    st = pl.BlockSpec((None,N,EG), lambda q,e,c:(q,0,e))
    return pl.pallas_call(partial(first_kernel,U), grid=(Q,NE,NC),
        in_specs=[row,row,sp,pl.BlockSpec((N,EG), lambda q,e,c:(0,e))]+[pl.BlockSpec(memory_space=pl.ANY)]*len(waits),
        out_specs=st,
        out_shape=jax.ShapeDtypeStruct((Q,N,E),F32),
        scratch_shapes=[pltpu.VMEM((N,EG),F32),pltpu.VMEM((TC,EG),F32)],
        compiler_params=pltpu.CompilerParams(dimension_semantics=("arbitrary",)*3, vmem_limit_bytes=60<<20),
        name="first_pass",
        cost_estimate=pl.CostEstimate(flops=5*T*E*N, bytes_accessed=10*T*E, transcendentals=T*E*N))(dt,x,bx,a2,*waits)

LOG2E = 1.4426950408889634


def sums(tb):
    return (lax.broadcasted_iota(jnp.int32,(tb,tb*8),1)//8 == lax.broadcasted_iota(jnp.int32,(tb,tb*8),0)).astype(BF16)

def fwd_kernel(U, TB, dt_ref, x_ref, gate_ref, gg_ref, b_ref, c_ref, a_ref, skip_ref, h0_ref,
               out_ref, gz_ref, g_ref, ck_ref, adj_ref, h_s, p_s, r_s, q_s, y_s, dtx_s):
    TC, EG = dt_ref.shape
    NT = EG//LN
    c = pl.program_id(2)
    @pl.when(c == 0)
    def _():
        h_s[...] = h0_ref[...]; p_s[...] = jnp.ones_like(p_s); r_s[...] = jnp.zeros_like(r_s)
    ck_ref[...] = h_s[...]
    dtx_s[...] = dt_ref[...]*x_ref[...].astype(F32)
    gate = gate_ref[...]
    g_ref[...] = gg_ref[...]*(gate*jax.nn.sigmoid(gate))
    sl = [slice(j*LN,(j+1)*LN) for j in range(NT)]
    A = [a_ref[:, s] for s in sl]
    G = TC//U
    def body(i, carry):
        h, p, r = [list(v) for v in carry]
        rows = pl.ds(pl.multiple_of(i*U,U),U)
        dv, xv, gv = dt_ref.at[rows], dtx_s.at[rows], g_ref.at[rows]
        low = [None]*NT
        for k in range(U):
            t = i*U+k
            bt = b_ref[t]; ct = c_ref[t]
            for j in range(NT):
                a = jnp.exp2(dv[k:k+1, sl[j]]*A[j])
                h[j] = a*h[j] + xv[k:k+1, sl[j]]*bt
                p[j] = p[j]*a
                r[j] = r[j] + p[j]*(ct*gv[k:k+1, sl[j]])
                q = h[j]*ct
                q = q[:8]+q[8:]
                if k % 2 == 0: low[j] = q
                else: q_s[pl.ds(pl.multiple_of(i*(U*8)+k*8-8,16),16), sl[j]] = jnp.concatenate([low[j],q],axis=0).astype(BF16)
        return tuple(h), tuple(p), tuple(r)
    init = tuple(tuple(s_[:, s] for s in sl) for s_ in (h_s, p_s, r_s))
    h, p, r = lax.fori_loop(0, G, body, init)
    S = sums(TB)
    for m in range(0, TC, TB):
        y_s[m:m+TB,:] = jnp.dot(S, q_s[m*8:(m+TB)*8,:], preferred_element_type=F32)
    for j in range(NT):
        h_s[:, sl[j]] = h[j]; p_s[:, sl[j]] = p[j]; r_s[:, sl[j]] = r[j]
    gate = gate_ref[...]
    sig = jax.nn.sigmoid(gate)
    y = y_s[...] + skip_ref[...]*x_ref[...].astype(F32)
    out_ref[...] = (y*(gate*sig)).astype(BF16)
    gz_ref[...] = (gg_ref[...]*y*sig*(1.0+gate*(1.0-sig))).astype(BF16)
    @pl.when(c == pl.num_programs(2)-1)
    def _(): adj_ref[...] = r_s[...]

def fwd_pass(dt, x, gate, gg, bx, cx, a2, skip, h0, Q, TC=256, EG=GROUP, U=8, TB=32):
    T,E = dt.shape; N = a2.shape[0]; L=T//Q; NC=L//TC; NE=E//EG
    row = pl.BlockSpec((TC,EG), lambda q,e,c:(q*NC+c, e))
    sp = pl.BlockSpec((TC,N,LN), lambda q,e,c:(q*NC+c,0,0))
    st = pl.BlockSpec((None,N,EG), lambda q,e,c:(q,0,e))
    return pl.pallas_call(partial(fwd_kernel,U,TB), grid=(Q,NE,NC),
        in_specs=[row,row,row,row,sp,sp,pl.BlockSpec((N,EG), lambda q,e,c:(0,e)), pl.BlockSpec((1,EG), lambda q,e,c:(0,e)), st],
        out_specs=[row, row, row, pl.BlockSpec((None,N,EG), lambda q,e,c:(q*NC+c,0,e)), st],
        out_shape=[jax.ShapeDtypeStruct((T,E),BF16)]*2 + [jax.ShapeDtypeStruct((T,E),F32),
            jax.ShapeDtypeStruct((Q*NC,N,E),F32), jax.ShapeDtypeStruct((Q,N,E),F32)],
        scratch_shapes=[pltpu.VMEM((N,EG),F32)]*3 + [pltpu.VMEM((TC*8,EG),BF16)] + [pltpu.VMEM((TC,EG),F32)]*2,
        compiler_params=pltpu.CompilerParams(dimension_semantics=("arbitrary",)*3, vmem_limit_bytes=60<<20),
        name="fwd_pass",
        cost_estimate=pl.CostEstimate(flops=11*T*E*N, bytes_accessed=22*T*E, transcendentals=T*E*N))(dt,x,gate,gg,bx,cx,a2,skip,h0)

def bwd_kernel(U, TB, n_in, *refs):
    dt_ref, x_ref, g_ref, b_ref, c_ref, a_ref, skip_ref, ck_ref, mu0_ref = refs[:9]
    (gl_ref, gx_ref, gb_ref, gc_ref, ga_ref, su_ref,
     mu_s, ga_s, su_s, qa_s, qb_s, zb_s, zc_s, sa_s, sb_s, dtx_s, a_s, h_s) = refs[n_in:]
    TC, EG = dt_ref.shape
    N = a_ref.shape[0]
    NT = EG//LN
    c = pl.program_id(2)
    @pl.when(c == 0)
    def _():
        mu_s[...] = mu0_ref[...]
        for v in (ga_s, su_s): v[...] = jnp.zeros_like(v)
    dtx_s[...] = dt_ref[...]*x_ref[...].astype(F32)
    sl = [slice(j*LN,(j+1)*LN) for j in range(NT)]
    A = [a_ref[:, s] for s in sl]
    h_s[0] = ck_ref[...]
    G = TC//U
    def up(i, carry):
        h = list(carry)
        rows = pl.ds(pl.multiple_of(i*U,U),U)
        dv, xv = dt_ref.at[rows], dtx_s.at[rows]
        for k in range(U):
            t = i*U+k
            bt = b_ref[t]
            for j in range(NT):
                a = jnp.exp2(dv[k:k+1, sl[j]]*A[j])
                h[j] = a*h[j] + xv[k:k+1, sl[j]]*bt
                a_s[t, :, sl[j]] = a
                h_s[t+1, :, sl[j]] = h[j]
        return tuple(h)
    h = lax.fori_loop(0, G, up, tuple(ck_ref[:, s] for s in sl))
    def down(ii, carry):
        i = G-1-ii
        mu, ga, h = [list(v) for v in carry]
        rows = pl.ds(pl.multiple_of(i*U,U),U)
        dv, gv, xv = dt_ref.at[rows], g_ref.at[rows], dtx_s.at[rows]
        la, lb = [None]*NT, [None]*NT
        for k in reversed(range(U)):
            t = i*U+k
            bt = b_ref[t]; ct = c_ref[t]
            zb = zc = None
            for j in range(NT):
                gr = gv[k:k+1, sl[j]]
                lam = mu[j] + ct*gr
                zcj = h[j]*gr
                zbj = lam*xv[k:k+1, sl[j]]
                zc = zcj if j == 0 else zc+zcj
                zb = zbj if j == 0 else zb+zbj
                mu[j] = a_s[t,:,sl[j]]*lam
                h[j] = h_s[t,:,sl[j]]
                w = mu[j]*h[j]
                ga[j] = ga[j] + dv[k:k+1, sl[j]]*w
                qa = A[j]*w
                qb = lam*bt
                qa = qa[:8]+qa[8:]
                qb = qb[:8]+qb[8:]
                if k % 2: la[j], lb[j] = qa, qb
                else:
                    r16 = pl.ds(pl.multiple_of(i*(U*8)+k*8,16),16)
                    qa_s[r16, sl[j]] = jnp.concatenate([qa,la[j]],axis=0).astype(BF16)
                    qb_s[r16, sl[j]] = jnp.concatenate([qb,lb[j]],axis=0).astype(BF16)
            rn = pl.ds(pl.multiple_of(t*N,N),N)
            zb_s[rn,:] = zb.astype(BF16)
            zc_s[rn,:] = zc.astype(BF16)
        return tuple(mu), tuple(ga), tuple(h)
    init = tuple(tuple(s_[:, s] for s in sl) for s_ in (mu_s, ga_s)) + (h,)
    mu, ga, h = lax.fori_loop(0, G, down, init)
    S = sums(TB)
    for m in range(0, TC, TB):
        sa_s[m:m+TB,:] = jnp.dot(S, qa_s[m*8:(m+TB)*8,:], preferred_element_type=F32)
        sb_s[m:m+TB,:] = jnp.dot(S, qb_s[m*8:(m+TB)*8,:], preferred_element_type=F32)
    ones = jnp.ones((8,LN),BF16)
    nt = (((1,),(1,)),((),()))
    gb_ref[...] = lax.dot_general(ones, zb_s[...], nt, preferred_element_type=F32)[:1]
    gc_ref[...] = lax.dot_general(ones, zc_s[...], nt, preferred_element_type=F32)[:1]
    for j in range(NT): ga_s[:, sl[j]] = ga[j]; mu_s[:, sl[j]] = mu[j]
    d = dt_ref[...]; x = x_ref[...].astype(F32); g = g_ref[...]
    sb = sb_s[...]
    gx_ref[...] = d*sb + skip_ref[...]*g
    sig = jnp.where(d < 0.03, d*(1.0-d*(0.5-d*(1.0/6.0-d*(1.0/24.0)))), 1.0-jnp.exp(-d))
    gp = (sa_s[...]*(1.0/LOG2E) + x*sb)*sig
    gl_ref[...] = gp.astype(BF16)
    su_s[...] = su_s[...] + jnp.concatenate([jnp.sum(gp,axis=0,keepdims=True), jnp.sum(g*x,axis=0,keepdims=True)],axis=0)
    @pl.when(c == pl.num_programs(2)-1)
    def _():
        ga_ref[...] = ga_s[...]; su_ref[...] = su_s[...]

def bwd_pass(dt, x, g, bx, cx, a2, skip, ck, mu0, Q, at, prev, waits, TC=256, EG=GROUP, U=8, TB=32):
    T,E = dt.shape; N = a2.shape[0]; L=T//Q; NC=L//TC; NE=E//EG
    row = pl.BlockSpec((TC,EG), lambda q,e,c:(q*NC+NC-1-c, at))
    sp = pl.BlockSpec((TC,N,LN), lambda q,e,c:(q*NC+NC-1-c,0,0))
    st = pl.BlockSpec((None,N,EG), lambda q,e,c:(q,0,at))
    nb = pl.BlockSpec((None,1,TC*N), lambda q,e,c:(at,0,q*NC+NC-1-c))
    args = (dt,x,g,bx,cx,a2,skip,ck,mu0)
    n_in = len(args)+len(prev)+len(waits)
    return pl.pallas_call(partial(bwd_kernel,U,TB,n_in), grid=(Q,1,NC),
        in_specs=[row,row,row,sp,sp,pl.BlockSpec((N,EG), lambda q,e,c:(0,at)), pl.BlockSpec((1,EG), lambda q,e,c:(0,at)),
            pl.BlockSpec((None,N,EG), lambda q,e,c:(q*NC+NC-1-c,0,at)), st]+[pl.BlockSpec(memory_space=pl.ANY)]*(len(prev)+len(waits)),
        out_specs=[row,row,nb,nb,st,pl.BlockSpec((None,2,EG), lambda q,e,c:(q,0,at))],
        out_shape=[jax.ShapeDtypeStruct((T,E),BF16), jax.ShapeDtypeStruct((T,E),F32)]+[jax.ShapeDtypeStruct((NE,1,T*N),F32)]*2
            +[jax.ShapeDtypeStruct((Q,N,E),F32), jax.ShapeDtypeStruct((Q,2,E),F32)],
        input_output_aliases={len(args)+i: i for i in range(len(prev))},
        scratch_shapes=[pltpu.VMEM((N,EG),F32)]*2+[pltpu.VMEM((2,EG),F32)]+[pltpu.VMEM((TC*8,EG),BF16)]*2+[pltpu.VMEM((TC*N,LN),BF16)]*2
            +[pltpu.VMEM((TC,EG),F32)]*3+[pltpu.VMEM((TC,N,EG),F32), pltpu.VMEM((TC+1,N,EG),F32)],
        compiler_params=pltpu.CompilerParams(dimension_semantics=("arbitrary",)*3, vmem_limit_bytes=62<<20),
        name="bwd_pass",
        cost_estimate=pl.CostEstimate(flops=20*T*EG*N, bytes_accessed=22*T*EG, transcendentals=T*EG*N))(*args,*prev,*waits)


def spread_kernel(count, at_ref, *refs):
    out_ref = refs[-1]
    part = out_ref.shape[1] // count
    for k in range(count):
        at = pl.multiple_of((at_ref[0] ^ k) * part, part)
        out_ref[:, pl.ds(at, part)] = refs[k][...].astype(F32)


def spread(pieces, at, rows, cols, part, start, prev):
    count = len(pieces)
    piece = pl.BlockSpec((rows, part), lambda s, a: (0, s))
    return pl.pallas_call(
        partial(spread_kernel, count),
        grid_spec=pltpu.PrefetchScalarGridSpec(
            num_scalar_prefetch=1,
            grid=(pieces[0].shape[1] // part,),
            in_specs=[piece] * count + [pl.BlockSpec(memory_space=pl.ANY)] * len(prev),
            out_specs=pl.BlockSpec((rows, count * part), lambda s, a: (0, start + s)),
        ),
        out_shape=jax.ShapeDtypeStruct((rows, cols), F32),
        input_output_aliases={1 + count + i: i for i in range(len(prev))},
        compiler_params=pltpu.CompilerParams(dimension_semantics=("arbitrary",)),
        name="spread",
        cost_estimate=pl.CostEstimate(flops=0, bytes_accessed=3 * rows * cols, transcendentals=0),
    )(at, *pieces, *prev)


def pick_kernel(count, at_ref, in_ref, out_ref):
    part = out_ref.shape[1] // count
    wide = in_ref.shape[1] // count
    at = at_ref[0] * part
    for k in range(count):
        out_ref[:, k * part:(k + 1) * part] = in_ref[:, pl.ds(pl.multiple_of(k * wide + at, part), part)]


def pick(value, at, n_rep, n_shard, part, half):
    rows, cols = value.shape
    count = 4 if n_shard % 4 == 0 else n_shard
    steps = n_shard // count
    wide = n_rep * part * count
    return pl.pallas_call(
        partial(pick_kernel, count),
        grid_spec=pltpu.PrefetchScalarGridSpec(
            num_scalar_prefetch=1,
            grid=(steps,),
            in_specs=[pl.BlockSpec((rows, wide), lambda s, a: (0, half * steps + s))],
            out_specs=pl.BlockSpec((rows, count * part), lambda s, a: (0, s)),
        ),
        out_shape=jax.ShapeDtypeStruct((rows, n_shard * part), value.dtype),
        compiler_params=pltpu.CompilerParams(dimension_semantics=("arbitrary",)),
        name="pick",
        cost_estimate=pl.CostEstimate(flops=0, bytes_accessed=2 * rows * cols, transcendentals=0),
    )(at, value)


def conv_kernel(x_ref, edge_ref, w_ref, *refs):
    o_ref, x_s = refs[-2:]
    L = x_ref.shape[0]
    taps = w_ref.shape[0] - 1
    x_s[0:8, :] = edge_ref[...]
    x_s[8:, :] = x_ref[...].astype(F32)
    pre = jnp.broadcast_to(w_ref[taps:taps + 1, :], x_ref.shape)
    for k in range(taps):
        at = 8 - (taps - 1) + k
        pre = pre + w_ref[k:k + 1, :] * x_s[at:at + L, :]
    o_ref[...] = (pre * jax.nn.sigmoid(pre)).astype(BF16)


def conv_pass(conv_in, edge, wb, Q, at, prev, EB=512):
    T, E = conv_in.shape
    L = T // Q
    at = at * (E // EB)
    row = pl.BlockSpec((L, EB), lambda q, e: (q, e))
    return pl.pallas_call(
        conv_kernel,
        grid=(Q, E // EB),
        in_specs=[
            row,
            pl.BlockSpec((None, 8, EB), lambda q, e: (q, 0, e)),
            pl.BlockSpec((wb.shape[0], EB), lambda q, e: (0, at + e)),
        ] + [pl.BlockSpec(memory_space=pl.ANY)] * len(prev),
        out_specs=pl.BlockSpec((L, EB), lambda q, e: (q, at + e)),
        out_shape=jax.ShapeDtypeStruct((T, wb.shape[1]), BF16),
        input_output_aliases={3 + i: i for i in range(len(prev))},
        scratch_shapes=[pltpu.VMEM((L + 8, EB), F32)],
        compiler_params=pltpu.CompilerParams(dimension_semantics=("arbitrary",) * 2),
        name="conv_pass",
        cost_estimate=pl.CostEstimate(flops=12 * T * E, bytes_accessed=4 * T * E, transcendentals=T * E),
    )(conv_in, edge, wb, *prev)


def conv_back_kernel(gp_ref, xp_ref, gx_ref, x_ref, edge_ref, w_ref, gi_ref, head_ref, tail_ref, gw_ref, x_s, g_s):
    L = x_ref.shape[0]
    taps = w_ref.shape[0] - 1
    x_s[0:8, :] = edge_ref[...]
    x_s[8:, :] = x_ref[...].astype(F32)
    at = [8 - (taps - 1) + k for k in range(taps)]
    pre = jnp.broadcast_to(w_ref[taps:taps + 1, :], x_ref.shape)
    for k in range(taps):
        pre = pre + w_ref[k:k + 1, :] * x_s[at[k]:at[k] + L, :]
    s = jax.nn.sigmoid(pre)
    g_out = contract_cols(gp_ref[...], xp_ref[...]) + gx_ref[...]
    g_pre = g_out * s * (1.0 + pre * (1.0 - s))
    g_s[0:L, :] = g_pre
    g_s[L:, :] = jnp.zeros((8, x_ref.shape[1]), F32)
    gw = [jnp.sum(g_pre * x_s[at[k]:at[k] + L, :], axis=0, keepdims=True) for k in range(taps)]
    gw.append(jnp.sum(g_pre, axis=0, keepdims=True))
    gw_ref[...] = jnp.concatenate(gw, axis=0)
    head_ref[...] = g_s[0:8, :]
    g_in = jnp.zeros(x_ref.shape, F32)
    for k in range(taps):
        g_in = g_in + w_ref[k:k + 1, :] * g_s[taps - 1 - k:taps - 1 - k + L, :]
    gi_ref[...] = g_in.astype(BF16)
    tail_ref[...] = g_in[L - 8:, :]


def conv_back(g_projected, x_proj, gx, conv_in, edge, wb, Q, at, EB=512):
    T, E = conv_in.shape
    L = T // Q
    at = at * (E // EB)
    row = pl.BlockSpec((L, EB), lambda q, e: (q, e))
    edges = pl.BlockSpec((None, 8, EB), lambda q, e: (q, 0, e))
    rows = wb.shape[0]
    return pl.pallas_call(
        conv_back_kernel,
        grid=(Q, E // EB),
        in_specs=[
            pl.BlockSpec((L, g_projected.shape[1]), lambda q, e: (q, 0)),
            pl.BlockSpec((EB, x_proj.shape[1]), lambda q, e: (at + e, 0)),
            pl.BlockSpec((L, EB), lambda q, e: (q, at + e)),
            row,
            edges,
            pl.BlockSpec((rows, EB), lambda q, e: (0, at + e)),
        ],
        out_specs=[row, edges, edges, pl.BlockSpec((None, rows, EB), lambda q, e: (q, 0, e))],
        out_shape=[
            jax.ShapeDtypeStruct((T, E), BF16),
            jax.ShapeDtypeStruct((Q, 8, E), F32),
            jax.ShapeDtypeStruct((Q, 8, E), F32),
            jax.ShapeDtypeStruct((Q, rows, E), F32),
        ],
        scratch_shapes=[pltpu.VMEM((L + 8, EB), F32)] * 2,
        compiler_params=pltpu.CompilerParams(dimension_semantics=("arbitrary",) * 2),
        name="conv_back",
        cost_estimate=pl.CostEstimate(flops=400 * T * E, bytes_accessed=10 * T * E, transcendentals=T * E),
    )(g_projected, x_proj, gx, conv_in, edge, wb)


def contract_rows(left, right):
    return lax.dot_general(left, right, (((0,), (0,)), ((), ())), preferred_element_type=F32)


def contract_cols(left, right):
    return lax.dot_general(left, right, (((1,), (1,)), ((), ())), preferred_element_type=F32)


def swap(value, flip):
    return lax.ppermute(value, "rep", [(i, i ^ flip) for i in range(lax.axis_size("rep"))])


def shifted(value, steps):
    count = lax.axis_size("shard")
    first, last = (max(0, -steps), min(count, count - steps))
    return lax.ppermute(value, "shard", [(i, i + steps) for i in range(first, last)])


def rep_gather(value):
    far = swap(value, 2)
    return [value, swap(value, 1), far, swap(far, 1)]


def rep_near(parts):
    low = [part.astype(BF16) for part in parts]
    near = [swap(low[k], 1).astype(F32) for k in (1, 3)]
    return parts[0] + near[0], (parts[2] + near[1]).astype(BF16)


def rep_far(mine, other):
    return mine + swap(other, 2).astype(F32)


def rep_sum(value):
    wide = value.shape[1] // lax.axis_size("rep")
    parts = [value[:, k * wide:(k + 1) * wide] for k in range(lax.axis_size("rep"))]
    near = [swap(parts[k].astype(BF16), 1).astype(F32) for k in (1, 3)]
    pair = [(parts[0] + near[0]).astype(BF16), (parts[2] + near[1]).astype(BF16)]
    far = [swap(value, 2).astype(F32) for value in pair]
    full = [pair[0].astype(F32) + far[1], pair[1].astype(F32) + far[0]]
    over = [swap(value.astype(BF16), 1).astype(F32) for value in full]
    return jnp.concatenate([full[0], over[0], full[1], over[1]], axis=1)


def in_order(pieces, at):
    def piece(k):
        flip = at ^ k
        odd, far = (flip % 2 == 1, flip // 2 == 1)
        return jnp.where(far, jnp.where(odd, pieces[3], pieces[2]), jnp.where(odd, pieces[1], pieces[0]))

    return [piece(k) for k in range(len(pieces))]


def other(value, axis, flip):
    return lax.ppermute(value, axis, [(i, i ^ flip) for i in range(lax.axis_size(axis))])


def add_all(value, axis):
    step = 1
    while step < lax.axis_size(axis):
        pair = value + other(value, axis, step)
        if step * 4 <= lax.axis_size(axis):
            far = [other(value, axis, step * k) for k in (2, 3)]
            pair = pair + (far[0] + far[1])
            step *= 2
        value = pair
        step *= 2
    return value


def halve(value):
    step = value.shape[0] // 2
    own = lax.axis_index("shard") // step % 2
    keep = lax.dynamic_slice_in_dim(value, own * step, step, 0)
    send = lax.dynamic_slice_in_dim(value, (1 - own) * step, step, 0)
    return keep + other(send.astype(BF16), "shard", step).astype(F32)


def carry_in(total, state, rates, place, span, reverse):
    if span == 1:
        return jnp.zeros_like(state)
    n_rep, states, chans = state.shape
    count = lax.axis_size("shard")
    group = 2 if span % 2 == 0 else 1

    def moved(total, state, target):
        sent = jnp.concatenate([state.reshape(n_rep * states, chans), total], axis=0).astype(BF16)
        pairs = [(i, target(i)) for i in range(count)]
        pairs = [(i, j) for i, j in pairs if 0 <= j < count and i // span == j // span]
        got = lax.ppermute(sent, "shard", pairs).astype(F32)
        return got[n_rep * states:], got[:n_rep * states].reshape(state.shape)

    def decay(amount):
        return jnp.exp(rates[None] * amount[:, None, :])

    second = place % group == 1
    if group == 2:
        other_total, other_state = moved(total, state, lambda i: i ^ 1)
        first_state, last_state = jnp.where(second, other_state, state), jnp.where(second, state, other_state)
        last_total = jnp.where(second, total, other_total)
        block_state = decay(last_total) * first_state + last_state
        block_total = total + other_total
    else:
        block_total, block_state = (total, state)
    step = -group if reverse else group
    got = [moved(block_total, block_state, lambda i, k=k: i + k * step) for k in range(1, span // group)]
    start, gone = (jnp.zeros_like(state), jnp.zeros_like(total))
    for far_total, far_state in got:
        start = start + decay(gone) * far_state
        gone = gone + far_total
    if group == 2:
        start = jnp.where(second, decay(other_total) * start + other_state, start)
    return start


def on_device(
    block_input,
    cotangent,
    seq_lengths,
    slot_order,
    norm_gain,
    in_proj,
    conv_weight,
    conv_bias,
    x_proj,
    dt_proj,
    dt_bias,
    a_log,
    d_skip,
    out_proj,
):
    n_shard, n_rep = (lax.axis_size("shard"), lax.axis_size("rep"))
    shard_at, rep_at = (lax.axis_index("shard"), lax.axis_index("rep"))
    rows, width = block_input.shape
    tokens = n_rep * rows
    taps, wide = conv_weight.shape
    part = wide // n_rep
    chans = part * n_shard
    rank = dt_proj.shape[0]
    states = a_log.shape[0]
    span = max(1, min(n_shard, SPAN_TOKENS // rows))
    in_slot = shard_at % span
    keep_prev = (in_slot != 0).astype(F32)
    keep_next = (in_slot != span - 1).astype(F32)
    places = in_slot * rows + jnp.arange(rows, dtype=jnp.int32)

    def valid_of(flip):
        slot_at = ((rep_at ^ flip) * n_shard + shard_at) // span
        slot_len = jnp.sum(jnp.where(slot_order == slot_at, seq_lengths, 0))
        return (places < slot_len).astype(F32)[:, None]

    valid = [valid_of(k) for k in range(n_rep)]

    def mine(value, axis):
        return lax.dynamic_slice_in_dim(value, rep_at * part, part, axis)

    x_far = swap(block_input, 2)
    small = jnp.concatenate(
        [
            mine(x_proj, 0),
            mine(dt_proj, 1).T,
            mine(a_log, 1).T,
            mine(conv_weight, 1).T,
            mine(conv_bias, 0)[:, None],
            mine(dt_bias, 0)[:, None],
            mine(d_skip, 0)[:, None],
            norm_gain.reshape(part, -1),
        ],
        axis=1,
    )
    groups = chans // GROUP
    if part % LN:
        in_mine = lax.dynamic_index_in_dim(
            in_proj.reshape(in_proj.shape[0], 2, n_shard, n_rep, part), rep_at, 3, keepdims=False
        ).reshape(in_proj.shape[0], 2, chans)
        in_conv, in_gate = (in_mine[:, 0], in_mine[:, 1])
        in_conv = [in_conv]
    else:
        in_conv = [pick(in_proj, rep_at.reshape(1), n_rep, n_shard, part, 0)]
        in_gate = pick(in_proj, rep_at.reshape(1), n_rep, n_shard, part, 1)
    small_all = lax.all_gather(small, "shard", axis=0, tiled=True)
    x_far, small_all = lax.optimization_barrier((x_far, small_all))
    x_all = [block_input, swap(block_input, 1), x_far, swap(x_far, 1)]
    conv_w = [lax.all_gather(value, "shard", axis=0, tiled=True) for value in in_conv]
    gate_w = lax.all_gather(in_gate, "shard", axis=0, tiled=True)
    out_all = lax.all_gather(mine(out_proj, 0), "shard", axis=0, tiled=True)

    cut = [x_proj.shape[1], rank, states, taps, 1, 1, 1]
    ends = [sum(cut[:i + 1]) for i in range(len(cut))]
    xproj_all = small_all[:, :ends[0]]
    dtproj_all = small_all[:, ends[0]:ends[1]].T
    log_rates = small_all[:, ends[1]:ends[2]].T.astype(F32)
    wb = small_all[:, ends[2]:ends[4]].T.astype(F32)
    dtbias_all = small_all[:, ends[4]].astype(F32)
    skip_all = small_all[:, ends[5]].astype(F32)
    gain_f = small_all[:, ends[6]:].reshape(width).astype(F32)

    def norm(value):
        value = value.astype(F32)
        scale = lax.rsqrt(jnp.mean(value * value, axis=1, keepdims=True) + EPSILON)
        return (value * scale * gain_f[None, :]).astype(BF16)

    normed = jnp.concatenate([norm(value) for value in x_all], axis=0)
    cot, normed = lax.optimization_barrier((cotangent, normed))
    cot_all = rep_gather(cot)
    conv_in, edge, conv_out = ([], [], [])
    for k in range(1):
        if k:
            normed, conv_out[0] = lax.optimization_barrier((normed, conv_out[0]))
        conv_in.append(jnp.dot(normed, conv_w[k], preferred_element_type=F32).astype(BF16))
        last = conv_in[k].reshape(n_rep, rows, chans)[:, rows - (taps - 1):]
        before = shifted(last, 1).astype(F32) * keep_prev
        edge.append(jnp.concatenate([jnp.zeros((n_rep, 8 - (taps - 1), chans), F32), before], axis=1))
        conv_out = [conv_pass(conv_in[k], edge[k], wb, n_rep, k, conv_out)]
    conv_out = conv_out[0]
    proj = rep_sum(lax.dot_general(xproj_all, conv_out, (((0,), (1,)), ((), ())), preferred_element_type=F32))
    step_low = proj[:rank].astype(BF16)
    b_all = jnp.broadcast_to(proj[rank:rank + states].T[:, :, None], (tokens, states, LN))
    c_all = jnp.broadcast_to(proj[rank + states:].T[:, :, None], (tokens, states, LN))
    step = jax.nn.softplus(contract_rows(step_low, dtproj_all) + dtbias_all[None, :])
    rates = -jnp.exp(log_rates)
    rates2 = rates * LOG2E
    gate_in = jnp.dot(normed, gate_w, preferred_element_type=F32)
    back = jnp.concatenate(
        [(cot_all[k].astype(F32) * valid[k]).astype(BF16) for k in range(n_rep)], axis=0
    )
    g_gated = contract_cols(back, out_all)
    skip = skip_all[None, :]
    local_end = first_pass(step, conv_out, b_all, rates2, [c_all, back], n_rep)
    total = jnp.sum(step.reshape(n_rep, rows, chans), axis=1)
    start_state = carry_in(total, local_end, rates, in_slot, span, False)
    gated, g_gate, g_scanned, kept, local_adj = fwd_pass(
        step, conv_out, gate_in, g_gated, b_all, c_all, rates2, skip, start_state, n_rep
    )
    end_grad = carry_in(total, local_adj, rates, span - 1 - in_slot, span, True)
    branch = jnp.dot(gated, out_all, preferred_element_type=F32)
    near, other = rep_near([branch[k * rows:(k + 1) * rows] for k in range(n_rep)])
    pieces = width // chans
    held = in_proj.shape[0]
    local = [contract_rows(normed, g_gate).astype(BF16).reshape(n_shard, held, chans)]
    for k in range(pieces):
        piece = contract_rows(gated, back[:, k * chans:(k + 1) * chans])
        local.append(piece.astype(BF16).reshape(n_shard, part, chans))
    local = jnp.concatenate(local, axis=1).reshape(-1, chans)
    local, other, end_grad = lax.optimization_barrier((local, other, end_grad))
    branch = rep_far(near, other)
    input_f = block_input.astype(F32)
    activations = (input_f + valid[0] * branch).astype(BF16)

    def scatter(value):
        return lax.psum_scatter(value, "shard", scatter_dimension=0, tiled=True)

    early = scatter(local)
    back_args = (step, conv_out, g_scanned, b_all, c_all, rates2, skip, kept, end_grad, n_rep)
    prev = []
    for k in range(groups):
        prev = bwd_pass(*back_args, k, prev, [local, other] if k == 0 else [activations])
    g_lin, g_scan_in, g_b, g_c, g_a, g_sums = prev
    grad_dt_bias, grad_skip = jnp.sum(g_sums, axis=0)
    grad_dt_proj = contract_rows(g_lin, step_low.T)
    g_low = contract_cols(dtproj_all, g_lin)
    g_b, g_c = [jnp.sum(v, axis=(0, 1)).reshape(tokens, states).T for v in (g_b, g_c)]
    g_proj = jnp.concatenate([g_low, g_b, g_c], axis=0)
    g_proj = rep_sum(g_proj).T.astype(BF16)
    half = rows // 2

    def rows_of(value, at):
        value = value.reshape(n_rep, rows, -1)[:, at:at + half]
        return value.reshape(n_rep * half, -1)

    early, g_proj = lax.optimization_barrier((early, g_proj))
    early = rep_gather(early)
    grad_x_proj = contract_rows(conv_out, g_proj)
    grad_a_log = rates * jnp.sum(g_a, axis=0)
    g_in, late, grad_wb = ([], [], [])
    for k in range(1):
        taps_k = wb[:, k * chans:(k + 1) * chans]
        out, head, tail, grad_taps = conv_back(g_proj, xproj_all, g_scan_in, conv_in[k], edge[k], wb, n_rep, k)
        grad_wb.append(jnp.sum(grad_taps, axis=0))
        after = shifted(head, -1) * keep_next
        joined = jnp.concatenate([jnp.zeros_like(after), after], axis=1)
        fix = tail
        for i in range(taps - 1):
            at = taps - 1 - i
            fix = fix + taps_k[i][None, None, :] * joined[:, at:at + 8]
        out = out.reshape(n_rep, rows, chans).at[:, rows - 8:].set(fix.astype(BF16)).reshape(tokens, chans)
        grad = contract_rows(normed, out).astype(BF16).reshape(n_shard, held, chans)
        small = [grad_x_proj, grad_dt_proj, grad_a_log.T, grad_wb[0].T, grad_dt_bias[:, None], grad_skip[:, None]]
        small.append(jnp.zeros((chans, -ends[6] % LN), F32))
        small = halve(jnp.concatenate(small, axis=1).reshape(n_shard, part, -1))
        grad = grad.reshape(-1, chans)
        grad, *early = lax.optimization_barrier((grad, *early))
        g_in.append(out)
        late.append(scatter(grad))
    pairs = []
    for at in (0, half):
        conv_rows, gate_rows = (rows_of(g_in[0], at), rows_of(g_gate, at))
        both = contract_cols(conv_rows, conv_w[0]) + contract_cols(gate_rows, gate_w)
        both = [both[k * half:(k + 1) * half] for k in range(n_rep)]
        pairs.append(rep_near(both))
    all_out = [value[held:].reshape(pieces, part, chans).transpose(1, 0, 2).reshape(part, width) for value in early]
    all_out = jnp.concatenate(in_order(all_out, rep_at), axis=0).astype(F32)
    early = [value[:held] for value in early]
    at = rep_at.reshape(1)
    direct = part % LN == 0
    if direct:
        all_in = spread(early, at, *in_proj.shape, part, n_shard, [])
        tied = [late[0], all_in, all_out, pairs[-1][0]]
        late[0], all_in, all_out, mine_last = lax.optimization_barrier(tied)
        pairs[-1] = (mine_last, pairs[-1][1])
    g_normed = [rep_far(*pair) for pair in pairs]
    g_normed[0], small = lax.optimization_barrier((g_normed[0], small))
    while small.shape[0] > 1:
        small = halve(small)
    small = rep_gather(small[0].astype(BF16))
    g_normed = jnp.concatenate(g_normed, axis=0)
    scale = lax.rsqrt(jnp.mean(input_f * input_f, axis=1, keepdims=True) + EPSILON)
    grad_gain = jnp.sum(g_normed * input_f * scale, axis=0)
    g_hat = g_normed * gain_f[None, :]
    input_grad = (
        cotangent.astype(F32)
        + scale * g_hat
        - input_f * (scale * scale * scale) * jnp.mean(g_hat * input_f, axis=1, keepdims=True)
    )
    grad_gain = add_all(add_all(grad_gain.reshape(-1, LN), "rep"), "shard").reshape(width)
    all_gain = lax.dynamic_slice_in_dim(grad_gain, shard_at * norm_gain.shape[0], norm_gain.shape[0])
    late = [rep_gather(value) for value in late]
    all_small = jnp.concatenate(in_order(small, rep_at), axis=0).astype(F32)
    if direct:
        all_in = spread(late[0], at, *in_proj.shape, part, 0, [all_in])
    else:
        late = [jnp.concatenate([values[k] for values in late], axis=1) for k in range(n_rep)]
        all_in = jnp.stack([jnp.stack(in_order(value, rep_at), axis=0) for value in (late, early)], axis=0)
        all_in = all_in.reshape(2, n_rep, -1, n_shard, part).transpose(2, 0, 3, 1, 4)
        all_in = all_in.reshape(in_proj.shape).astype(F32)
    return (
        activations,
        input_grad,
        all_gain,
        all_in,
        all_small[:, ends[2]:ends[3]].T,
        all_small[:, ends[3]],
        all_small[:, :ends[0]],
        all_small[:, ends[0]:ends[1]].T,
        all_small[:, ends[4]],
        all_small[:, ends[1]:ends[2]].T,
        all_small[:, ends[5]],
        all_out,
    )


def solution(mesh):
    tokens = P(("rep", "shard"), None)
    rows, cols, line, full = (P("shard", None), P(None, "shard"), P("shard"), P())
    return jax.shard_map(
        on_device,
        mesh=mesh,
        in_specs=(tokens, tokens, full, full, line, rows, cols, line, rows, cols, line, cols, line, rows),
        out_specs=(tokens, tokens, line, rows, cols, line, rows, cols, line, cols, line, rows),
        check_vma=False,
    )
```

```python
from functools import partial

import jax
import jax.numpy as jnp
from jax import lax
from jax.experimental import pallas as pl
from jax.experimental.pallas import tpu as pltpu
from jax.sharding import PartitionSpec as P

EPSILON = 1e-05
SPAN_TOKENS = 4096
GROUP = 512
F32=jnp.float32; BF16=jnp.bfloat16
LN=128
def first_kernel(U, dt_ref, x_ref, b_ref, a_ref, *refs):
    hend_ref, h_s, dtx_s = refs[-3:]
    TC, EG = dt_ref.shape
    NT = EG//LN
    c = pl.program_id(2)
    @pl.when(c == 0)
    def _():
        h_s[...] = jnp.zeros_like(h_s)
    dtx_s[...] = dt_ref[...]*x_ref[...].astype(F32)
    sl = [slice(j*LN,(j+1)*LN) for j in range(NT)]
    A = [a_ref[:, s] for s in sl]
    def body(i, carry):
        h = list(carry)
        rows = pl.ds(pl.multiple_of(i*U,U),U)
        dv, xv = dt_ref.at[rows], dtx_s.at[rows]
        for k in range(U):
            bt = b_ref[i*U+k]
            for j in range(NT):
                a = jnp.exp2(dv[k:k+1, sl[j]]*A[j])
                h[j] = a*h[j] + xv[k:k+1, sl[j]]*bt
        return tuple(h)
    h = lax.fori_loop(0, TC//U, body, tuple(h_s[:, s] for s in sl))
    for j in range(NT): h_s[:, sl[j]] = h[j]
    @pl.when(c == pl.num_programs(2)-1)
    def _():
        hend_ref[...] = h_s[...]

def first_pass(dt, x, bx, a2, waits, Q, TC=512, EG=GROUP, U=8):
    T,E = dt.shape; N = a2.shape[0]; L=T//Q; NC=L//TC; NE=E//EG
    row = pl.BlockSpec((TC,EG), lambda q,e,c:(q*NC+c, e))
    sp = pl.BlockSpec((TC,N,LN), lambda q,e,c:(q*NC+c,0,0))
    st = pl.BlockSpec((None,N,EG), lambda q,e,c:(q,0,e))
    return pl.pallas_call(partial(first_kernel,U), grid=(Q,NE,NC),
        in_specs=[row,row,sp,pl.BlockSpec((N,EG), lambda q,e,c:(0,e))]+[pl.BlockSpec(memory_space=pl.ANY)]*len(waits),
        out_specs=st,
        out_shape=jax.ShapeDtypeStruct((Q,N,E),F32),
        scratch_shapes=[pltpu.VMEM((N,EG),F32),pltpu.VMEM((TC,EG),F32)],
        compiler_params=pltpu.CompilerParams(dimension_semantics=("arbitrary",)*3, vmem_limit_bytes=60<<20),
        name="first_pass",
        cost_estimate=pl.CostEstimate(flops=5*T*E*N, bytes_accessed=10*T*E, transcendentals=T*E*N))(dt,x,bx,a2,*waits)

LOG2E = 1.4426950408889634


def sums(tb):
    return (lax.broadcasted_iota(jnp.int32,(tb,tb*8),1)//8 == lax.broadcasted_iota(jnp.int32,(tb,tb*8),0)).astype(BF16)

def fwd_kernel(U, TB, dt_ref, x_ref, gate_ref, gg_ref, b_ref, c_ref, a_ref, skip_ref, h0_ref,
               out_ref, gz_ref, g_ref, ck_ref, adj_ref, h_s, p_s, r_s, q_s, y_s, dtx_s):
    TC, EG = dt_ref.shape
    NT = EG//LN
    c = pl.program_id(2)
    @pl.when(c == 0)
    def _():
        h_s[...] = h0_ref[...]; p_s[...] = jnp.ones_like(p_s); r_s[...] = jnp.zeros_like(r_s)
    ck_ref[...] = h_s[...]
    dtx_s[...] = dt_ref[...]*x_ref[...].astype(F32)
    gate = gate_ref[...]
    g_ref[...] = gg_ref[...]*(gate*jax.nn.sigmoid(gate))
    sl = [slice(j*LN,(j+1)*LN) for j in range(NT)]
    A = [a_ref[:, s] for s in sl]
    G = TC//U
    def body(i, carry):
        h, p, r = [list(v) for v in carry]
        rows = pl.ds(pl.multiple_of(i*U,U),U)
        dv, xv, gv = dt_ref.at[rows], dtx_s.at[rows], g_ref.at[rows]
        low = [None]*NT
        for k in range(U):
            t = i*U+k
            bt = b_ref[t]; ct = c_ref[t]
            for j in range(NT):
                a = jnp.exp2(dv[k:k+1, sl[j]]*A[j])
                h[j] = a*h[j] + xv[k:k+1, sl[j]]*bt
                p[j] = p[j]*a
                r[j] = r[j] + p[j]*(ct*gv[k:k+1, sl[j]])
                q = h[j]*ct
                q = q[:8]+q[8:]
                if k % 2 == 0: low[j] = q
                else: q_s[pl.ds(pl.multiple_of(i*(U*8)+k*8-8,16),16), sl[j]] = jnp.concatenate([low[j],q],axis=0).astype(BF16)
        return tuple(h), tuple(p), tuple(r)
    init = tuple(tuple(s_[:, s] for s in sl) for s_ in (h_s, p_s, r_s))
    h, p, r = lax.fori_loop(0, G, body, init)
    S = sums(TB)
    for m in range(0, TC, TB):
        y_s[m:m+TB,:] = jnp.dot(S, q_s[m*8:(m+TB)*8,:], preferred_element_type=F32)
    for j in range(NT):
        h_s[:, sl[j]] = h[j]; p_s[:, sl[j]] = p[j]; r_s[:, sl[j]] = r[j]
    gate = gate_ref[...]
    sig = jax.nn.sigmoid(gate)
    y = y_s[...] + skip_ref[...]*x_ref[...].astype(F32)
    out_ref[...] = (y*(gate*sig)).astype(BF16)
    gz_ref[...] = (gg_ref[...]*y*sig*(1.0+gate*(1.0-sig))).astype(BF16)
    @pl.when(c == pl.num_programs(2)-1)
    def _(): adj_ref[...] = r_s[...]

def fwd_pass(dt, x, gate, gg, bx, cx, a2, skip, h0, Q, TC=256, EG=GROUP, U=8, TB=32):
    T,E = dt.shape; N = a2.shape[0]; L=T//Q; NC=L//TC; NE=E//EG
    row = pl.BlockSpec((TC,EG), lambda q,e,c:(q*NC+c, e))
    sp = pl.BlockSpec((TC,N,LN), lambda q,e,c:(q*NC+c,0,0))
    st = pl.BlockSpec((None,N,EG), lambda q,e,c:(q,0,e))
    return pl.pallas_call(partial(fwd_kernel,U,TB), grid=(Q,NE,NC),
        in_specs=[row,row,row,row,sp,sp,pl.BlockSpec((N,EG), lambda q,e,c:(0,e)), pl.BlockSpec((1,EG), lambda q,e,c:(0,e)), st],
        out_specs=[row, row, row, pl.BlockSpec((None,N,EG), lambda q,e,c:(q*NC+c,0,e)), st],
        out_shape=[jax.ShapeDtypeStruct((T,E),BF16)]*2 + [jax.ShapeDtypeStruct((T,E),F32),
            jax.ShapeDtypeStruct((Q*NC,N,E),F32), jax.ShapeDtypeStruct((Q,N,E),F32)],
        scratch_shapes=[pltpu.VMEM((N,EG),F32)]*3 + [pltpu.VMEM((TC*8,EG),BF16)] + [pltpu.VMEM((TC,EG),F32)]*2,
        compiler_params=pltpu.CompilerParams(dimension_semantics=("arbitrary",)*3, vmem_limit_bytes=60<<20),
        name="fwd_pass",
        cost_estimate=pl.CostEstimate(flops=11*T*E*N, bytes_accessed=22*T*E, transcendentals=T*E*N))(dt,x,gate,gg,bx,cx,a2,skip,h0)

def bwd_kernel(U, TB, n_in, *refs):
    dt_ref, x_ref, g_ref, b_ref, c_ref, a_ref, skip_ref, ck_ref, mu0_ref = refs[:9]
    (gl_ref, gx_ref, gb_ref, gc_ref, ga_ref, su_ref,
     mu_s, ga_s, su_s, qa_s, qb_s, zb_s, zc_s, sa_s, sb_s, dtx_s, a_s, h_s) = refs[n_in:]
    TC, EG = dt_ref.shape
    N = a_ref.shape[0]
    NT = EG//LN
    c = pl.program_id(2)
    @pl.when(c == 0)
    def _():
        mu_s[...] = mu0_ref[...]
        for v in (ga_s, su_s): v[...] = jnp.zeros_like(v)
    dtx_s[...] = dt_ref[...]*x_ref[...].astype(F32)
    sl = [slice(j*LN,(j+1)*LN) for j in range(NT)]
    A = [a_ref[:, s] for s in sl]
    h_s[0] = ck_ref[...]
    G = TC//U
    def up(i, carry):
        h = list(carry)
        rows = pl.ds(pl.multiple_of(i*U,U),U)
        dv, xv = dt_ref.at[rows], dtx_s.at[rows]
        for k in range(U):
            t = i*U+k
            bt = b_ref[t]
            for j in range(NT):
                a = jnp.exp2(dv[k:k+1, sl[j]]*A[j])
                h[j] = a*h[j] + xv[k:k+1, sl[j]]*bt
                a_s[t, :, sl[j]] = a
                h_s[t+1, :, sl[j]] = h[j]
        return tuple(h)
    h = lax.fori_loop(0, G, up, tuple(ck_ref[:, s] for s in sl))
    def down(ii, carry):
        i = G-1-ii
        mu, ga, h = [list(v) for v in carry]
        rows = pl.ds(pl.multiple_of(i*U,U),U)
        dv, gv, xv = dt_ref.at[rows], g_ref.at[rows], dtx_s.at[rows]
        la, lb = [None]*NT, [None]*NT
        for k in reversed(range(U)):
            t = i*U+k
            bt = b_ref[t]; ct = c_ref[t]
            zb = zc = None
            for j in range(NT):
                gr = gv[k:k+1, sl[j]]
                lam = mu[j] + ct*gr
                zcj = h[j]*gr
                zbj = lam*xv[k:k+1, sl[j]]
                zc = zcj if j == 0 else zc+zcj
                zb = zbj if j == 0 else zb+zbj
                mu[j] = a_s[t,:,sl[j]]*lam
                h[j] = h_s[t,:,sl[j]]
                w = mu[j]*h[j]
                ga[j] = ga[j] + dv[k:k+1, sl[j]]*w
                qa = A[j]*w
                qb = lam*bt
                qa = qa[:8]+qa[8:]
                qb = qb[:8]+qb[8:]
                if k % 2: la[j], lb[j] = qa, qb
                else:
                    r16 = pl.ds(pl.multiple_of(i*(U*8)+k*8,16),16)
                    qa_s[r16, sl[j]] = jnp.concatenate([qa,la[j]],axis=0).astype(BF16)
                    qb_s[r16, sl[j]] = jnp.concatenate([qb,lb[j]],axis=0).astype(BF16)
            rn = pl.ds(pl.multiple_of(t*N,N),N)
            zb_s[rn,:] = zb.astype(BF16)
            zc_s[rn,:] = zc.astype(BF16)
        return tuple(mu), tuple(ga), tuple(h)
    init = tuple(tuple(s_[:, s] for s in sl) for s_ in (mu_s, ga_s)) + (h,)
    mu, ga, h = lax.fori_loop(0, G, down, init)
    S = sums(TB)
    for m in range(0, TC, TB):
        sa_s[m:m+TB,:] = jnp.dot(S, qa_s[m*8:(m+TB)*8,:], preferred_element_type=F32)
        sb_s[m:m+TB,:] = jnp.dot(S, qb_s[m*8:(m+TB)*8,:], preferred_element_type=F32)
    ones = jnp.ones((8,LN),BF16)
    nt = (((1,),(1,)),((),()))
    gb_ref[...] = lax.dot_general(ones, zb_s[...], nt, preferred_element_type=F32)[:1]
    gc_ref[...] = lax.dot_general(ones, zc_s[...], nt, preferred_element_type=F32)[:1]
    for j in range(NT): ga_s[:, sl[j]] = ga[j]; mu_s[:, sl[j]] = mu[j]
    d = dt_ref[...]; x = x_ref[...].astype(F32); g = g_ref[...]
    sb = sb_s[...]
    gx_ref[...] = d*sb + skip_ref[...]*g
    sig = jnp.where(d < 0.03, d*(1.0-d*(0.5-d*(1.0/6.0-d*(1.0/24.0)))), 1.0-jnp.exp(-d))
    gp = (sa_s[...]*(1.0/LOG2E) + x*sb)*sig
    gl_ref[...] = gp.astype(BF16)
    su_s[...] = su_s[...] + jnp.concatenate([jnp.sum(gp,axis=0,keepdims=True), jnp.sum(g*x,axis=0,keepdims=True)],axis=0)
    @pl.when(c == pl.num_programs(2)-1)
    def _():
        ga_ref[...] = ga_s[...]; su_ref[...] = su_s[...]

def bwd_pass(dt, x, g, bx, cx, a2, skip, ck, mu0, Q, at, prev, waits, TC=256, EG=GROUP, U=8, TB=32):
    T,E = dt.shape; N = a2.shape[0]; L=T//Q; NC=L//TC; NE=E//EG
    row = pl.BlockSpec((TC,EG), lambda q,e,c:(q*NC+NC-1-c, at))
    sp = pl.BlockSpec((TC,N,LN), lambda q,e,c:(q*NC+NC-1-c,0,0))
    st = pl.BlockSpec((None,N,EG), lambda q,e,c:(q,0,at))
    nb = pl.BlockSpec((None,1,TC*N), lambda q,e,c:(at,0,q*NC+NC-1-c))
    args = (dt,x,g,bx,cx,a2,skip,ck,mu0)
    n_in = len(args)+len(prev)+len(waits)
    return pl.pallas_call(partial(bwd_kernel,U,TB,n_in), grid=(Q,1,NC),
        in_specs=[row,row,row,sp,sp,pl.BlockSpec((N,EG), lambda q,e,c:(0,at)), pl.BlockSpec((1,EG), lambda q,e,c:(0,at)),
            pl.BlockSpec((None,N,EG), lambda q,e,c:(q*NC+NC-1-c,0,at)), st]+[pl.BlockSpec(memory_space=pl.ANY)]*(len(prev)+len(waits)),
        out_specs=[row,row,nb,nb,st,pl.BlockSpec((None,2,EG), lambda q,e,c:(q,0,at))],
        out_shape=[jax.ShapeDtypeStruct((T,E),BF16), jax.ShapeDtypeStruct((T,E),F32)]+[jax.ShapeDtypeStruct((NE,1,T*N),F32)]*2
            +[jax.ShapeDtypeStruct((Q,N,E),F32), jax.ShapeDtypeStruct((Q,2,E),F32)],
        input_output_aliases={len(args)+i: i for i in range(len(prev))},
        scratch_shapes=[pltpu.VMEM((N,EG),F32)]*2+[pltpu.VMEM((2,EG),F32)]+[pltpu.VMEM((TC*8,EG),BF16)]*2+[pltpu.VMEM((TC*N,LN),BF16)]*2
            +[pltpu.VMEM((TC,EG),F32)]*3+[pltpu.VMEM((TC,N,EG),F32), pltpu.VMEM((TC+1,N,EG),F32)],
        compiler_params=pltpu.CompilerParams(dimension_semantics=("arbitrary",)*3, vmem_limit_bytes=62<<20),
        name="bwd_pass",
        cost_estimate=pl.CostEstimate(flops=20*T*EG*N, bytes_accessed=22*T*EG, transcendentals=T*EG*N))(*args,*prev,*waits)


def spread_kernel(count, at_ref, *refs):
    out_ref = refs[-1]
    part = out_ref.shape[1] // count
    for k in range(count):
        at = pl.multiple_of((at_ref[0] ^ k) * part, part)
        out_ref[:, pl.ds(at, part)] = refs[k][...].astype(F32)


def spread(pieces, at, rows, cols, part, start, prev):
    count = len(pieces)
    piece = pl.BlockSpec((rows, part), lambda s, a: (0, s))
    return pl.pallas_call(
        partial(spread_kernel, count),
        grid_spec=pltpu.PrefetchScalarGridSpec(
            num_scalar_prefetch=1,
            grid=(pieces[0].shape[1] // part,),
            in_specs=[piece] * count + [pl.BlockSpec(memory_space=pl.ANY)] * len(prev),
            out_specs=pl.BlockSpec((rows, count * part), lambda s, a: (0, start + s)),
        ),
        out_shape=jax.ShapeDtypeStruct((rows, cols), F32),
        input_output_aliases={1 + count + i: i for i in range(len(prev))},
        compiler_params=pltpu.CompilerParams(dimension_semantics=("arbitrary",)),
        name="spread",
        cost_estimate=pl.CostEstimate(flops=0, bytes_accessed=3 * rows * cols, transcendentals=0),
    )(at, *pieces, *prev)


def pick_kernel(count, at_ref, in_ref, out_ref):
    part = out_ref.shape[1] // count
    wide = in_ref.shape[1] // count
    at = at_ref[0] * part
    for k in range(count):
        out_ref[:, k * part:(k + 1) * part] = in_ref[:, pl.ds(pl.multiple_of(k * wide + at, part), part)]


def pick(value, at, n_rep, n_shard, part, half):
    rows, cols = value.shape
    count = 4 if n_shard % 4 == 0 else n_shard
    steps = n_shard // count
    wide = n_rep * part * count
    return pl.pallas_call(
        partial(pick_kernel, count),
        grid_spec=pltpu.PrefetchScalarGridSpec(
            num_scalar_prefetch=1,
            grid=(steps,),
            in_specs=[pl.BlockSpec((rows, wide), lambda s, a: (0, half * steps + s))],
            out_specs=pl.BlockSpec((rows, count * part), lambda s, a: (0, s)),
        ),
        out_shape=jax.ShapeDtypeStruct((rows, n_shard * part), value.dtype),
        compiler_params=pltpu.CompilerParams(dimension_semantics=("arbitrary",)),
        name="pick",
        cost_estimate=pl.CostEstimate(flops=0, bytes_accessed=2 * rows * cols, transcendentals=0),
    )(at, value)


def conv_kernel(x_ref, edge_ref, w_ref, *refs):
    o_ref, x_s = refs[-2:]
    L = x_ref.shape[0]
    taps = w_ref.shape[0] - 1
    x_s[0:8, :] = edge_ref[...]
    x_s[8:, :] = x_ref[...].astype(F32)
    pre = jnp.broadcast_to(w_ref[taps:taps + 1, :], x_ref.shape)
    for k in range(taps):
        at = 8 - (taps - 1) + k
        pre = pre + w_ref[k:k + 1, :] * x_s[at:at + L, :]
    o_ref[...] = (pre * jax.nn.sigmoid(pre)).astype(BF16)


def conv_pass(conv_in, edge, wb, Q, at, prev, EB=512):
    T, E = conv_in.shape
    L = T // Q
    at = at * (E // EB)
    row = pl.BlockSpec((L, EB), lambda q, e: (q, e))
    return pl.pallas_call(
        conv_kernel,
        grid=(Q, E // EB),
        in_specs=[
            row,
            pl.BlockSpec((None, 8, EB), lambda q, e: (q, 0, e)),
            pl.BlockSpec((wb.shape[0], EB), lambda q, e: (0, at + e)),
        ] + [pl.BlockSpec(memory_space=pl.ANY)] * len(prev),
        out_specs=pl.BlockSpec((L, EB), lambda q, e: (q, at + e)),
        out_shape=jax.ShapeDtypeStruct((T, wb.shape[1]), BF16),
        input_output_aliases={3 + i: i for i in range(len(prev))},
        scratch_shapes=[pltpu.VMEM((L + 8, EB), F32)],
        compiler_params=pltpu.CompilerParams(dimension_semantics=("arbitrary",) * 2),
        name="conv_pass",
        cost_estimate=pl.CostEstimate(flops=12 * T * E, bytes_accessed=4 * T * E, transcendentals=T * E),
    )(conv_in, edge, wb, *prev)


def conv_back_kernel(gp_ref, xp_ref, gx_ref, x_ref, edge_ref, w_ref, gi_ref, head_ref, tail_ref, gw_ref, x_s, g_s):
    L = x_ref.shape[0]
    taps = w_ref.shape[0] - 1
    x_s[0:8, :] = edge_ref[...]
    x_s[8:, :] = x_ref[...].astype(F32)
    at = [8 - (taps - 1) + k for k in range(taps)]
    pre = jnp.broadcast_to(w_ref[taps:taps + 1, :], x_ref.shape)
    for k in range(taps):
        pre = pre + w_ref[k:k + 1, :] * x_s[at[k]:at[k] + L, :]
    s = jax.nn.sigmoid(pre)
    g_out = contract_cols(gp_ref[...], xp_ref[...]) + gx_ref[...]
    g_pre = g_out * s * (1.0 + pre * (1.0 - s))
    g_s[0:L, :] = g_pre
    g_s[L:, :] = jnp.zeros((8, x_ref.shape[1]), F32)
    gw = [jnp.sum(g_pre * x_s[at[k]:at[k] + L, :], axis=0, keepdims=True) for k in range(taps)]
    gw.append(jnp.sum(g_pre, axis=0, keepdims=True))
    gw_ref[...] = jnp.concatenate(gw, axis=0)
    head_ref[...] = g_s[0:8, :]
    g_in = jnp.zeros(x_ref.shape, F32)
    for k in range(taps):
        g_in = g_in + w_ref[k:k + 1, :] * g_s[taps - 1 - k:taps - 1 - k + L, :]
    gi_ref[...] = g_in.astype(BF16)
    tail_ref[...] = g_in[L - 8:, :]


def conv_back(g_projected, x_proj, gx, conv_in, edge, wb, Q, at, EB=512):
    T, E = conv_in.shape
    L = T // Q
    at = at * (E // EB)
    row = pl.BlockSpec((L, EB), lambda q, e: (q, e))
    edges = pl.BlockSpec((None, 8, EB), lambda q, e: (q, 0, e))
    rows = wb.shape[0]
    return pl.pallas_call(
        conv_back_kernel,
        grid=(Q, E // EB),
        in_specs=[
            pl.BlockSpec((L, g_projected.shape[1]), lambda q, e: (q, 0)),
            pl.BlockSpec((EB, x_proj.shape[1]), lambda q, e: (at + e, 0)),
            pl.BlockSpec((L, EB), lambda q, e: (q, at + e)),
            row,
            edges,
            pl.BlockSpec((rows, EB), lambda q, e: (0, at + e)),
        ],
        out_specs=[row, edges, edges, pl.BlockSpec((None, rows, EB), lambda q, e: (q, 0, e))],
        out_shape=[
            jax.ShapeDtypeStruct((T, E), BF16),
            jax.ShapeDtypeStruct((Q, 8, E), F32),
            jax.ShapeDtypeStruct((Q, 8, E), F32),
            jax.ShapeDtypeStruct((Q, rows, E), F32),
        ],
        scratch_shapes=[pltpu.VMEM((L + 8, EB), F32)] * 2,
        compiler_params=pltpu.CompilerParams(dimension_semantics=("arbitrary",) * 2),
        name="conv_back",
        cost_estimate=pl.CostEstimate(flops=400 * T * E, bytes_accessed=10 * T * E, transcendentals=T * E),
    )(g_projected, x_proj, gx, conv_in, edge, wb)


def contract_rows(left, right):
    return lax.dot_general(left, right, (((0,), (0,)), ((), ())), preferred_element_type=F32)


def contract_cols(left, right):
    return lax.dot_general(left, right, (((1,), (1,)), ((), ())), preferred_element_type=F32)


def swap(value, flip):
    return lax.ppermute(value, "rep", [(i, i ^ flip) for i in range(lax.axis_size("rep"))])


def shifted(value, steps):
    count = lax.axis_size("shard")
    first, last = (max(0, -steps), min(count, count - steps))
    return lax.ppermute(value, "shard", [(i, i + steps) for i in range(first, last)])


def rep_gather(value):
    far = swap(value, 2)
    return [value, swap(value, 1), far, swap(far, 1)]


def rep_near(parts):
    low = [part.astype(BF16) for part in parts]
    near = [swap(low[k], 1).astype(F32) for k in (1, 3)]
    return parts[0] + near[0], (parts[2] + near[1]).astype(BF16)


def rep_far(mine, other):
    return mine + swap(other, 2).astype(F32)


def rep_sum(value):
    wide = value.shape[1] // lax.axis_size("rep")
    parts = [value[:, k * wide:(k + 1) * wide] for k in range(lax.axis_size("rep"))]
    near = [swap(parts[k].astype(BF16), 1).astype(F32) for k in (1, 3)]
    pair = [(parts[0] + near[0]).astype(BF16), (parts[2] + near[1]).astype(BF16)]
    far = [swap(value, 2).astype(F32) for value in pair]
    full = [pair[0].astype(F32) + far[1], pair[1].astype(F32) + far[0]]
    over = [swap(value.astype(BF16), 1).astype(F32) for value in full]
    return jnp.concatenate([full[0], over[0], full[1], over[1]], axis=1)


def in_order(pieces, at):
    def piece(k):
        flip = at ^ k
        odd, far = (flip % 2 == 1, flip // 2 == 1)
        return jnp.where(far, jnp.where(odd, pieces[3], pieces[2]), jnp.where(odd, pieces[1], pieces[0]))

    return [piece(k) for k in range(len(pieces))]


def other(value, axis, flip):
    return lax.ppermute(value, axis, [(i, i ^ flip) for i in range(lax.axis_size(axis))])


def add_all(value, axis):
    step = 1
    while step < lax.axis_size(axis):
        pair = value + other(value, axis, step)
        if step * 4 <= lax.axis_size(axis):
            far = [other(value, axis, step * k) for k in (2, 3)]
            pair = pair + (far[0] + far[1])
            step *= 2
        value = pair
        step *= 2
    return value


def halve(value):
    step = value.shape[0] // 2
    own = lax.axis_index("shard") // step % 2
    keep = lax.dynamic_slice_in_dim(value, own * step, step, 0)
    send = lax.dynamic_slice_in_dim(value, (1 - own) * step, step, 0)
    return keep + other(send.astype(BF16), "shard", step).astype(F32)


def carry_in(total, state, rates, place, span, reverse):
    if span == 1:
        return jnp.zeros_like(state)
    n_rep, states, chans = state.shape
    count = lax.axis_size("shard")
    group = 2 if span % 2 == 0 else 1

    def moved(total, state, target):
        sent = jnp.concatenate([state.reshape(n_rep * states, chans), total], axis=0).astype(BF16)
        pairs = [(i, target(i)) for i in range(count)]
        pairs = [(i, j) for i, j in pairs if 0 <= j < count and i // span == j // span]
        got = lax.ppermute(sent, "shard", pairs).astype(F32)
        return got[n_rep * states:], got[:n_rep * states].reshape(state.shape)

    def decay(amount):
        return jnp.exp(rates[None] * amount[:, None, :])

    second = place % group == 1
    if group == 2:
        other_total, other_state = moved(total, state, lambda i: i ^ 1)
        first_state, last_state = jnp.where(second, other_state, state), jnp.where(second, state, other_state)
        last_total = jnp.where(second, total, other_total)
        block_state = decay(last_total) * first_state + last_state
        block_total = total + other_total
    else:
        block_total, block_state = (total, state)
    step = -group if reverse else group
    got = [moved(block_total, block_state, lambda i, k=k: i + k * step) for k in range(1, span // group)]
    start, gone = (jnp.zeros_like(state), jnp.zeros_like(total))
    for far_total, far_state in got:
        start = start + decay(gone) * far_state
        gone = gone + far_total
    if group == 2:
        start = jnp.where(second, decay(other_total) * start + other_state, start)
    return start


def on_device(
    block_input,
    cotangent,
    seq_lengths,
    slot_order,
    norm_gain,
    in_proj,
    conv_weight,
    conv_bias,
    x_proj,
    dt_proj,
    dt_bias,
    a_log,
    d_skip,
    out_proj,
):
    n_shard, n_rep = (lax.axis_size("shard"), lax.axis_size("rep"))
    shard_at, rep_at = (lax.axis_index("shard"), lax.axis_index("rep"))
    rows, width = block_input.shape
    tokens = n_rep * rows
    taps, wide = conv_weight.shape
    part = wide // n_rep
    chans = part * n_shard
    rank = dt_proj.shape[0]
    states = a_log.shape[0]
    span = max(1, min(n_shard, SPAN_TOKENS // rows))
    in_slot = shard_at % span
    keep_prev = (in_slot != 0).astype(F32)
    keep_next = (in_slot != span - 1).astype(F32)
    places = in_slot * rows + jnp.arange(rows, dtype=jnp.int32)

    def valid_of(flip):
        slot_at = ((rep_at ^ flip) * n_shard + shard_at) // span
        slot_len = jnp.sum(jnp.where(slot_order == slot_at, seq_lengths, 0))
        return (places < slot_len).astype(F32)[:, None]

    valid = [valid_of(k) for k in range(n_rep)]

    def mine(value, axis):
        return lax.dynamic_slice_in_dim(value, rep_at * part, part, axis)

    x_far = swap(block_input, 2)
    small = jnp.concatenate(
        [
            mine(x_proj, 0),
            mine(dt_proj, 1).T,
            mine(a_log, 1).T,
            mine(conv_weight, 1).T,
            mine(conv_bias, 0)[:, None],
            mine(dt_bias, 0)[:, None],
            mine(d_skip, 0)[:, None],
            norm_gain.reshape(part, -1),
        ],
        axis=1,
    )
    groups = chans // GROUP
    if part % LN:
        in_mine = lax.dynamic_index_in_dim(
            in_proj.reshape(in_proj.shape[0], 2, n_shard, n_rep, part), rep_at, 3, keepdims=False
        ).reshape(in_proj.shape[0], 2, chans)
        in_conv, in_gate = (in_mine[:, 0], in_mine[:, 1])
        in_conv = [in_conv]
    else:
        in_conv = [pick(in_proj, rep_at.reshape(1), n_rep, n_shard, part, 0)]
        in_gate = pick(in_proj, rep_at.reshape(1), n_rep, n_shard, part, 1)
    small_all = lax.all_gather(small, "shard", axis=0, tiled=True)
    x_far, small_all = lax.optimization_barrier((x_far, small_all))
    x_all = [block_input, swap(block_input, 1), x_far, swap(x_far, 1)]
    conv_w = [lax.all_gather(value, "shard", axis=0, tiled=True) for value in in_conv]
    gate_w = lax.all_gather(in_gate, "shard", axis=0, tiled=True)
    out_all = lax.all_gather(mine(out_proj, 0), "shard", axis=0, tiled=True)

    cut = [x_proj.shape[1], rank, states, taps, 1, 1, 1]
    ends = [sum(cut[:i + 1]) for i in range(len(cut))]
    xproj_all = small_all[:, :ends[0]]
    dtproj_all = small_all[:, ends[0]:ends[1]].T
    log_rates = small_all[:, ends[1]:ends[2]].T.astype(F32)
    wb = small_all[:, ends[2]:ends[4]].T.astype(F32)
    dtbias_all = small_all[:, ends[4]].astype(F32)
    skip_all = small_all[:, ends[5]].astype(F32)
    gain_f = small_all[:, ends[6]:].reshape(width).astype(F32)

    def norm(value):
        value = value.astype(F32)
        scale = lax.rsqrt(jnp.mean(value * value, axis=1, keepdims=True) + EPSILON)
        return (value * scale * gain_f[None, :]).astype(BF16)

    normed = jnp.concatenate([norm(value) for value in x_all], axis=0)
    cot, normed = lax.optimization_barrier((cotangent, normed))
    cot_all = rep_gather(cot)
    conv_in, edge, conv_out = ([], [], [])
    for k in range(1):
        if k:
            normed, conv_out[0] = lax.optimization_barrier((normed, conv_out[0]))
        conv_in.append(jnp.dot(normed, conv_w[k], preferred_element_type=F32).astype(BF16))
        last = conv_in[k].reshape(n_rep, rows, chans)[:, rows - (taps - 1):]
        before = shifted(last, 1).astype(F32) * keep_prev
        edge.append(jnp.concatenate([jnp.zeros((n_rep, 8 - (taps - 1), chans), F32), before], axis=1))
        conv_out = [conv_pass(conv_in[k], edge[k], wb, n_rep, k, conv_out)]
    conv_out = conv_out[0]
    proj = rep_sum(lax.dot_general(xproj_all, conv_out, (((0,), (1,)), ((), ())), preferred_element_type=F32))
    step_low = proj[:rank].astype(BF16)
    b_all = jnp.broadcast_to(proj[rank:rank + states].T[:, :, None], (tokens, states, LN))
    c_all = jnp.broadcast_to(proj[rank + states:].T[:, :, None], (tokens, states, LN))
    step = jax.nn.softplus(contract_rows(step_low, dtproj_all) + dtbias_all[None, :])
    rates = -jnp.exp(log_rates)
    rates2 = rates * LOG2E
    gate_in = jnp.dot(normed, gate_w, preferred_element_type=F32)
    back = jnp.concatenate(
        [(cot_all[k].astype(F32) * valid[k]).astype(BF16) for k in range(n_rep)], axis=0
    )
    g_gated = contract_cols(back, out_all)
    skip = skip_all[None, :]
    local_end = first_pass(step, conv_out, b_all, rates2, [c_all, back], n_rep)
    total = jnp.sum(step.reshape(n_rep, rows, chans), axis=1)
    start_state = carry_in(total, local_end, rates, in_slot, span, False)
    gated, g_gate, g_scanned, kept, local_adj = fwd_pass(
        step, conv_out, gate_in, g_gated, b_all, c_all, rates2, skip, start_state, n_rep
    )
    end_grad = carry_in(total, local_adj, rates, span - 1 - in_slot, span, True)
    branch = jnp.dot(gated, out_all, preferred_element_type=F32)
    near, other = rep_near([branch[k * rows:(k + 1) * rows] for k in range(n_rep)])
    pieces = width // chans
    held = in_proj.shape[0]
    local = [contract_rows(normed, g_gate).astype(BF16).reshape(n_shard, held, chans)]
    for k in range(pieces):
        piece = contract_rows(gated, back[:, k * chans:(k + 1) * chans])
        local.append(piece.astype(BF16).reshape(n_shard, part, chans))
    local = jnp.concatenate(local, axis=1).reshape(-1, chans)
    local, other, end_grad = lax.optimization_barrier((local, other, end_grad))
    branch = rep_far(near, other)
    input_f = block_input.astype(F32)
    activations = (input_f + valid[0] * branch).astype(BF16)

    def scatter(value):
        return lax.psum_scatter(value, "shard", scatter_dimension=0, tiled=True)

    early = scatter(local)
    back_args = (step, conv_out, g_scanned, b_all, c_all, rates2, skip, kept, end_grad, n_rep)
    prev = []
    for k in range(groups):
        prev = bwd_pass(*back_args, k, prev, [local, other] if k == 0 else [activations])
    g_lin, g_scan_in, g_b, g_c, g_a, g_sums = prev
    grad_dt_bias, grad_skip = jnp.sum(g_sums, axis=0)
    grad_dt_proj = contract_rows(g_lin, step_low.T)
    g_low = contract_cols(dtproj_all, g_lin)
    g_b, g_c = [jnp.sum(v, axis=(0, 1)).reshape(tokens, states).T for v in (g_b, g_c)]
    g_proj = jnp.concatenate([g_low, g_b, g_c], axis=0)
    g_proj = rep_sum(g_proj).T.astype(BF16)
    half = rows // 2

    def rows_of(value, at):
        value = value.reshape(n_rep, rows, -1)[:, at:at + half]
        return value.reshape(n_rep * half, -1)

    early, g_proj = lax.optimization_barrier((early, g_proj))
    early = rep_gather(early)
    grad_x_proj = contract_rows(conv_out, g_proj)
    grad_a_log = rates * jnp.sum(g_a, axis=0)
    g_in, late, grad_wb = ([], [], [])
    for k in range(1):
        taps_k = wb[:, k * chans:(k + 1) * chans]
        out, head, tail, grad_taps = conv_back(g_proj, xproj_all, g_scan_in, conv_in[k], edge[k], wb, n_rep, k)
        grad_wb.append(jnp.sum(grad_taps, axis=0))
        after = shifted(head, -1) * keep_next
        joined = jnp.concatenate([jnp.zeros_like(after), after], axis=1)
        fix = tail
        for i in range(taps - 1):
            at = taps - 1 - i
            fix = fix + taps_k[i][None, None, :] * joined[:, at:at + 8]
        out = out.reshape(n_rep, rows, chans).at[:, rows - 8:].set(fix.astype(BF16)).reshape(tokens, chans)
        grad = contract_rows(normed, out).astype(BF16).reshape(n_shard, held, chans)
        small = [grad_x_proj, grad_dt_proj, grad_a_log.T, grad_wb[0].T, grad_dt_bias[:, None], grad_skip[:, None]]
        small.append(jnp.zeros((chans, -ends[6] % LN), F32))
        small = halve(jnp.concatenate(small, axis=1).reshape(n_shard, part, -1))
        grad = grad.reshape(-1, chans)
        grad, *early = lax.optimization_barrier((grad, *early))
        g_in.append(out)
        late.append(scatter(grad))
    pairs = []
    for at in (0, half):
        conv_rows, gate_rows = (rows_of(g_in[0], at), rows_of(g_gate, at))
        both = contract_cols(conv_rows, conv_w[0]) + contract_cols(gate_rows, gate_w)
        both = [both[k * half:(k + 1) * half] for k in range(n_rep)]
        pairs.append(rep_near(both))
    all_out = [value[held:].reshape(pieces, part, chans).transpose(1, 0, 2).reshape(part, width) for value in early]
    all_out = jnp.concatenate(in_order(all_out, rep_at), axis=0).astype(F32)
    early = [value[:held] for value in early]
    at = rep_at.reshape(1)
    direct = part % LN == 0
    if direct:
        all_in = spread(early, at, *in_proj.shape, part, n_shard, [])
        tied = [late[0], all_in, all_out, pairs[-1][0]]
        late[0], all_in, all_out, mine_last = lax.optimization_barrier(tied)
        pairs[-1] = (mine_last, pairs[-1][1])
    g_normed = [rep_far(*pair) for pair in pairs]
    g_normed[0], small = lax.optimization_barrier((g_normed[0], small))
    while small.shape[0] > 1:
        small = halve(small)
    small = rep_gather(small[0].astype(BF16))
    g_normed = jnp.concatenate(g_normed, axis=0)
    scale = lax.rsqrt(jnp.mean(input_f * input_f, axis=1, keepdims=True) + EPSILON)
    grad_gain = jnp.sum(g_normed * input_f * scale, axis=0)
    g_hat = g_normed * gain_f[None, :]
    input_grad = (
        cotangent.astype(F32)
        + scale * g_hat
        - input_f * (scale * scale * scale) * jnp.mean(g_hat * input_f, axis=1, keepdims=True)
    )
    grad_gain = add_all(add_all(grad_gain.reshape(-1, LN), "rep"), "shard").reshape(width)
    all_gain = lax.dynamic_slice_in_dim(grad_gain, shard_at * norm_gain.shape[0], norm_gain.shape[0])
    late = [rep_gather(value) for value in late]
    all_small = jnp.concatenate(in_order(small, rep_at), axis=0).astype(F32)
    if direct:
        all_in = spread(late[0], at, *in_proj.shape, part, 0, [all_in])
    else:
        late = [jnp.concatenate([values[k] for values in late], axis=1) for k in range(n_rep)]
        all_in = jnp.stack([jnp.stack(in_order(value, rep_at), axis=0) for value in (late, early)], axis=0)
        all_in = all_in.reshape(2, n_rep, -1, n_shard, part).transpose(2, 0, 3, 1, 4)
        all_in = all_in.reshape(in_proj.shape).astype(F32)
    return (
        activations,
        input_grad,
        all_gain,
        all_in,
        all_small[:, ends[2]:ends[3]].T,
        all_small[:, ends[3]],
        all_small[:, :ends[0]],
        all_small[:, ends[0]:ends[1]].T,
        all_small[:, ends[4]],
        all_small[:, ends[1]:ends[2]].T,
        all_small[:, ends[5]],
        all_out,
    )


def solution(mesh):
    tokens = P(("rep", "shard"), None)
    rows, cols, line, full = (P("shard", None), P(None, "shard"), P("shard"), P())
    return jax.shard_map(
        on_device,
        mesh=mesh,
        in_specs=(tokens, tokens, full, full, line, rows, cols, line, rows, cols, line, cols, line, rows),
        out_specs=(tokens, tokens, line, rows, cols, line, rows, cols, line, cols, line, rows),
        check_vma=False,
    )
```
